32 devices in a mesh: gx: 4 (over z), gy: 4 (over y, x), gz: 2 (over core).
Axes of the slice: x: 2, y: 2, z: 4, core: 2. Of those that a mesh axis runs over, the one named last changes fastest.
Arguments:
- e_field: float32 [3, 8, 128, 512], P(None, 'gz', 'gx', 'gy'), may hold values from -6 to 6
- h_field: float32 [3, 8, 128, 512], P(None, 'gz', 'gx', 'gy'), may hold values from -6 to 6
- pole_current: float32 [3, 8, 128, 512], P(None, 'gz', 'gx', 'gy'), may hold values from -6 to 6
- material: int32 [8, 128, 512], P('gz', 'gx', 'gy'), may hold values from 0 to 3
- pole_table: float32 [3, 4], replicated, may hold values from 0.2 to 0.9
- cotangent: float32 [16, 8, 4096], P(None, None, ('gx', 'gy', 'gz')), may hold values from -6 to 6
- cosines: float32 [2, 4096], P(None, ('gx', 'gy', 'gz')), may hold values from -0.7 to 0.7
- wavenumber: float32 [16], replicated, may hold values from 0.6 to 0.8
- time_phase: float32 [16], replicated, may hold values from -3.140625 to 3.140625
Outputs:
- e_next: float32 [3, 8, 128, 512], P(None, 'gz', 'gx', 'gy')
- h_next: float32 [3, 8, 128, 512], P(None, 'gz', 'gx', 'gy')
- pole_next: float32 [3, 8, 128, 512], P(None, 'gz', 'gx', 'gy')
The draws below stay inside these ranges and needn't reach their ends.
All inputs are finite; a program needn't handle non-finite values.
Results may differ from the reference program's by a relative error of at most 0.0003.
Values sent between devices are 32-bit elements; how exact they have to be, the bound alone decides.
No kernel may reach another device: no remote copies, remote signals or barrier semaphores. Data moves between devices by JAX's collectives and lax.ppermute only.
A program may use at most 64 MiB of HBM per device.

```python
import math
import jax
import jax.numpy as jnp
from jax import lax

FREQS = 16
DIRS = 4096
NPOLE = 4
NX = 128
NY = 512
NZ = 8


def draw_cosines(key, part):
    sign_key = jax.random.fold_in(key, 11)
    size_key = jax.random.fold_in(key, 23)
    magnitude = jax.random.uniform(size_key, (2, DIRS), jnp.float32, 0.55, 0.7)
    positive = jax.random.bernoulli(sign_key, 0.5, (2, DIRS))
    signs = jnp.where(positive, 1.0, -1.0).astype(jnp.float32)
    return (signs * magnitude).astype(jnp.float32)


def plant(entries, rng, smallest, high):
    longest = entries.shape.index(max(entries.shape))
    spots = []
    for shift in (0, 1):
        where = [jax.random.randint(jax.random.fold_in(rng, axis), (), 0, length) for axis, length in enumerate(entries.shape)]
        where[longest] = (where[longest] + shift) % entries.shape[longest]
        spots.append(tuple(where))
    return entries.at[spots[0]].set(smallest).at[spots[1]].set(high)


def levels(own_key, shape, cuts, smallest, high):
    def one(axis_at, parts):
        steps = jax.random.uniform(jax.random.fold_in(jax.random.fold_in(own_key, 6), axis_at), (parts,), jnp.float32, smallest / len(cuts), high / len(cuts))
        return jnp.repeat(jnp.exp(steps), shape[axis_at] // parts).reshape((-1,) + (1,) * (len(shape) - axis_at - 1))

    loudness = one(*cuts[0])
    for cut in cuts[1:]:
        loudness = loudness * one(*cut)
    return loudness


def bell_draw(stream_key, extent, deviation, reach, cuts=(), kind=jnp.bfloat16):
    factor_of = levels(stream_key, extent, cuts, -0.22, 0.18) if cuts else 1.0
    array = jax.random.normal(stream_key, extent, jnp.float32) * deviation * factor_of
    return jnp.minimum(jnp.maximum(array, -reach), reach).astype(kind)


def setup_inputs(seed: int = 0) -> dict:
    splits = jax.random.split(jax.random.key(seed), 10)
    return {
        "e_field": bell_draw(splits[0], (3, NZ, NX, NY), 1.0, 6.0, ((1, 2), (2, 4), (3, 4)), jnp.float32),
        "h_field": bell_draw(splits[1], (3, NZ, NX, NY), 1.0, 6.0, ((1, 2), (2, 4), (3, 4)), jnp.float32),
        "pole_current": bell_draw(splits[2], (3, NZ, NX, NY), 1.0, 6.0, ((1, 2), (2, 4), (3, 4)), jnp.float32),
        "material": plant(jax.random.randint(splits[3], (NZ, NX, NY), 0, NPOLE), jax.random.fold_in(splits[3], 1), 0, NPOLE - 1).astype(jnp.int32),
        "pole_table": jnp.clip(jax.random.uniform(splits[4], (3, NPOLE), jnp.float32, 0.2, 0.9), 0.2, 0.9),
        "cotangent": bell_draw(splits[5], (FREQS, 8, DIRS), 1.0, 6.0, ((2, 32),), jnp.float32),
        "cosines": draw_cosines(jax.random.fold_in(splits[9], 71), 0),
        "wavenumber": jnp.clip(jnp.exp(jax.random.uniform(splits[7], (FREQS,), jnp.float32, math.log(0.6), math.log(0.8))), 0.6, 0.8),
        "time_phase": jnp.clip(jax.random.uniform(splits[8], (FREQS,), jnp.float32, -3.140625, 3.140625), -3.140625, 3.140625),
    }


courant = 0.5

def surface_source(cotangent, cosines, wavenumber, time_phase, xs, ys):
    count = cotangent.shape[2]
    rows_x = xs.shape[0]
    rows_y = ys.shape[0]

    def one_freq(total, freq):
        wave = wavenumber[freq]
        along_x = wave * cosines[0]
        along_y = wave * cosines[1]
        phase_x = xs[:, None] * along_x[None, :] - time_phase[freq]
        phase_y = ys[:, None] * along_y[None, :]
        cos_x = jnp.cos(phase_x)[None]
        sin_x = jnp.sin(phase_x)[None]
        weights = cotangent[freq]
        real_part = weights[0::2][:, None, :]
        imag_part = weights[1::2][:, None, :]
        first = real_part * cos_x - imag_part * sin_x
        second = -(real_part * sin_x + imag_part * cos_x)
        left = jnp.concatenate([first, second], axis=2).reshape(4 * rows_x, 2 * count)
        right = jnp.concatenate([jnp.cos(phase_y), jnp.sin(phase_y)], axis=1).T
        part = jnp.dot(left, right, preferred_element_type=jnp.float32, precision=lax.Precision.HIGHEST)
        return (total + part.reshape(4, rows_x, rows_y), None)
    start = jnp.zeros((4, rows_x, rows_y), jnp.float32)
    total, _ = lax.scan(one_freq, start, jnp.arange(cotangent.shape[0], dtype=jnp.int32))
    return total

def ahead(value, nearby, axis):
    rest = lax.slice_in_dim(value, 1, value.shape[axis], axis=axis)
    return jnp.concatenate([rest, nearby], axis) - value

def behind(value, nearby, axis):
    rest = lax.slice_in_dim(value, 0, value.shape[axis] - 1, axis=axis)
    return value - jnp.concatenate([nearby, rest], axis)

def edge_zero(value, axis):
    return jnp.zeros_like(lax.slice_in_dim(value, 0, 1, axis=axis))

def reference(e_field, h_field, pole_current, material, pole_table, cotangent, cosines, wavenumber, time_phase):
    xs = jnp.arange(NX).astype(jnp.float32)
    ys = jnp.arange(NY).astype(jnp.float32)
    source = surface_source(cotangent, cosines, wavenumber, time_phase, xs, ys) * (1.0 / math.sqrt(DIRS * FREQS))
    top = (jnp.arange(NZ) == NZ - 1).astype(jnp.float32)[:, None, None]
    ex, ey, ez = (e_field[0], e_field[1], e_field[2])
    curl_x = ahead(ez, edge_zero(ez, 2), 2) - ahead(ey, edge_zero(ey, 0), 0)
    curl_y = ahead(ex, edge_zero(ex, 0), 0) - ahead(ez, edge_zero(ez, 1), 1)
    curl_z = ahead(ey, edge_zero(ey, 1), 1) - ahead(ex, edge_zero(ex, 2), 2)
    hx = h_field[0] - courant * curl_x - courant * top * source[2][None]
    hy = h_field[1] - courant * curl_y - courant * top * source[3][None]
    hz = h_field[2] - courant * curl_z
    h_next = jnp.stack([hx, hy, hz])
    chosen = (material[None] == jnp.arange(NPOLE, dtype=jnp.int32)[:, None, None, None]).astype(jnp.float32)
    decay = lax.optimization_barrier(jnp.sum(chosen * pole_table[0][:, None, None, None], axis=0))
    drive = lax.optimization_barrier(jnp.sum(chosen * pole_table[1][:, None, None, None], axis=0))
    coef = lax.optimization_barrier(jnp.sum(chosen * pole_table[2][:, None, None, None], axis=0))
    pole_next = decay[None] * pole_current + drive[None] * e_field
    side_x = behind(hz, edge_zero(hz, 2), 2) - behind(hy, edge_zero(hy, 0), 0)
    side_y = behind(hx, edge_zero(hx, 0), 0) - behind(hz, edge_zero(hz, 1), 1)
    side_z = behind(hy, edge_zero(hy, 1), 1) - behind(hx, edge_zero(hx, 2), 2)
    curl_h = jnp.stack([side_x, side_y, side_z])
    inject = jnp.stack([top * source[0][None], top * source[1][None], jnp.zeros_like(ex)])
    e_next = e_field + coef[None] * (curl_h - 0.5 * (pole_next + pole_current)) - coef[None] * inject
    return (e_next, h_next, pole_next)
```

```python
import math

import jax
import jax.numpy as jnp
from jax import lax
from jax.experimental import pallas as pl
from jax.experimental.pallas import tpu as pltpu
from jax.sharding import PartitionSpec as P

NPOLE = 4
LANES = 128


courant = 0.5


def from_behind(array, axis, by):
    size = lax.axis_size(axis)
    pairs = [(i, i + by) for i in range(size) if 0 <= i + by < size]
    return lax.ppermute(array, axis, pairs)


def exchange(array, axis, mask):
    return lax.ppermute(array, axis, [(i, i ^ mask) for i in range(lax.axis_size(axis))])


def gray(index):
    return index ^ (index >> 1)


def ungray(code, bits):
    index = code
    for step in range(1, bits):
        index = index ^ (code >> step)
    return index


def bits_of(size):
    return size.bit_length() - 1


def cmul(a, b):
    return (a[0] * b[0] - a[1] * b[1], a[0] * b[1] + a[1] * b[0])


def small_turn(angle):
    q = angle * angle
    c = 1.0 + q * (-1 / 2 + q * (1 / 24 + q * (-1 / 720 + q * (1 / 40320))))
    s = angle * (1.0 + q * (-1 / 6 + q * (1 / 120 + q * (-1 / 5040 + q * (1 / 362880)))))
    return c, s


def doubled(turn):
    c, s = turn
    return (c - s) * (c + s), 2.0 * (c * s)


def rotations(base, powers, rows):
    sub = lax.broadcasted_iota(jnp.int32, (8, base[0].shape[-1]), 0)
    value = tuple(jnp.broadcast_to(part, sub.shape) for part in base)
    for k in range(3):
        picked = (sub & (1 << k)) != 0
        value = cmul(value, (jnp.where(picked, powers[k][0], 1.0), jnp.where(picked, powers[k][1], 0.0)))
    blocks = [value]
    k = 3
    while len(blocks) * 8 < rows:
        blocks = blocks + [cmul(block, powers[k]) for block in blocks]
        k += 1
    return tuple(jnp.concatenate([block[i] for block in blocks], axis=0)[:rows] for i in (0, 1))


def split(value):
    high = value.astype(jnp.bfloat16)
    return high, (value - high.astype(jnp.float32)).astype(jnp.bfloat16)


def dot_nt(a, b):
    return lax.dot_general(a, b, (((1,), (1,)), ((), ())), preferred_element_type=jnp.float32)


def source_kernel(freqs, wx, half, tiles_y, zslots, xslots, scale, chunks):
    xbits = max(3, (wx - 1).bit_length())
    ybits = max(3, (half - 1).bit_length())
    per = 4 // zslots

    def body(*refs):
        ints, wave_ref, phase_ref = refs[:3]
        cots = refs[3 : 3 + chunks]
        coss = refs[3 + chunks : 3 + 2 * chunks]
        out = refs[3 + 2 * chunks]
        xbase, xpow, ypow, acc_even, acc_odd = refs[4 + 2 * chunks :]
        center = (2 * half - 1) / 2.0
        for n in range(chunks):
            along_x = wave_ref[...] * coss[n][0:1, :]
            along_y = wave_ref[...] * coss[n][1:2, :]
            origin = along_y * center - phase_ref[...]
            for xr in range(xslots):
                angle = along_x * ints[xr].astype(jnp.float32) + origin
                xbase[n, xr, 0] = jnp.cos(angle)
                xbase[n, xr, 1] = jnp.sin(angle)
            turn = doubled(small_turn(0.5 * along_x))
            for k in range(xbits):
                xpow[n, k, 0], xpow[n, k, 1] = turn
                turn = doubled(turn)
            turn = small_turn(0.5 * along_y)
            for k in range(ybits + 1):
                ypow[n, k, 0], ypow[n, k, 1] = turn
                turn = doubled(turn)
        acc_even[...] = jnp.zeros_like(acc_even)
        acc_odd[...] = jnp.zeros_like(acc_odd)
        zcode = ints[xslots]

        def one(f, carry):
            firsts, seconds, coses, sines = [], [], [], []
            for n in range(chunks):
                def row(ref, *where):
                    return tuple(ref[(n, *where, i, pl.ds(f, 1), slice(None))] for i in (0, 1))

                powers = [row(ypow, k) for k in range(ybits + 1)]
                cy, sy = rotations(powers[0], powers[1:], half)
                coses.append(cy)
                sines.append(sy)
                powers = [row(xpow, k) for k in range(xbits)]
                turns = [rotations(row(xbase, xr), powers, wx) for xr in range(xslots)]
                first, second = [], []
                for zr in range(zslots):
                    for xr in range(xslots):
                        cx, sx = turns[xr]
                        for c2 in range(per):
                            at = 2 * ((zcode ^ zr) * per + c2)
                            p = cots[n][f, pl.ds(at, 1), :]
                            q = cots[n][f, pl.ds(at + 1, 1), :]
                            first.append(p * cx - q * sx)
                            second.append(p * sx + q * cx)
                firsts.append(jnp.concatenate(first, axis=0))
                seconds.append(jnp.concatenate(second, axis=0))

            def product(lefts, rights):
                lh, ll = split(jnp.concatenate(lefts, axis=1))
                rh, rl = split(jnp.concatenate(rights, axis=1))
                return dot_nt(lh, rh) + dot_nt(lh, rl) + dot_nt(ll, rh)

            acc_even[...] += product(firsts, coses)
            acc_odd[...] += product(seconds, sines)
            return carry

        lax.fori_loop(0, freqs, one, 0)
        ycode = ints[xslots + 1]
        ybit = bits_of(tiles_y)

        def slot(tile):
            code = gray(tile) ^ ycode
            place = 0
            for k in range(ybit):
                place = place * 2 + ((code >> k) & 1)
            return place

        for j in range(tiles_y // 2):
            lanes = slice(j * LANES, (j + 1) * LANES)
            up = slot(tiles_y // 2 + j)
            down = slot(tiles_y // 2 - 1 - j)
            at = 0
            for zr in range(zslots):
                for xr in range(xslots):
                    for c2 in range(per):
                        rows = slice(at * wx, (at + 1) * wx)
                        even = acc_even[rows, lanes] * scale
                        odd = acc_odd[rows, lanes] * scale
                        out[zr, up, xr, c2] = even - odd
                        out[zr, down, xr, c2] = even + odd
                        at += 1

    return body


def surface_source(cotangent, cosines, wavenumber, time_phase, wx, wy):
    sx, sy, sz = (lax.axis_size(name) for name in ("gx", "gy", "gz"))
    ix, iy, iz = (lax.axis_index(name) for name in ("gx", "gy", "gz"))
    freqs, _, count = cotangent.shape
    scale = 1.0 / math.sqrt(freqs * count * sx * sy * sz)
    assert wy == LANES and sx > 1 and sy > 1
    pad = -count % LANES
    if pad:
        cotangent = jnp.pad(cotangent, ((0, 0), (0, 0), (0, pad)))
        cosines = jnp.pad(cosines, ((0, 0), (0, pad)))
    cots = [cotangent, exchange(cotangent, "gx", 1)]
    coss = [cosines, exchange(cosines, "gx", 1)]
    chunks = 2
    xslots = sx // 2
    zslots = min(sz, 4)
    xbit, ybit, zbit = bits_of(sx), bits_of(sy), bits_of(zslots)
    codes = []
    for slot in range(xslots):
        code = gray(ix)
        for k in range(1, xbit):
            code = code ^ (((slot >> (xbit - 1 - k)) & 1) << k)
        codes.append(ungray(code, xbit) * wx)
    zcode = 0
    for k in range(zbit):
        zcode = zcode * 2 + ((gray(iz) >> k) & 1)
    ints = jnp.stack([*codes, jnp.asarray(zcode, jnp.int32), gray(iy)]).astype(jnp.int32)
    half = sy * wy // 2
    rows = 4 * xslots * wx
    per = 4 // zslots
    xlevels = max(3, (wx - 1).bit_length())
    ylevels = max(3, (half - 1).bit_length()) + 1
    width = count + pad
    smem = pl.BlockSpec(memory_space=pltpu.SMEM)
    vmem = pl.BlockSpec(memory_space=pltpu.VMEM)
    f32 = jnp.float32
    part = pl.pallas_call(
        source_kernel(freqs, wx, half, sy, zslots, xslots, scale, chunks),
        out_shape=jax.ShapeDtypeStruct((zslots, sy, xslots, per, wx, wy), f32),
        in_specs=[smem] + [vmem] * (2 + 2 * chunks),
        out_specs=vmem,
        scratch_shapes=[
            pltpu.VMEM((chunks, xslots, 2, freqs, width), f32),
            pltpu.VMEM((chunks, xlevels, 2, freqs, width), f32),
            pltpu.VMEM((chunks, ylevels, 2, freqs, width), f32),
            pltpu.VMEM((rows, half), f32),
            pltpu.VMEM((rows, half), f32),
        ],
        name="source",
    )(ints, wavenumber[:, None], time_phase[:, None], *cots, *coss)
    for k in range(bits_of(sz)):
        mask = (2 << k) - 1
        if k < zbit:
            half_z = part.shape[0] // 2
            part = part[:half_z] + exchange(part[half_z:], "gz", mask)
        else:
            part = part + exchange(part, "gz", mask)
    part = part[0]
    for k in range(ybit):
        half_y = part.shape[0] // 2
        part = part[:half_y] + exchange(part[half_y:], "gy", (2 << k) - 1)
    part = part[0]
    for k in range(1, xbit):
        half_x = part.shape[0] // 2
        part = part[:half_x] + exchange(part[half_x:], "gx", (2 << k) - 1)
    part = part[0]
    top = gray(sz - 1)
    for k in reversed(range(zbit)):
        other = exchange(part, "gz", (2 << k) - 1)
        part = jnp.concatenate([other, part] if (top >> k) & 1 else [part, other], axis=0)
    return part


def ahead(value, nearby, axis):
    rest = lax.slice_in_dim(value, 1, value.shape[axis], axis=axis)
    return jnp.concatenate([rest, nearby], axis) - value


def behind(value, nearby, axis):
    rest = lax.slice_in_dim(value, 0, value.shape[axis] - 1, axis=axis)
    return value - jnp.concatenate([nearby, rest], axis)


def local(
    e_field, h_field, pole_current, material, pole_table, cotangent, cosines, wavenumber, time_phase
):
    depth, width_x, width_y = material.shape
    source = surface_source(cotangent, cosines, wavenumber, time_phase, width_x, width_y)
    flipped = lax.axis_index("gy") < lax.axis_size("gy") // 2
    source = jnp.where(flipped, source[..., ::-1], source)
    is_top = lax.axis_index("gz") == lax.axis_size("gz") - 1
    top = ((jnp.arange(depth) == depth - 1) & is_top).astype(jnp.float32)[:, None, None]
    next_x = from_behind(e_field[1:3, :, :1, :], "gx", -1)
    next_y = from_behind(e_field[0::2, :, :, :1], "gy", -1)
    next_z = from_behind(e_field[0:2, :1], "gz", -1)
    ex, ey, ez = (e_field[0], e_field[1], e_field[2])
    curl_x = ahead(ez, next_y[1], 2) - ahead(ey, next_z[1], 0)
    curl_y = ahead(ex, next_z[0], 0) - ahead(ez, next_x[1], 1)
    curl_z = ahead(ey, next_x[0], 1) - ahead(ex, next_y[0], 2)
    hx = h_field[0] - courant * curl_x - courant * top * source[2][None]
    hy = h_field[1] - courant * curl_y - courant * top * source[3][None]
    hz = h_field[2] - courant * curl_z
    h_next = jnp.stack([hx, hy, hz])
    prev_x = from_behind(h_next[1:3, :, -1:, :], "gx", 1)
    prev_y = from_behind(h_next[0::2, :, :, -1:], "gy", 1)
    prev_z = from_behind(h_next[0:2, -1:], "gz", 1)
    chosen = (material[None] == jnp.arange(NPOLE, dtype=jnp.int32)[:, None, None, None]).astype(
        jnp.float32
    )
    decay = jnp.sum(chosen * pole_table[0][:, None, None, None], axis=0)
    drive = jnp.sum(chosen * pole_table[1][:, None, None, None], axis=0)
    coef = jnp.sum(chosen * pole_table[2][:, None, None, None], axis=0)
    pole_next = decay[None] * pole_current + drive[None] * e_field
    side_x = behind(hz, prev_y[1], 2) - behind(hy, prev_z[1], 0)
    side_y = behind(hx, prev_z[0], 0) - behind(hz, prev_x[1], 1)
    side_z = behind(hy, prev_x[0], 1) - behind(hx, prev_y[0], 2)
    curl_h = jnp.stack([side_x, side_y, side_z])
    inject = jnp.stack([top * source[0][None], top * source[1][None], jnp.zeros_like(ex)])
    e_next = (
        e_field + coef[None] * (curl_h - 0.5 * (pole_next + pole_current)) - coef[None] * inject
    )
    return (e_next, h_next, pole_next)


def solution(mesh):
    in_specs = (
        P(None, "gz", "gx", "gy"),
        P(None, "gz", "gx", "gy"),
        P(None, "gz", "gx", "gy"),
        P("gz", "gx", "gy"),
        P(),
        P(None, None, ("gx", "gy", "gz")),
        P(None, ("gx", "gy", "gz")),
        P(),
        P(),
    )
    out_specs = (P(None, "gz", "gx", "gy"), P(None, "gz", "gx", "gy"), P(None, "gz", "gx", "gy"))
    return jax.shard_map(local, mesh=mesh, in_specs=in_specs, out_specs=out_specs, check_vma=False)
```

```python
import math

import jax
import jax.numpy as jnp
from jax import lax
from jax.experimental import pallas as pl
from jax.experimental.pallas import tpu as pltpu
from jax.sharding import PartitionSpec as P

NPOLE = 4
LANES = 128


courant = 0.5


def exchange(array, axis, mask):
    return lax.ppermute(array, axis, [(i, i ^ mask) for i in range(lax.axis_size(axis))])


def gray(index):
    return index ^ (index >> 1)


def ungray(code, bits):
    index = code
    for step in range(1, bits):
        index = index ^ (code >> step)
    return index


def bits_of(size):
    return size.bit_length() - 1


def cmul(a, b):
    return (a[0] * b[0] - a[1] * b[1], a[0] * b[1] + a[1] * b[0])


def small_turn(angle):
    q = angle * angle
    c = 1.0 + q * (-1 / 2 + q * (1 / 24 + q * (-1 / 720 + q * (1 / 40320))))
    s = angle * (1.0 + q * (-1 / 6 + q * (1 / 120 + q * (-1 / 5040 + q * (1 / 362880)))))
    return c, s


def doubled(turn):
    c, s = turn
    return (c - s) * (c + s), 2.0 * (c * s)


def rotations(base, powers, rows):
    sub = lax.broadcasted_iota(jnp.int32, (8, base[0].shape[-1]), 0)
    value = tuple(jnp.broadcast_to(part, sub.shape) for part in base)
    for k in range(3):
        picked = (sub & (1 << k)) != 0
        value = cmul(value, (jnp.where(picked, powers[k][0], 1.0), jnp.where(picked, powers[k][1], 0.0)))
    blocks = [value]
    k = 3
    while len(blocks) * 8 < rows:
        blocks = blocks + [cmul(block, powers[k]) for block in blocks]
        k += 1
    return tuple(jnp.concatenate([block[i] for block in blocks], axis=0)[:rows] for i in (0, 1))


def split(value):
    high = value.astype(jnp.bfloat16)
    return high, (value - high.astype(jnp.float32)).astype(jnp.bfloat16)


def dot_nt(a, b):
    return lax.dot_general(a, b, (((1,), (1,)), ((), ())), preferred_element_type=jnp.float32)


def source_kernel(freqs, wx, half, sizes, zslots, xslots, scale, chunks):
    sx, sy, sz = sizes
    xbits = max(3, (wx - 1).bit_length())
    ybits = max(3, (half - 1).bit_length())
    per = 4 // zslots
    main = 4 * xslots * wx

    def body(*refs):
        wave_ref, phase_ref = refs[:2]
        cots = refs[2 : 2 + chunks]
        coss = refs[2 + chunks : 2 + 2 * chunks]
        keep, send = refs[2 + 2 * chunks : 4 + 2 * chunks]
        xbase, xpow, ypow, acc_even, acc_odd = refs[4 + 2 * chunks :]
        ix, iy, iz = (lax.axis_index(name) for name in ("gx", "gy", "gz"))
        xbit, ybit, zbit = bits_of(sx), bits_of(sy), bits_of(zslots)
        starts = []
        for slot in range(xslots):
            code = gray(ix)
            for k in range(1, xbit):
                code = code ^ (((slot >> (xbit - 1 - k)) & 1) << k)
            starts.append((ungray(code, xbit) * wx).astype(jnp.float32))
        zcode = 0
        for k in range(zbit):
            zcode = zcode * 2 + ((gray(iz) >> k) & 1)
        ycode = gray(iy)
        center = (2 * half - 1) / 2.0
        which = lax.broadcasted_iota(jnp.int32, (freqs, 1), 0)
        wave = jnp.zeros((freqs, 1), jnp.float32)
        phase = jnp.zeros((freqs, 1), jnp.float32)
        for f in range(freqs):
            wave = jnp.where(which == f, wave_ref[f], wave)
            phase = jnp.where(which == f, phase_ref[f], phase)
        for n in range(chunks):
            along_x = wave * coss[n][0:1, :]
            along_y = wave * coss[n][1:2, :]
            origin = along_y * center - phase
            for xr in range(xslots):
                angle = along_x * starts[xr] + origin
                xbase[n, xr, 0] = jnp.cos(angle)
                xbase[n, xr, 1] = jnp.sin(angle)
            turn = doubled(small_turn(0.5 * along_x))
            for k in range(xbits):
                xpow[n, k, 0], xpow[n, k, 1] = turn
                turn = doubled(turn)
            turn = small_turn(0.5 * along_y)
            for k in range(ybits + 1):
                ypow[n, k, 0], ypow[n, k, 1] = turn
                turn = doubled(turn)
        acc_even[...] = jnp.zeros_like(acc_even)
        acc_odd[...] = jnp.zeros_like(acc_odd)

        def one(f, carry):
            firsts, seconds, coses, sines = [], [], [], []
            for n in range(chunks):
                def row(ref, *where):
                    return tuple(ref[(n, *where, i, pl.ds(f, 1), slice(None))] for i in (0, 1))

                powers = [row(ypow, k) for k in range(ybits + 1)]
                cy, sy_ = rotations(powers[0], powers[1:], half)
                coses.append(cy)
                sines.append(sy_)
                powers = [row(xpow, k) for k in range(xbits)]
                bases = [row(xbase, xr) for xr in range(xslots)]
                turns = [rotations(base, powers, wx) for base in bases]
                first, second = [], []
                for zr in range(zslots):
                    for xr in range(xslots):
                        cx, sx_ = turns[xr]
                        for c2 in range(per):
                            at = 2 * ((zcode ^ zr) * per + c2)
                            p = cots[n][f, pl.ds(at, 1), :]
                            q = cots[n][f, pl.ds(at + 1, 1), :]
                            first.append(p * cx - q * sx_)
                            second.append(p * sx_ + q * cx)
                back = (powers[0][0], -powers[0][1])
                p = cots[n][f, 6:7, :]
                q = cots[n][f, 7:8, :]
                line = lax.broadcasted_iota(jnp.int32, (8, p.shape[-1]), 0)
                one_first = jnp.zeros(line.shape, jnp.float32)
                one_second = one_first
                for xr in range(xslots):
                    cx, sx_ = cmul(bases[xr], back)
                    one_first = jnp.where(line == xr, p * cx - q * sx_, one_first)
                    one_second = jnp.where(line == xr, p * sx_ + q * cx, one_second)
                firsts.append(jnp.concatenate(first + [one_first], axis=0))
                seconds.append(jnp.concatenate(second + [one_second], axis=0))

            def product(lefts, rights):
                lh, ll = split(jnp.concatenate(lefts, axis=1))
                rh, rl = split(jnp.concatenate(rights, axis=1))
                return dot_nt(lh, rh) + dot_nt(lh, rl) + dot_nt(ll, rh)

            acc_even[...] += product(firsts, coses)
            acc_odd[...] += product(seconds, sines)
            return carry

        lax.fori_loop(0, freqs, one, 0)

        def slot(tile):
            code = gray(tile) ^ ycode
            place = 0
            for k in range(ybit):
                place = place * 2 + ((code >> k) & 1)
            return place

        def place(zr):
            return (keep, zr) if zr < zslots // 2 else (send, zr - zslots // 2)

        extra = per * wx
        for zr in range(zslots):
            ref, z = place(zr)
            for y in range(sy):
                for xr in range(xslots):
                    ref[z, y, xr, extra : extra + 8] = jnp.zeros((8, LANES), jnp.float32)
        turned = 2 // per
        spare = 2 % per
        for j in range(sy // 2):
            lanes = slice(j * LANES, (j + 1) * LANES)
            up = slot(sy // 2 + j)
            down = slot(sy // 2 - 1 - j)
            at = 0
            for zr in range(zslots):
                ref, z = place(zr)
                for xr in range(xslots):
                    for c2 in range(per):
                        rows = slice(at * wx, (at + 1) * wx)
                        even = acc_even[rows, lanes] * scale
                        odd = acc_odd[rows, lanes] * scale
                        ref[z, up, xr, c2 * wx : (c2 + 1) * wx] = even - odd
                        ref[z, down, xr, c2 * wx : (c2 + 1) * wx] = even + odd
                        at += 1
            for xr in range(xslots):
                even = acc_even[main + xr : main + xr + 1, lanes] * scale
                odd = acc_odd[main + xr : main + xr + 1, lanes] * scale
                for zr in range(zslots):
                    ref, z = place(zr)
                    ref[z, up, xr, extra : extra + 1] = even - odd
                    ref[z, down, xr, extra : extra + 1] = even + odd
                start = (((zcode ^ turned) * xslots + xr) * per + spare) * wx
                rows = pl.ds(pl.multiple_of(start, wx), wx)
                even = (acc_even[rows, lanes] * scale).T
                odd = (acc_odd[rows, lanes] * scale).T
                lower = slot(sy // 2 - j)
                for zr in range(zslots):
                    ref, z = place(zr)
                    ref[z, lower, xr, extra + 1 : extra + 2, 0:wx] = even[0:1] + odd[0:1]
                if j < sy // 2 - 1:
                    upper = slot(sy // 2 + j + 1)
                    for zr in range(zslots):
                        ref, z = place(zr)
                        ref[z, upper, xr, extra + 1 : extra + 2, 0:wx] = even[LANES - 1 :] - odd[LANES - 1 :]

    return body


def near_flags(index, bits):
    low, high = [], []
    for k in range(bits):
        upper = (index >> k) & 1
        rest = index & ((1 << k) - 1)
        low.append(((upper == 1) & (rest == 0)).astype(jnp.float32))
        high.append(((upper == 0) & (rest == (1 << k) - 1)).astype(jnp.float32))
    return low, high


def weighted(flags, values):
    total = flags[0] * values[0]
    for flag, value in zip(flags[1:], values[1:]):
        total = total + flag * value
    return total


def column_kernel(depth, wx, wy, zbits):
    def body(*refs):
        e, h, xe = refs[:3]
        zs = refs[3 : 3 + zbits]
        first, last = refs[3 + zbits :]
        low, high = near_flags(lax.axis_index("gz"), zbits)
        lane = lax.broadcasted_iota(jnp.int32, (1, LANES), 1)
        first[...] = jnp.zeros_like(first)
        last[...] = jnp.zeros_like(last)
        for i, field in enumerate((e[0], e[1], e[2], h[0], h[2])):
            turned = field.reshape(depth * wx, wy).T
            first[i : i + 1] = turned[0:1]
            last[i : i + 1] = turned[wy - 1 :]
        for i, layer in (
            (5, weighted(high, [z[1, 0:wx] for z in zs])),
            (6, weighted(low, [z[2, 0:wx] for z in zs])),
        ):
            turned = layer.T
            first[i : i + 1, 0:wx] = turned[0:1]
            last[i : i + 1, 0:wx] = turned[wy - 1 :]
        for ref, y in ((first, 0), (last, wy - 1)):
            corner = jnp.zeros((1, LANES), jnp.float32)
            for z in range(depth):
                corner = jnp.where(lane == z, xe[0, z : z + 1, y : y + 1], corner)
                corner = jnp.where(lane == z * wx + wx - 1, xe[1, z : z + 1, y : y + 1], corner)
            ref[7:8] = corner

    return body


def row_kernel(depth, wx, wy, zbits, ybits, k):
    def body(*refs):
        e, h = refs[:2]
        zs = refs[2 : 2 + zbits]
        ys = refs[2 + zbits : 2 + zbits + ybits]
        out = refs[2 + zbits + ybits]
        zlow, zhigh = near_flags(lax.axis_index("gz"), zbits)
        ylow, yhigh = near_flags(lax.axis_index("gy"), ybits)
        at = (1 - ((lax.axis_index("gx") >> k) & 1)) * (wx - 1)
        for i in range(3):
            for z in range(depth):
                out[i * depth + z : i * depth + z + 1] = e[i, z, pl.ds(at, 1), :]
                out[(3 + i) * depth + z : (3 + i) * depth + z + 1] = h[i, z, pl.ds(at, 1), :]
        base = 6 * depth
        out[base : base + 1] = weighted(zhigh, [z[0, pl.ds(at, 1), :] for z in zs])
        out[base + 1 : base + 2] = weighted(zlow, [z[2, pl.ds(at, 1), :] for z in zs])
        out[base + 2 : base + 3] = weighted(yhigh, [y[0:1] for y in ys])
        out[base + 3 : base + 4] = weighted(ylow, [y[1:2] for y in ys])
        out[base + 4 : base + 8] = jnp.zeros((4, LANES), jnp.float32)

    return body


def field_kernel(depth, wx, wy, xbits, ybits, zbits):
    def body(*refs):
        table, e, h, pole, material, first, xe = refs[:7]
        zs = refs[7 : 7 + zbits]
        ys = refs[7 + zbits : 7 + zbits + ybits]
        xs = refs[7 + zbits + ybits : 6 + zbits + ybits + xbits]
        e_out, h_out, pole_out, e_top, h_top, coef_top = refs[6 + zbits + ybits + xbits :]
        ix, iy, iz = (lax.axis_index(name) for name in ("gx", "gy", "gz"))
        xlow, xhigh = near_flags(ix, xbits)
        ylow, yhigh = near_flags(iy, ybits)
        zlow, zhigh = near_flags(iz, zbits)
        size = depth * wx
        base = 6 * depth
        lane = lax.broadcasted_iota(jnp.int32, (size, wy), 1)
        line = lax.broadcasted_iota(jnp.int32, (size, wy), 0) & (wx - 1)
        inside_x, inside_y, inside_z = (
            (index > 0).astype(jnp.float32) for index in (ix, iy, iz)
        )

        def flat(ref, i):
            return ref[i].reshape(size, wy)

        ex, ey, ez = (flat(e, i) for i in range(3))
        oldx, oldy, oldz = (flat(h, i) for i in range(3))

        def spread(rows):
            return jnp.broadcast_to(rows[:, None, :], (depth, wx, wy)).reshape(size, wy)

        def next_y(value, column):
            rows = value.shape[0]
            return jnp.where(lane[:rows] == wy - 1, column, pltpu.roll(value, wy - 1, 1))

        def next_x(value, rows):
            return jnp.where(line == wx - 1, spread(rows), pltpu.roll(value, size - 1, 0))

        def next_z(value, layer):
            return jnp.concatenate([value[wx:], layer], axis=0)

        def last_y(value, column):
            return jnp.where(lane == 0, column, pltpu.roll(value, 1, 1))

        def last_x(value, rows):
            return jnp.where(line == 0, spread(rows), pltpu.roll(value, 1, 0))

        def last_z(value, layer):
            return jnp.concatenate([layer, value[:-wx]], axis=0)

        ylo = weighted(ylow, [y[...] for y in ys])
        yhi = weighted(yhigh, [y[...] for y in ys])
        above = yhi.T

        def rows_of(flags, i):
            at = slice(i * depth, (i + 1) * depth)
            return weighted(flags, [xe[i]] + [x[at] for x in xs])

        def extra_of(flags, early, i):
            return weighted(flags, [early] + [x[base + i : base + i + 1] for x in xs])

        def layer_of(flags, i):
            return weighted(flags, [z[i, 0:wx] for z in zs])

        def side_of(flags, i):
            return weighted(flags, [z[i, wx : wx + 1] for z in zs])

        up_x, up_y = layer_of(zhigh, 0), layer_of(zhigh, 1)
        hx = oldx - courant * ((next_y(ez, above[:, 2:3]) - ez) - (next_z(ey, up_y) - ey))
        hy = oldy - courant * (
            (next_z(ex, up_x) - ex) - (next_x(ez, rows_of(xhigh, 2)) - ez)
        )
        hz = oldz - courant * (
            (next_x(ey, rows_of(xhigh, 1)) - ey) - (next_y(ex, above[:, 0:1]) - ex)
        )
        mx, my, mz = (rows_of(xlow, i) for i in range(3))
        up = jnp.concatenate([mx[1:], extra_of(xlow, side_of(zhigh, 0), 0)], axis=0)
        low_hy = rows_of(xlow, 4) - courant * ((up - mx) - (e[2, :, 0, :] - mz))
        corner = xlow[0] * above[0:depth, 7:8]
        for flag, x in zip(xlow[1:], xs):
            tail = x[base : base + 8].T
            picks = [tail[z * wx + wx - 1 : (z + 1) * wx, 2:3] for z in range(depth)]
            corner = corner + flag * jnp.concatenate(picks, axis=0)
        low_hz = rows_of(xlow, 5) - courant * (
            (e[1, :, 0, :] - my) - (next_y(mx, corner) - mx)
        )
        strip = lax.broadcasted_iota(jnp.int32, (1, LANES), 1)
        lx, ly, lz = ylo[0:1], ylo[1:2], ylo[2:3]
        up = jnp.where(
            strip >= size - wx, pltpu.roll(ylo[5:6], size - wx, 1), pltpu.roll(ly, LANES - wx, 1)
        )
        side_hx = ylo[3:4] - courant * ((first[2:3] - lz) - (up - ly))
        corner = xhigh[0] * ylo[7:8]
        for flag, x in zip(xhigh[1:], xs):
            corner = corner + flag * pltpu.roll(x[base + 3 : base + 4], wx - 1, 1)
        right = jnp.where((strip & (wx - 1)) == wx - 1, corner, pltpu.roll(ly, LANES - 1, 1))
        side_hz = ylo[4:5] - courant * ((right - ly) - (first[0:1] - lx))
        both = jnp.concatenate([side_hx, side_hz, jnp.zeros((6, LANES), jnp.float32)], axis=0)
        both = (inside_y * both).T
        bx, by, bz = (layer_of(zlow, i) for i in range(3))
        under_hx = layer_of(zlow, 3) - courant * (
            (next_y(bz, above[0:wx, 6:7]) - bz) - (ey[:wx] - by)
        )
        right = jnp.concatenate([bz[1:], extra_of(xhigh, side_of(zlow, 2), 1)], axis=0)
        under_hy = layer_of(zlow, 4) - courant * ((ex[:wx] - bx) - (right - bz))
        under_hx = inside_z * under_hx
        under_hy = inside_z * under_hy
        low_hy = inside_x * low_hy
        low_hz = inside_x * low_hz
        curl = (
            (hz - last_y(hz, both[:, 1:2])) - (hy - last_z(hy, under_hy)),
            (hx - last_z(hx, under_hx)) - (hz - last_x(hz, low_hz)),
            (hy - last_x(hy, low_hy)) - (hx - last_y(hx, both[:, 0:1])),
        )
        kind = material[...].reshape(size, wy)

        def chosen(i):
            value = jnp.full((size, wy), table[i, NPOLE - 1], jnp.float32)
            for m in range(NPOLE - 1):
                value = jnp.where(kind == m, table[i, m], value)
            return value

        decay, drive, coef = (chosen(i) for i in range(3))
        shape = (depth, wx, wy)
        tail = size - wx
        for i, (electric, magnetic) in enumerate(zip((ex, ey, ez), (hx, hy, hz))):
            old = flat(pole, i)
            new = decay * old + drive * electric
            value = electric + coef * (curl[i] - 0.5 * (new + old))
            pole_out[i] = new.reshape(shape)
            h_out[i] = magnetic.reshape(shape)
            e_out[i] = value.reshape(shape)
            e_top[i] = value[tail:]
            h_top[i] = magnetic[tail:]
        coef_top[...] = coef[tail:]

    return body


def inject_kernel(depth, wx, wy, sz, per):
    def body(source, col, e_top, h_top, coef_top, e_in, h_in, e_out, h_out, e_new, h_new, sems):
        ix, iy, iz = (lax.axis_index(name) for name in ("gx", "gy", "gz"))

        @pl.when(iz == sz - 1)
        def _():
            inside_x, inside_y = ((index > 0).astype(jnp.float32) for index in (ix, iy))
            lane = lax.broadcasted_iota(jnp.int32, (wx, wy), 1)
            line = lax.broadcasted_iota(jnp.int32, (wx, wy), 0)
            block = per * wx + 8

            def channel(c):
                start = (c // per) * block + (c % per) * wx
                return source[start : start + wx]

            electric_x, electric_y, magnetic_x, magnetic_y = (channel(c) for c in range(4))
            start = (3 // per) * block + per * wx
            before = inside_x * source[start : start + 1]
            beside = inside_y * col[...].T[0:wx, 1:2]
            last_x = jnp.where(line == 0, before, pltpu.roll(magnetic_y, 1, 0))
            last_y = jnp.where(lane == 0, beside, pltpu.roll(magnetic_x, 1, 1))
            coef = coef_top[...]
            h_new[0] = h_top[0] - courant * magnetic_x
            h_new[1] = h_top[1] - courant * magnetic_y
            e_new[0] = e_top[0] + coef * (courant * magnetic_y - electric_x)
            e_new[1] = e_top[1] - coef * (courant * magnetic_x + electric_y)
            e_new[2] = e_top[2] + coef * courant * (
                (magnetic_x - last_y) - (magnetic_y - last_x)
            )
            copies = [
                pltpu.make_async_copy(e_new, e_out.at[:, depth - 1], sems.at[0]),
                pltpu.make_async_copy(h_new, h_out.at[0:2, depth - 1], sems.at[1]),
            ]
            for copy in copies:
                copy.start()
            for copy in copies:
                copy.wait()

    return body


def in_vmem(*arrays):
    return [pltpu.with_memory_space_constraint(array, pltpu.VMEM) for array in arrays]


def local(
    e_field, h_field, pole_current, material, pole_table, cotangent, cosines, wavenumber, time_phase
):
    depth, wx, wy = material.shape
    sizes = sx, sy, sz = tuple(lax.axis_size(name) for name in ("gx", "gy", "gz"))
    ix, iy, iz = (lax.axis_index(name) for name in ("gx", "gy", "gz"))
    freqs, _, count = cotangent.shape
    scale = 1.0 / math.sqrt(freqs * count * sx * sy * sz)
    assert wy == LANES and depth * wx == LANES and sx > 1 and sy > 1 and sz > 1
    pad = -count % LANES
    if pad:
        cotangent = jnp.pad(cotangent, ((0, 0), (0, 0), (0, pad)))
        cosines = jnp.pad(cosines, ((0, 0), (0, pad)))
    f32 = jnp.float32
    smem = pl.BlockSpec(memory_space=pltpu.SMEM)
    vmem = pl.BlockSpec(memory_space=pltpu.VMEM)
    hbm = pl.BlockSpec(memory_space=pl.ANY)
    small = pltpu.CompilerParams(vmem_limit_bytes=8 << 20)
    xslots = sx // 2
    zslots = min(sz, 4)
    per = 4 // zslots
    xbits, ybits, zbits = bits_of(sx), bits_of(sy), bits_of(sz)
    zcut = bits_of(zslots)

    cots = [cotangent, exchange(cotangent, "gx", 1)]
    coss = [cosines, exchange(cosines, "gx", 1)]
    at = (1 - (ix & 1)) * (wx - 1)
    rows = [lax.dynamic_index_in_dim(v, at, 2, keepdims=False) for v in (e_field, h_field)]
    xe = exchange(jnp.concatenate(rows, axis=0), "gx", 1)
    zs = []
    for k in range(zbits):
        at = (1 - ((iz >> k) & 1)) * (depth - 1)
        layers = [lax.dynamic_index_in_dim(v, at, 1, keepdims=False) for v in (e_field, h_field)]
        side = lax.dynamic_slice_in_dim(xe, at, 1, axis=1)
        message = jnp.concatenate([jnp.concatenate(layers, axis=0), side], axis=1)
        zs.append(exchange(message, "gz", (2 << k) - 1))

    half = sy * wy // 2
    xlevels = max(3, (wx - 1).bit_length())
    ylevels = max(3, (half - 1).bit_length()) + 1
    width = count + pad
    block = per * wx + 8
    part_shape = pltpu.VMEM((zslots // 2, sy, xslots, block, wy), f32)
    keep, send = pl.pallas_call(
        source_kernel(freqs, wx, half, sizes, zslots, xslots, scale, 2),
        out_shape=(part_shape, part_shape),
        in_specs=[smem, smem] + [vmem] * 4,
        out_specs=(vmem, vmem),
        scratch_shapes=[
            pltpu.VMEM((2, xslots, 2, freqs, width), f32),
            pltpu.VMEM((2, xlevels, 2, freqs, width), f32),
            pltpu.VMEM((2, ylevels, 2, freqs, width), f32),
            pltpu.VMEM((4 * xslots * wx + 8, half), f32),
            pltpu.VMEM((4 * xslots * wx + 8, half), f32),
        ],
        compiler_params=pltpu.CompilerParams(vmem_limit_bytes=24 << 20),
        name="source",
    )(wavenumber, time_phase, *in_vmem(*cots, *coss))

    e_near, h_near = in_vmem(e_field, h_field)
    strip = pltpu.VMEM((8, LANES), f32)
    first, last = pl.pallas_call(
        column_kernel(depth, wx, wy, zbits),
        out_shape=(strip, strip),
        in_specs=[vmem] * (3 + zbits),
        out_specs=(vmem, vmem),
        compiler_params=small,
        name="columns",
    )(e_near, h_near, *in_vmem(xe, *zs))

    part = keep + exchange(send, "gz", 1)
    for k in range(1, zbits):
        mask = (2 << k) - 1
        if k < zcut:
            cut = part.shape[0] // 2
            part = part[:cut] + exchange(part[cut:], "gz", mask)
        else:
            part = part + exchange(part, "gz", mask)
    part = part[0]

    def swap(part, halo, axis, k):
        cut = part.shape[0] // 2
        away = part[cut:].reshape(-1, LANES)
        got = exchange(jnp.concatenate([away, halo], axis=0), axis, (2 << k) - 1)
        return part[:cut] + got[: away.shape[0]].reshape(part[:cut].shape), got[away.shape[0] :]

    ys = []
    for k in range(ybits):
        part, halo = swap(part, jnp.where((iy >> k) & 1 == 1, first, last), "gy", k)
        ys.append(halo)
    part = part[0]
    near = in_vmem(*zs, *ys)
    xs = []
    for k in range(1, xbits):
        halo = pl.pallas_call(
            row_kernel(depth, wx, wy, zbits, ybits, k),
            out_shape=pltpu.VMEM((6 * depth + 8, LANES), f32),
            in_specs=[vmem] * (2 + zbits + ybits),
            out_specs=vmem,
            compiler_params=small,
            name="rows",
        )(e_near, h_near, *near)
        part, halo = swap(part, halo, "gx", k)
        xs.append(halo)
    part = part[0]

    whole = jax.ShapeDtypeStruct((3, depth, wx, wy), f32)
    layer = pltpu.VMEM((3, wx, wy), f32)
    e_next, h_next, pole_next, e_top, h_top, coef_top = pl.pallas_call(
        field_kernel(depth, wx, wy, xbits, ybits, zbits),
        out_shape=(whole, whole, whole, layer, layer, pltpu.VMEM((wx, wy), f32)),
        in_specs=[smem] + [vmem] * (5 + xbits + ybits + zbits),
        out_specs=(vmem,) * 6,
        compiler_params=pltpu.CompilerParams(vmem_limit_bytes=16 << 20),
        name="fields",
    )(
        pole_table,
        e_near,
        h_near,
        *in_vmem(pole_current, material, first, xe),
        *near,
        *in_vmem(*xs),
    )

    top = gray(sz - 1)
    for k in reversed(range(zcut)):
        other = exchange(part, "gz", (2 << k) - 1)
        part = jnp.concatenate([other, part] if (top >> k) & 1 else [part, other], axis=0)
    flipped = iy < sy // 2
    source = jnp.where(flipped, part[:, ::-1], part)
    start = (2 // per) * block + per * wx
    col = part[start : start + 8]
    e_next, h_next = pl.pallas_call(
        inject_kernel(depth, wx, wy, sz, per),
        out_shape=(whole, whole),
        in_specs=[vmem] * 5 + [hbm] * 2,
        out_specs=(hbm, hbm),
        scratch_shapes=[
            pltpu.VMEM((3, wx, wy), f32),
            pltpu.VMEM((2, wx, wy), f32),
            pltpu.SemaphoreType.DMA((2,)),
        ],
        input_output_aliases={5: 0, 6: 1},
        compiler_params=small,
        name="inject",
    )(*in_vmem(source, col, e_top, h_top, coef_top), e_next, h_next)
    return (e_next, h_next, pole_next)


def solution(mesh):
    in_specs = (
        P(None, "gz", "gx", "gy"),
        P(None, "gz", "gx", "gy"),
        P(None, "gz", "gx", "gy"),
        P("gz", "gx", "gy"),
        P(),
        P(None, None, ("gx", "gy", "gz")),
        P(None, ("gx", "gy", "gz")),
        P(),
        P(),
    )
    out_specs = (P(None, "gz", "gx", "gy"), P(None, "gz", "gx", "gy"), P(None, "gz", "gx", "gy"))
    return jax.shard_map(local, mesh=mesh, in_specs=in_specs, out_specs=out_specs, check_vma=False)
```

```python
import math

import jax
import jax.numpy as jnp
from jax import lax
from jax.experimental import pallas as pl
from jax.experimental.pallas import tpu as pltpu
from jax.sharding import PartitionSpec as P

NPOLE = 4
LANES = 128


courant = 0.5


def exchange(array, axis, mask):
    return lax.ppermute(array, axis, [(i, i ^ mask) for i in range(lax.axis_size(axis))])


def gray(index):
    return index ^ (index >> 1)


def ungray(code, bits):
    index = code
    for step in range(1, bits):
        index = index ^ (code >> step)
    return index


def bits_of(size):
    return size.bit_length() - 1


def cmul(a, b):
    return (a[0] * b[0] - a[1] * b[1], a[0] * b[1] + a[1] * b[0])


def small_turn(angle):
    q = angle * angle
    c = 1.0 + q * (-1 / 2 + q * (1 / 24 + q * (-1 / 720 + q * (1 / 40320))))
    s = angle * (1.0 + q * (-1 / 6 + q * (1 / 120 + q * (-1 / 5040 + q * (1 / 362880)))))
    return c, s


def doubled(turn):
    c, s = turn
    return (c - s) * (c + s), 2.0 * (c * s)


def rotations(base, powers, rows):
    sub = lax.broadcasted_iota(jnp.int32, (8, base[0].shape[-1]), 0)
    value = tuple(jnp.broadcast_to(part, sub.shape) for part in base)
    for k in range(3):
        picked = (sub & (1 << k)) != 0
        value = cmul(value, (jnp.where(picked, powers[k][0], 1.0), jnp.where(picked, powers[k][1], 0.0)))
    blocks = [value]
    k = 3
    while len(blocks) * 8 < rows:
        blocks = blocks + [cmul(block, powers[k]) for block in blocks]
        k += 1
    return tuple(jnp.concatenate([block[i] for block in blocks], axis=0)[:rows] for i in (0, 1))


def split(value):
    high = value.astype(jnp.bfloat16)
    return high, (value - high.astype(jnp.float32)).astype(jnp.bfloat16)


def dot_nt(a, b):
    return lax.dot_general(a, b, (((1,), (1,)), ((), ())), preferred_element_type=jnp.float32)


def source_kernel(freqs, wx, half, sizes, zslots, xslots, scale, chunks):
    sx, sy, sz = sizes
    xbits = max(3, (wx - 1).bit_length())
    ybits = max(3, (half - 1).bit_length())
    per = 4 // zslots
    main = 4 * xslots * wx

    def body(*refs):
        waves = refs[0]
        cots = refs[1 : 1 + chunks]
        keep, send = refs[1 + chunks : 3 + chunks]
        xbase, xpow, ypow, acc_even, acc_odd = refs[3 + chunks :]
        ix, iy, iz = (lax.axis_index(name) for name in ("gx", "gy", "gz"))
        xbit, ybit, zbit = bits_of(sx), bits_of(sy), bits_of(zslots)
        starts = []
        for slot in range(xslots):
            code = gray(ix)
            for k in range(1, xbit):
                code = code ^ (((slot >> (xbit - 1 - k)) & 1) << k)
            starts.append((ungray(code, xbit) * wx).astype(jnp.float32))
        zcode = 0
        for k in range(zbit):
            zcode = zcode * 2 + ((gray(iz) >> k) & 1)
        ycode = gray(iy)
        center = (2 * half - 1) / 2.0
        wave, phase = waves[0], waves[1]
        for n in range(chunks):
            along_x = wave * cots[n][freqs, 0:1, :]
            along_y = wave * cots[n][freqs, 1:2, :]
            origin = along_y * center - phase
            for xr in range(xslots):
                angle = along_x * starts[xr] + origin
                xbase[n, xr, 0] = jnp.cos(angle)
                xbase[n, xr, 1] = jnp.sin(angle)
            turn = doubled(small_turn(0.5 * along_x))
            for k in range(xbits):
                xpow[n, k, 0], xpow[n, k, 1] = turn
                turn = doubled(turn)
            turn = small_turn(0.5 * along_y)
            for k in range(ybits + 1):
                ypow[n, k, 0], ypow[n, k, 1] = turn
                turn = doubled(turn)
        acc_even[...] = jnp.zeros_like(acc_even)
        acc_odd[...] = jnp.zeros_like(acc_odd)

        def one(f, carry):
            firsts, seconds, coses, sines = [], [], [], []
            for n in range(chunks):
                def row(ref, *where):
                    return tuple(ref[(n, *where, i, pl.ds(f, 1), slice(None))] for i in (0, 1))

                powers = [row(ypow, k) for k in range(ybits + 1)]
                cy, sy_ = rotations(powers[0], powers[1:], half)
                coses.append(cy)
                sines.append(sy_)
                powers = [row(xpow, k) for k in range(xbits)]
                bases = [row(xbase, xr) for xr in range(xslots)]
                turns = [rotations(base, powers, wx) for base in bases]
                first, second = [], []
                for zr in range(zslots):
                    for xr in range(xslots):
                        cx, sx_ = turns[xr]
                        for c2 in range(per):
                            at = 2 * ((zcode ^ zr) * per + c2)
                            p = cots[n][f, pl.ds(at, 1), :]
                            q = cots[n][f, pl.ds(at + 1, 1), :]
                            first.append(p * cx - q * sx_)
                            second.append(p * sx_ + q * cx)
                back = (powers[0][0], -powers[0][1])
                p = cots[n][f, 6:7, :]
                q = cots[n][f, 7:8, :]
                line = lax.broadcasted_iota(jnp.int32, (8, p.shape[-1]), 0)
                one_first = jnp.zeros(line.shape, jnp.float32)
                one_second = one_first
                for xr in range(xslots):
                    cx, sx_ = cmul(bases[xr], back)
                    one_first = jnp.where(line == xr, p * cx - q * sx_, one_first)
                    one_second = jnp.where(line == xr, p * sx_ + q * cx, one_second)
                firsts.append(jnp.concatenate(first + [one_first], axis=0))
                seconds.append(jnp.concatenate(second + [one_second], axis=0))

            def product(lefts, rights):
                lh, ll = split(jnp.concatenate(lefts, axis=1))
                rh, rl = split(jnp.concatenate(rights, axis=1))
                return dot_nt(lh, rh) + dot_nt(lh, rl) + dot_nt(ll, rh)

            acc_even[...] += product(firsts, coses)
            acc_odd[...] += product(seconds, sines)
            return carry

        lax.fori_loop(0, freqs, one, 0)

        def slot(tile):
            code = gray(tile) ^ ycode
            place = 0
            for k in range(ybit):
                place = place * 2 + ((code >> k) & 1)
            return place

        def place(zr):
            return (keep, zr) if zr < zslots // 2 else (send, zr - zslots // 2)

        extra = per * wx
        for zr in range(zslots):
            ref, z = place(zr)
            for y in range(sy):
                for xr in range(xslots):
                    ref[z, y, xr, extra : extra + 8] = jnp.zeros((8, LANES), jnp.float32)
        turned = 2 // per
        spare = 2 % per
        for j in range(sy // 2):
            lanes = slice(j * LANES, (j + 1) * LANES)
            up = slot(sy // 2 + j)
            down = slot(sy // 2 - 1 - j)
            at = 0
            for zr in range(zslots):
                ref, z = place(zr)
                for xr in range(xslots):
                    for c2 in range(per):
                        rows = slice(at * wx, (at + 1) * wx)
                        even = acc_even[rows, lanes] * scale
                        odd = acc_odd[rows, lanes] * scale
                        ref[z, up, xr, c2 * wx : (c2 + 1) * wx] = even - odd
                        ref[z, down, xr, c2 * wx : (c2 + 1) * wx] = even + odd
                        at += 1
            for xr in range(xslots):
                even = acc_even[main + xr : main + xr + 1, lanes] * scale
                odd = acc_odd[main + xr : main + xr + 1, lanes] * scale
                for zr in range(zslots):
                    ref, z = place(zr)
                    ref[z, up, xr, extra : extra + 1] = even - odd
                    ref[z, down, xr, extra : extra + 1] = even + odd
                start = (((zcode ^ turned) * xslots + xr) * per + spare) * wx
                rows = pl.ds(pl.multiple_of(start, wx), wx)
                even = (acc_even[rows, lanes] * scale).T
                odd = (acc_odd[rows, lanes] * scale).T
                lower = slot(sy // 2 - j)
                for zr in range(zslots):
                    ref, z = place(zr)
                    ref[z, lower, xr, extra + 1 : extra + 2, 0:wx] = even[0:1] + odd[0:1]
                if j < sy // 2 - 1:
                    upper = slot(sy // 2 + j + 1)
                    for zr in range(zslots):
                        ref, z = place(zr)
                        ref[z, upper, xr, extra + 1 : extra + 2, 0:wx] = even[LANES - 1 :] - odd[LANES - 1 :]

    return body


def near_flags(index, bits):
    low, high = [], []
    for k in range(bits):
        upper = (index >> k) & 1
        rest = index & ((1 << k) - 1)
        low.append(((upper == 1) & (rest == 0)).astype(jnp.float32))
        high.append(((upper == 0) & (rest == (1 << k) - 1)).astype(jnp.float32))
    return low, high


def weighted(flags, values):
    total = flags[0] * values[0]
    for flag, value in zip(flags[1:], values[1:]):
        total = total + flag * value
    return total


def pack_kernel(freqs, depth, wx, zbits):
    def body(*refs):
        e_in, h_in, cotangent, cosines, wavenumber, time_phase = refs[:6]
        message, waves, e, h = refs[6:10]
        layers = refs[10 : 10 + zbits]
        cos_near, wave_near, phase_near, sems = refs[10 + zbits :]
        copies = [
            pltpu.make_async_copy(source, target, sems.at[i])
            for i, (source, target) in enumerate(
                (
                    (e_in, e),
                    (h_in, h),
                    (cotangent, message.at[0:freqs]),
                    (cosines, cos_near),
                    (wavenumber, wave_near),
                    (time_phase, phase_near),
                )
            )
        ]
        for copy in copies:
            copy.start()
        for copy in copies:
            copy.wait()
        message[freqs, 0:2] = cos_near[...]
        message[freqs, 2:8] = jnp.zeros((6, LANES), jnp.float32)
        which = lax.broadcasted_iota(jnp.int32, (freqs, LANES), 0)
        for i, near in enumerate((wave_near, phase_near)):
            value = jnp.zeros((freqs, LANES), jnp.float32)
            for f in range(freqs):
                value = jnp.where(which == f, near[f], value)
            waves[i] = value
        at = (1 - (lax.axis_index("gx") & 1)) * (wx - 1)
        for i in range(6):
            for z in range(depth):
                row = i * depth + z
                field = (e, h)[i // 3]
                message[freqs + 1 + row // 8, row % 8 : row % 8 + 1] = field[i % 3, z, pl.ds(at, 1), :]
        for k, layer in enumerate(layers):
            at_z = (1 - ((lax.axis_index("gz") >> k) & 1)) * (depth - 1)
            for i in range(3):
                layer[i] = e[i, at_z]
                layer[3 + i] = h[i, at_z]

    return body


def early_rows(message, freqs, depth, i):
    row = i * depth
    return message[freqs + 1 + row // 8, row % 8 : row % 8 + depth]


def column_kernel(freqs, depth, wx, wy, zbits):
    def body(*refs):
        e, h, message = refs[:3]
        zs = refs[3 : 3 + zbits]
        first, last = refs[3 + zbits :]
        low, high = near_flags(lax.axis_index("gz"), zbits)
        lane = lax.broadcasted_iota(jnp.int32, (1, LANES), 1)
        first[...] = jnp.zeros_like(first)
        last[...] = jnp.zeros_like(last)
        for i, field in enumerate((e[0], e[1], e[2], h[0], h[2])):
            turned = field.reshape(depth * wx, wy).T
            first[i : i + 1] = turned[0:1]
            last[i : i + 1] = turned[wy - 1 :]
        for i, layer in (
            (5, weighted(high, [z[1, 0:wx] for z in zs])),
            (6, weighted(low, [z[2, 0:wx] for z in zs])),
        ):
            turned = layer.T
            first[i : i + 1, 0:wx] = turned[0:1]
            last[i : i + 1, 0:wx] = turned[wy - 1 :]
        for ref, y in ((first, 0), (last, wy - 1)):
            corner = jnp.zeros((1, LANES), jnp.float32)
            side_x, side_y = (early_rows(message, freqs, depth, i)[:, y : y + 1] for i in (0, 1))
            for z in range(depth):
                corner = jnp.where(lane == z, side_x[z : z + 1], corner)
                corner = jnp.where(lane == z * wx + wx - 1, side_y[z : z + 1], corner)
            ref[7:8] = corner

    return body


def total_of(terms, rows):
    value = terms[0][rows]
    for term in terms[1:]:
        value = value + term[rows]
    return value


def merge_y_kernel(count, rows, k, ybits):
    def body(*refs):
        terms, (first, last), outs = refs[:count], refs[count : count + 2], refs[count + 2 :]
        iy = lax.axis_index("gy")
        size = rows // len(outs)
        swaps = (None, k) if len(outs) == 2 else (None, k + 1, k, None)
        for i, (out, swap) in enumerate(zip(outs, swaps)):
            out[0:size] = total_of(terms, slice(i * size, (i + 1) * size))
            if swap is not None:
                upper = ((iy >> swap) & 1).astype(jnp.float32)
                out[size : size + 8] = upper * first[...] + (1.0 - upper) * last[...]

    return body


def halo_at(ref):
    rows = ref.shape[0]
    return ref[rows - 8 : rows]


def merge_x_kernel(count, rows, depth, wx, wy, zbits, ybits, k):
    def body(*refs):
        terms = refs[:count]
        e, h = refs[count : count + 2]
        zs = refs[count + 2 : count + 2 + zbits]
        ys = refs[count + 2 + zbits : count + 2 + zbits + ybits]
        keep, out = refs[count + 3 + zbits + ybits :]
        size = rows // 2
        keep[...] = total_of(terms, slice(0, size))
        out[0:size] = total_of(terms, slice(size, rows))
        zlow, zhigh = near_flags(lax.axis_index("gz"), zbits)
        ylow, yhigh = near_flags(lax.axis_index("gy"), ybits)
        at = (1 - ((lax.axis_index("gx") >> k) & 1)) * (wx - 1)
        for i in range(3):
            for z in range(depth):
                row = size + i * depth + z
                out[row : row + 1] = e[i, z, pl.ds(at, 1), :]
                row = size + (3 + i) * depth + z
                out[row : row + 1] = h[i, z, pl.ds(at, 1), :]
        base = size + 6 * depth
        halos = [halo_at(y) for y in ys]
        out[base : base + 1] = weighted(zhigh, [z[0, pl.ds(at, 1), :] for z in zs])
        out[base + 1 : base + 2] = weighted(zlow, [z[2, pl.ds(at, 1), :] for z in zs])
        out[base + 2 : base + 3] = weighted(yhigh, [y[0:1] for y in halos])
        out[base + 3 : base + 4] = weighted(ylow, [y[1:2] for y in halos])
        out[base + 4 : base + 8] = jnp.zeros((4, LANES), jnp.float32)

    return body


def pole_kernel(depth, wx, wy):
    def body(table_in, e, pole_in, material_in, after, pole_out, base, coef_out, *scratch):
        table, pole, material, new_pole, sems = scratch
        copies = [
            pltpu.make_async_copy(source, target, sems.at[i])
            for i, (source, target) in enumerate(
                ((table_in, table), (material_in, material), (pole_in, pole))
            )
        ]
        for copy in copies:
            copy.start()
        for copy in copies:
            copy.wait()
        kind = material[...]

        def chosen(i):
            value = jnp.full(kind.shape, table[i, NPOLE - 1], jnp.float32)
            for m in range(NPOLE - 1):
                value = jnp.where(kind == m, table[i, m], value)
            return value

        decay, drive, coef = (chosen(i) for i in range(3))
        coef_out[...] = coef
        for i in range(3):
            old = pole[i]
            electric = e[i]
            new = decay * old + drive * electric
            new_pole[i] = new
            base[i] = electric - coef * (0.5 * (new + old))
        copy = pltpu.make_async_copy(new_pole, pole_out, sems.at[0])
        copy.start()
        copy.wait()

    return body


def field_kernel(freqs, depth, wx, wy, xbits, ybits, zbits):
    def body(*refs):
        e, h, base_e, coef_ref, first, message = refs[:6]
        zs = refs[6 : 6 + zbits]
        ys = refs[6 + zbits : 6 + zbits + ybits]
        xs = [x[x.shape[0] - 6 * depth - 8 :] for x in refs[6 + zbits + ybits : 5 + zbits + ybits + xbits]]
        e_out, h_out, e_top, h_top, coef_top = refs[5 + zbits + ybits + xbits :]
        ix, iy, iz = (lax.axis_index(name) for name in ("gx", "gy", "gz"))
        xlow, xhigh = near_flags(ix, xbits)
        ylow, yhigh = near_flags(iy, ybits)
        zlow, zhigh = near_flags(iz, zbits)
        size = depth * wx
        base = 6 * depth
        lane = lax.broadcasted_iota(jnp.int32, (size, wy), 1)
        line = lax.broadcasted_iota(jnp.int32, (size, wy), 0) & (wx - 1)
        inside_x, inside_y, inside_z = (
            (index > 0).astype(jnp.float32) for index in (ix, iy, iz)
        )

        def flat(ref, i):
            return ref[i].reshape(size, wy)

        ex, ey, ez = (flat(e, i) for i in range(3))
        oldx, oldy, oldz = (flat(h, i) for i in range(3))

        def spread(rows):
            return jnp.broadcast_to(rows[:, None, :], (depth, wx, wy)).reshape(size, wy)

        def next_y(value, column):
            rows = value.shape[0]
            return jnp.where(lane[:rows] == wy - 1, column, pltpu.roll(value, wy - 1, 1))

        def next_x(value, rows):
            return jnp.where(line == wx - 1, spread(rows), pltpu.roll(value, size - 1, 0))

        def next_z(value, layer):
            return jnp.concatenate([value[wx:], layer], axis=0)

        def last_y(value, column):
            return jnp.where(lane == 0, column, pltpu.roll(value, 1, 1))

        def last_x(value, rows):
            return jnp.where(line == 0, spread(rows), pltpu.roll(value, 1, 0))

        def last_z(value, layer):
            return jnp.concatenate([layer, value[:-wx]], axis=0)

        ylo = weighted(ylow, [halo_at(y) for y in ys])
        yhi = weighted(yhigh, [halo_at(y) for y in ys])
        above = yhi.T

        def rows_of(flags, i):
            at = slice(i * depth, (i + 1) * depth)
            return weighted(flags, [early_rows(message, freqs, depth, i)] + [x[at] for x in xs])

        def extra_of(flags, early, i):
            return weighted(flags, [early] + [x[base + i : base + i + 1] for x in xs])

        def layer_of(flags, i):
            return weighted(flags, [z[i, 0:wx] for z in zs])

        def side_of(flags, i):
            return weighted(flags, [z[i, wx : wx + 1] for z in zs])

        up_x, up_y = layer_of(zhigh, 0), layer_of(zhigh, 1)
        hx = oldx - courant * ((next_y(ez, above[:, 2:3]) - ez) - (next_z(ey, up_y) - ey))
        hy = oldy - courant * (
            (next_z(ex, up_x) - ex) - (next_x(ez, rows_of(xhigh, 2)) - ez)
        )
        hz = oldz - courant * (
            (next_x(ey, rows_of(xhigh, 1)) - ey) - (next_y(ex, above[:, 0:1]) - ex)
        )
        mx, my, mz = (rows_of(xlow, i) for i in range(3))
        up = jnp.concatenate([mx[1:], extra_of(xlow, side_of(zhigh, 0), 0)], axis=0)
        low_hy = rows_of(xlow, 4) - courant * ((up - mx) - (e[2, :, 0, :] - mz))
        corner = xlow[0] * above[0:depth, 7:8]
        for flag, x in zip(xlow[1:], xs):
            tail = x[base : base + 8].T
            picks = [tail[z * wx + wx - 1 : (z + 1) * wx, 2:3] for z in range(depth)]
            corner = corner + flag * jnp.concatenate(picks, axis=0)
        low_hz = rows_of(xlow, 5) - courant * (
            (e[1, :, 0, :] - my) - (next_y(mx, corner) - mx)
        )
        strip = lax.broadcasted_iota(jnp.int32, (1, LANES), 1)
        lx, ly, lz = ylo[0:1], ylo[1:2], ylo[2:3]
        up = jnp.where(
            strip >= size - wx, pltpu.roll(ylo[5:6], size - wx, 1), pltpu.roll(ly, LANES - wx, 1)
        )
        side_hx = ylo[3:4] - courant * ((first[2:3] - lz) - (up - ly))
        corner = xhigh[0] * ylo[7:8]
        for flag, x in zip(xhigh[1:], xs):
            corner = corner + flag * pltpu.roll(x[base + 3 : base + 4], wx - 1, 1)
        right = jnp.where((strip & (wx - 1)) == wx - 1, corner, pltpu.roll(ly, LANES - 1, 1))
        side_hz = ylo[4:5] - courant * ((right - ly) - (first[0:1] - lx))
        both = jnp.concatenate([side_hx, side_hz, jnp.zeros((6, LANES), jnp.float32)], axis=0)
        both = (inside_y * both).T
        bx, by, bz = (layer_of(zlow, i) for i in range(3))
        under_hx = layer_of(zlow, 3) - courant * (
            (next_y(bz, above[0:wx, 6:7]) - bz) - (ey[:wx] - by)
        )
        right = jnp.concatenate([bz[1:], extra_of(xhigh, side_of(zlow, 2), 1)], axis=0)
        under_hy = layer_of(zlow, 4) - courant * ((ex[:wx] - bx) - (right - bz))
        under_hx = inside_z * under_hx
        under_hy = inside_z * under_hy
        low_hy = inside_x * low_hy
        low_hz = inside_x * low_hz
        curl = (
            (hz - last_y(hz, both[:, 1:2])) - (hy - last_z(hy, under_hy)),
            (hx - last_z(hx, under_hx)) - (hz - last_x(hz, low_hz)),
            (hy - last_x(hy, low_hy)) - (hx - last_y(hx, both[:, 0:1])),
        )
        coef = coef_ref[...].reshape(size, wy)
        shape = (depth, wx, wy)
        tail = size - wx
        for i, magnetic in enumerate((hx, hy, hz)):
            value = flat(base_e, i) + coef * curl[i]
            h_out[i] = magnetic.reshape(shape)
            e_out[i] = value.reshape(shape)
            e_top[i] = value[tail:]
            h_top[i] = magnetic[tail:]
        coef_top[...] = coef[tail:]

    return body


def inject_kernel(depth, wx, wy, sy, sz, per, zcut):
    def body(*refs):
        blocks = refs[: 1 << zcut]
        e_top, h_top, coef_top, e_in, h_in, e_out, h_out, e_new, h_new, sems = refs[1 << zcut :]
        ix, iy, iz = (lax.axis_index(name) for name in ("gx", "gy", "gz"))

        @pl.when(iz == sz - 1)
        def _():
            inside_x, inside_y = ((index > 0).astype(jnp.float32) for index in (ix, iy))
            lane = lax.broadcasted_iota(jnp.int32, (wx, wy), 1)
            line = lax.broadcasted_iota(jnp.int32, (wx, wy), 0)
            flip = (
                lax.broadcasted_iota(jnp.int32, (wy, wy), 0)
                + lax.broadcasted_iota(jnp.int32, (wy, wy), 1)
                == wy - 1
            ).astype(jnp.float32)
            flipped = iy < sy // 2

            def straight(value):
                turned = jnp.dot(
                    value, flip, precision=lax.Precision.HIGHEST, preferred_element_type=jnp.float32
                )
                return jnp.where(flipped, turned, value)

            tiles = [straight(ref[...]) for ref in blocks]

            def channel(c):
                start = (c % per) * wx
                return tiles[c // per][start : start + wx]

            electric_x, electric_y, magnetic_x, magnetic_y = (channel(c) for c in range(4))
            before = inside_x * tiles[3 // per][per * wx : per * wx + 1]
            beside = inside_y * blocks[2 // per][per * wx : per * wx + 8].T[0:wx, 1:2]
            last_x = jnp.where(line == 0, before, pltpu.roll(magnetic_y, 1, 0))
            last_y = jnp.where(lane == 0, beside, pltpu.roll(magnetic_x, 1, 1))
            coef = coef_top[...]
            h_new[0] = h_top[0] - courant * magnetic_x
            h_new[1] = h_top[1] - courant * magnetic_y
            e_new[0] = e_top[0] + coef * (courant * magnetic_y - electric_x)
            e_new[1] = e_top[1] - coef * (courant * magnetic_x + electric_y)
            e_new[2] = e_top[2] + coef * courant * (
                (magnetic_x - last_y) - (magnetic_y - last_x)
            )
            copies = [
                pltpu.make_async_copy(e_new, e_out.at[:, depth - 1], sems.at[0]),
                pltpu.make_async_copy(h_new, h_out.at[0:2, depth - 1], sems.at[1]),
            ]
            for copy in copies:
                copy.start()
            for copy in copies:
                copy.wait()

    return body


def in_hbm(*arrays):
    return [pltpu.with_memory_space_constraint(array, pltpu.HBM) for array in arrays]


def in_vmem(*arrays):
    return [pltpu.with_memory_space_constraint(array, pltpu.VMEM) for array in arrays]


def local(
    e_field, h_field, pole_current, material, pole_table, cotangent, cosines, wavenumber, time_phase
):
    depth, wx, wy = material.shape
    sizes = sx, sy, sz = tuple(lax.axis_size(name) for name in ("gx", "gy", "gz"))
    ix, iy, iz = (lax.axis_index(name) for name in ("gx", "gy", "gz"))
    freqs, _, count = cotangent.shape
    scale = 1.0 / math.sqrt(freqs * count * sx * sy * sz)
    assert wy == LANES and depth * wx == LANES and sx > 1 and sy > 1 and sz > 1
    pad = -count % LANES
    if pad:
        cotangent = jnp.pad(cotangent, ((0, 0), (0, 0), (0, pad)))
        cosines = jnp.pad(cosines, ((0, 0), (0, pad)))
    f32 = jnp.float32
    smem = pl.BlockSpec(memory_space=pltpu.SMEM)
    vmem = pl.BlockSpec(memory_space=pltpu.VMEM)
    hbm = pl.BlockSpec(memory_space=pltpu.HBM)
    small = pltpu.CompilerParams(vmem_limit_bytes=8 << 20)
    xslots = sx // 2
    zslots = min(sz, 4)
    per = 4 // zslots
    xbits, ybits, zbits = bits_of(sx), bits_of(sy), bits_of(sz)
    zcut = bits_of(zslots)

    assert 8 % depth == 0
    mine, waves, e_near, h_near, *layers = pl.pallas_call(
        pack_kernel(freqs, depth, wx, zbits),
        out_shape=[
            pltpu.VMEM((freqs + 1 + 6 * depth // 8, 8, LANES), f32),
            pltpu.VMEM((2, freqs, LANES), f32),
            pltpu.VMEM(e_field.shape, f32),
            pltpu.VMEM(h_field.shape, f32),
        ]
        + [pltpu.VMEM((6, wx, wy), f32)] * zbits,
        in_specs=[hbm] * 6,
        out_specs=[vmem] * (4 + zbits),
        scratch_shapes=[
            pltpu.VMEM((2, LANES), f32),
            pltpu.SMEM((freqs,), f32),
            pltpu.SMEM((freqs,), f32),
            pltpu.SemaphoreType.DMA((6,)),
        ],
        compiler_params=small,
        name="pack",
    )(*in_hbm(e_field, h_field, cotangent, cosines, wavenumber, time_phase))
    e_near, h_near = in_vmem(e_near, h_near)
    theirs = exchange(mine, "gx", 1)
    side = theirs[freqs + 1 :].reshape(6, depth, LANES)
    zs = []
    for k in range(zbits):
        at = (1 - ((iz >> k) & 1)) * (depth - 1)
        row = lax.dynamic_slice_in_dim(side, at, 1, axis=1)
        zs.append(exchange(jnp.concatenate([layers[k], row], axis=1), "gz", (2 << k) - 1))

    half = sy * wy // 2
    xlevels = max(3, (wx - 1).bit_length())
    ylevels = max(3, (half - 1).bit_length()) + 1
    width = count + pad
    block = per * wx + 8
    part_shape = pltpu.VMEM((zslots // 2, sy, xslots, block, wy), f32)
    keep, send = pl.pallas_call(
        source_kernel(freqs, wx, half, sizes, zslots, xslots, scale, 2),
        out_shape=(part_shape, part_shape),
        in_specs=[vmem] * 3,
        out_specs=(vmem, vmem),
        scratch_shapes=[
            pltpu.VMEM((2, xslots, 2, freqs, width), f32),
            pltpu.VMEM((2, xlevels, 2, freqs, width), f32),
            pltpu.VMEM((2, ylevels, 2, freqs, width), f32),
            pltpu.VMEM((4 * xslots * wx + 8, half), f32),
            pltpu.VMEM((4 * xslots * wx + 8, half), f32),
        ],
        compiler_params=pltpu.CompilerParams(vmem_limit_bytes=24 << 20),
        name="source",
    )(*in_vmem(waves, mine, theirs))

    strip = pltpu.VMEM((8, LANES), f32)
    first, last = pl.pallas_call(
        column_kernel(freqs, depth, wx, wy, zbits),
        out_shape=(strip, strip),
        in_specs=[vmem] * (3 + zbits),
        out_specs=(vmem, vmem),
        compiler_params=small,
        name="columns",
    )(e_near, h_near, *in_vmem(theirs, *zs))

    whole = jax.ShapeDtypeStruct((3, depth, wx, wy), f32)
    pole_next, base_e, coef = pl.pallas_call(
        pole_kernel(depth, wx, wy),
        out_shape=(whole, pltpu.VMEM(whole.shape, f32), pltpu.VMEM((depth, wx, wy), f32)),
        in_specs=[hbm, vmem, hbm, hbm, vmem],
        out_specs=(hbm, vmem, vmem),
        scratch_shapes=[
            pltpu.SMEM(pole_table.shape, f32),
            pltpu.VMEM(whole.shape, f32),
            pltpu.VMEM((depth, wx, wy), jnp.int32),
            pltpu.VMEM(whole.shape, f32),
            pltpu.SemaphoreType.DMA((3,)),
        ],
        compiler_params=small,
        name="pole",
    )(*in_hbm(pole_table), e_near, *in_hbm(pole_current, material), *in_vmem(first))
    base_e, coef = in_vmem(base_e, coef)

    def flat(value):
        return value.reshape(-1, LANES)

    terms = [keep, exchange(send, "gz", 1)]
    for k in range(1, zbits):
        part = terms[0] + terms[1]
        mask = (2 << k) - 1
        if k < zcut:
            middle = part.shape[0] // 2
            terms = [part[:middle], exchange(part[middle:], "gz", mask)]
        else:
            terms = [part, exchange(part, "gz", mask)]
    terms = [flat(term) for term in terms]
    rows = sy * xslots * block

    ys = [None] * ybits
    k = 0
    while k < ybits:
        both = k + 1 < ybits
        size = rows // 4 if both else rows // 2
        plain, laden = pltpu.VMEM((size, LANES), f32), pltpu.VMEM((size + 8, LANES), f32)
        shapes = (plain, laden, laden, plain) if both else (plain, laden)
        keep, *away = pl.pallas_call(
            merge_y_kernel(len(terms), rows, k, ybits),
            out_shape=shapes,
            in_specs=[vmem] * (len(terms) + 2),
            out_specs=(vmem,) * len(shapes),
            compiler_params=small,
            name="merge_y",
        )(*in_vmem(*terms, first, last))
        if both:
            ys[k] = exchange(away[1], "gy", (2 << k) - 1)
            other = exchange(away[2], "gy", 2 << k)
            ys[k + 1] = exchange(away[0], "gy", (4 << k) - 1)
            terms = [keep, ys[k], ys[k + 1], other]
            k += 2
        else:
            ys[k] = exchange(away[0], "gy", (2 << k) - 1)
            terms = [keep, ys[k]]
            k += 1
        rows = size
    near = in_vmem(*zs, *ys)
    xs = []
    for k in range(1, xbits):
        keep, away = pl.pallas_call(
            merge_x_kernel(len(terms), rows, depth, wx, wy, zbits, ybits, k),
            out_shape=(
                pltpu.VMEM((rows // 2, LANES), f32),
                pltpu.VMEM((rows // 2 + 6 * depth + 8, LANES), f32),
            ),
            in_specs=[vmem] * (len(terms) + 3 + zbits + ybits),
            out_specs=(vmem, vmem),
            compiler_params=small,
            name="merge_x",
        )(*in_vmem(*terms), e_near, h_near, *near, coef)
        xs.append(exchange(away, "gx", (2 << k) - 1))
        rows //= 2
        terms = [keep, xs[-1]]
    part = sum(term[:rows] for term in terms)

    layer = pltpu.VMEM((3, wx, wy), f32)
    e_next, h_next, e_top, h_top, coef_top = pl.pallas_call(
        field_kernel(freqs, depth, wx, wy, xbits, ybits, zbits),
        out_shape=(whole, whole, layer, layer, pltpu.VMEM((wx, wy), f32)),
        in_specs=[vmem] * (5 + xbits + ybits + zbits),
        out_specs=(vmem,) * 5,
        compiler_params=pltpu.CompilerParams(vmem_limit_bytes=16 << 20),
        name="fields",
    )(e_near, h_near, base_e, coef, *in_vmem(first, theirs), *near, *in_vmem(*xs))

    top = gray(sz - 1)
    blocks = [part]
    for k in reversed(range(zcut)):
        others = [exchange(value, "gz", (2 << k) - 1) for value in blocks]
        blocks = others + blocks if (top >> k) & 1 else blocks + others
    e_next, h_next = pl.pallas_call(
        inject_kernel(depth, wx, wy, sy, sz, per, zcut),
        out_shape=(whole, whole),
        in_specs=[vmem] * (len(blocks) + 3) + [hbm] * 2,
        out_specs=(hbm, hbm),
        scratch_shapes=[
            pltpu.VMEM((3, wx, wy), f32),
            pltpu.VMEM((2, wx, wy), f32),
            pltpu.SemaphoreType.DMA((2,)),
        ],
        input_output_aliases={len(blocks) + 3: 0, len(blocks) + 4: 1},
        compiler_params=small,
        name="inject",
    )(*in_vmem(*blocks, e_top, h_top, coef_top), e_next, h_next)
    return (e_next, h_next, pole_next)


def solution(mesh):
    in_specs = (
        P(None, "gz", "gx", "gy"),
        P(None, "gz", "gx", "gy"),
        P(None, "gz", "gx", "gy"),
        P("gz", "gx", "gy"),
        P(),
        P(None, None, ("gx", "gy", "gz")),
        P(None, ("gx", "gy", "gz")),
        P(),
        P(),
    )
    out_specs = (P(None, "gz", "gx", "gy"), P(None, "gz", "gx", "gy"), P(None, "gz", "gx", "gy"))
    return jax.shard_map(local, mesh=mesh, in_specs=in_specs, out_specs=out_specs, check_vma=False)
```

```python
import math

import jax
import jax.numpy as jnp
from jax import lax
from jax.experimental import pallas as pl
from jax.experimental.pallas import tpu as pltpu
from jax.sharding import PartitionSpec as P

NPOLE = 4
LANES = 128


courant = 0.5


def exchange(array, axis, mask):
    return lax.ppermute(array, axis, [(i, i ^ mask) for i in range(lax.axis_size(axis))])


def gray(index):
    return index ^ (index >> 1)


def ungray(code, bits):
    index = code
    for step in range(1, bits):
        index = index ^ (code >> step)
    return index


def bits_of(size):
    return size.bit_length() - 1


def cmul(a, b):
    return (a[0] * b[0] - a[1] * b[1], a[0] * b[1] + a[1] * b[0])


def small_turn(angle):
    q = angle * angle
    c = 1.0 + q * (-1 / 2 + q * (1 / 24 + q * (-1 / 720 + q * (1 / 40320))))
    s = angle * (1.0 + q * (-1 / 6 + q * (1 / 120 + q * (-1 / 5040 + q * (1 / 362880)))))
    return c, s


def doubled(turn):
    c, s = turn
    return (c - s) * (c + s), 2.0 * (c * s)


def rotations(base, powers, rows):
    sub = lax.broadcasted_iota(jnp.int32, (8, base[0].shape[-1]), 0)
    value = tuple(jnp.broadcast_to(part, sub.shape) for part in base)
    for k in range(3):
        picked = (sub & (1 << k)) != 0
        value = cmul(value, (jnp.where(picked, powers[k][0], 1.0), jnp.where(picked, powers[k][1], 0.0)))
    blocks = [value]
    k = 3
    while len(blocks) * 8 < rows:
        blocks = blocks + [cmul(block, powers[k]) for block in blocks]
        k += 1
    return tuple(jnp.concatenate([block[i] for block in blocks], axis=0)[:rows] for i in (0, 1))


def split(value):
    high = value.astype(jnp.bfloat16)
    return high, (value - high.astype(jnp.float32)).astype(jnp.bfloat16)


def dot_nt(a, b):
    return lax.dot_general(a, b, (((1,), (1,)), ((), ())), preferred_element_type=jnp.float32)


def source_kernel(freqs, depth, wx, half, sizes, zslots, xslots, scale, zbits, closing):
    sx, sy, sz = sizes
    xbits = max(3, (wx - 1).bit_length())
    ybits = max(3, (half - 1).bit_length())
    per = 4 // zslots
    main = 4 * xslots * wx

    def body(*refs):
        waves, packed = refs[:2]
        if closing:
            old_even, old_odd = refs[2:4]
            keep, send, xbase, xpow, ypow, acc_even, acc_odd = refs[4 + zbits :]
        else:
            acc_even, acc_odd, xbase, xpow, ypow = refs[2:]
        ix, iy, iz = (lax.axis_index(name) for name in ("gx", "gy", "gz"))
        xbit, ybit, zbit = bits_of(sx), bits_of(sy), bits_of(zslots)
        starts = []
        for slot in range(xslots):
            code = gray(ix)
            for k in range(1, xbit):
                code = code ^ (((slot >> (xbit - 1 - k)) & 1) << k)
            starts.append((ungray(code, xbit) * wx).astype(jnp.float32))
        zcode = 0
        for k in range(zbit):
            zcode = zcode * 2 + ((gray(iz) >> k) & 1)
        ycode = gray(iy)
        center = (2 * half - 1) / 2.0
        wave, phase = waves[0], waves[1]
        along_x = wave * packed[freqs, 0:1, :]
        along_y = wave * packed[freqs, 1:2, :]
        origin = along_y * center - phase
        for xr in range(xslots):
            angle = along_x * starts[xr] + origin
            xbase[xr, 0] = jnp.cos(angle)
            xbase[xr, 1] = jnp.sin(angle)
        turn = doubled(small_turn(0.5 * along_x))
        for k in range(xbits):
            xpow[k, 0], xpow[k, 1] = turn
            turn = doubled(turn)
        turn = small_turn(0.5 * along_y)
        for k in range(ybits + 1):
            ypow[k, 0], ypow[k, 1] = turn
            turn = doubled(turn)
        if closing:
            acc_even[...] = old_even[...]
            acc_odd[...] = old_odd[...]
        else:
            acc_even[...] = jnp.zeros_like(acc_even)
            acc_odd[...] = jnp.zeros_like(acc_odd)

        def pair(step, carry):
            firsts, seconds, coses, sines = [], [], [], []
            for n in range(2):
                f = 2 * step + n

                def row(ref, *where):
                    return tuple(ref[(*where, i, pl.ds(f, 1), slice(None))] for i in (0, 1))

                powers = [row(ypow, k) for k in range(ybits + 1)]
                cy, sy_ = rotations(powers[0], powers[1:], half)
                coses.append(cy)
                sines.append(sy_)
                powers = [row(xpow, k) for k in range(xbits)]
                bases = [row(xbase, xr) for xr in range(xslots)]
                turns = [rotations(base, powers, wx) for base in bases]
                first, second = [], []
                for zr in range(zslots):
                    for xr in range(xslots):
                        cx, sx_ = turns[xr]
                        for c2 in range(per):
                            at = 2 * ((zcode ^ zr) * per + c2)
                            p = packed[f, pl.ds(at, 1), :]
                            q = packed[f, pl.ds(at + 1, 1), :]
                            first.append(p * cx - q * sx_)
                            second.append(p * sx_ + q * cx)
                back = (powers[0][0], -powers[0][1])
                p = packed[f, 6:7, :]
                q = packed[f, 7:8, :]
                line = lax.broadcasted_iota(jnp.int32, (8, p.shape[-1]), 0)
                one_first = jnp.zeros(line.shape, jnp.float32)
                one_second = one_first
                for xr in range(xslots):
                    cx, sx_ = cmul(bases[xr], back)
                    one_first = jnp.where(line == xr, p * cx - q * sx_, one_first)
                    one_second = jnp.where(line == xr, p * sx_ + q * cx, one_second)
                firsts.append(jnp.concatenate(first + [one_first], axis=0))
                seconds.append(jnp.concatenate(second + [one_second], axis=0))

            def product(lefts, rights):
                lh, ll = split(jnp.concatenate(lefts, axis=1))
                rh, rl = split(jnp.concatenate(rights, axis=1))
                return dot_nt(lh, rh) + dot_nt(lh, rl) + dot_nt(ll, rh)

            acc_even[...] += product(firsts, coses)
            acc_odd[...] += product(seconds, sines)
            return carry

        lax.fori_loop(0, freqs // 2, pair, 0)
        if not closing:
            return

        def slot(tile):
            code = gray(tile) ^ ycode
            place = 0
            for k in range(ybit):
                place = place * 2 + ((code >> k) & 1)
            return place

        def place(zr):
            return (keep, zr) if zr < zslots // 2 else (send, zr - zslots // 2)

        extra = per * wx
        for zr in range(zslots):
            ref, z = place(zr)
            for y in range(sy):
                for xr in range(xslots):
                    ref[z, y, xr, extra : extra + 8] = jnp.zeros((8, LANES), jnp.float32)
        at_z = (1 - (iz & 1)) * (depth - 1)
        for i in range(6):
            row = i * depth
            send[0, 0, 0, extra + 2 + i : extra + 3 + i] = packed[
                freqs + 1 + row // 8, pl.ds(row % 8 + at_z, 1), :
            ]
        turned = 2 // per
        spare = 2 % per
        for j in range(sy // 2):
            lanes = slice(j * LANES, (j + 1) * LANES)
            up = slot(sy // 2 + j)
            down = slot(sy // 2 - 1 - j)
            at = 0
            for zr in range(zslots):
                ref, z = place(zr)
                for xr in range(xslots):
                    for c2 in range(per):
                        rows = slice(at * wx, (at + 1) * wx)
                        even = acc_even[rows, lanes] * scale
                        odd = acc_odd[rows, lanes] * scale
                        ref[z, up, xr, c2 * wx : (c2 + 1) * wx] = even - odd
                        ref[z, down, xr, c2 * wx : (c2 + 1) * wx] = even + odd
                        at += 1
            for xr in range(xslots):
                even = acc_even[main + xr : main + xr + 1, lanes] * scale
                odd = acc_odd[main + xr : main + xr + 1, lanes] * scale
                for zr in range(zslots):
                    ref, z = place(zr)
                    ref[z, up, xr, extra : extra + 1] = even - odd
                    ref[z, down, xr, extra : extra + 1] = even + odd
                start = (((zcode ^ turned) * xslots + xr) * per + spare) * wx
                rows = pl.ds(pl.multiple_of(start, wx), wx)
                even = (acc_even[rows, lanes] * scale).T
                odd = (acc_odd[rows, lanes] * scale).T
                lower = slot(sy // 2 - j)
                for zr in range(zslots):
                    ref, z = place(zr)
                    ref[z, lower, xr, extra + 1 : extra + 2, 0:wx] = even[0:1] + odd[0:1]
                if j < sy // 2 - 1:
                    upper = slot(sy // 2 + j + 1)
                    for zr in range(zslots):
                        ref, z = place(zr)
                        ref[z, upper, xr, extra + 1 : extra + 2, 0:wx] = even[LANES - 1 :] - odd[LANES - 1 :]

    return body


def near_flags(index, bits):
    low, high = [], []
    for k in range(bits):
        upper = (index >> k) & 1
        rest = index & ((1 << k) - 1)
        low.append(((upper == 1) & (rest == 0)).astype(jnp.float32))
        high.append(((upper == 0) & (rest == (1 << k) - 1)).astype(jnp.float32))
    return low, high


def weighted(flags, values):
    total = flags[0] * values[0]
    for flag, value in zip(flags[1:], values[1:]):
        total = total + flag * value
    return total


def pack_kernel(freqs, depth, wx, zbits):
    def body(*refs):
        e_in, h_in, cotangent, cosines, wavenumber, time_phase = refs[:6]
        message, waves, e, h = refs[6:10]
        layers = refs[10 : 10 + zbits]
        cos_near, wave_near, phase_near, sems = refs[10 + zbits :]
        copies = [
            pltpu.make_async_copy(source, target, sems.at[i])
            for i, (source, target) in enumerate(
                (
                    (e_in, e),
                    (h_in, h),
                    (cotangent, message.at[0:freqs]),
                    (cosines, cos_near),
                    (wavenumber, wave_near),
                    (time_phase, phase_near),
                )
            )
        ]
        for copy in copies:
            copy.start()
        for copy in copies:
            copy.wait()
        message[freqs, 0:2] = cos_near[...]
        message[freqs, 2:8] = jnp.zeros((6, LANES), jnp.float32)
        which = lax.broadcasted_iota(jnp.int32, (freqs, LANES), 0)
        for i, near in enumerate((wave_near, phase_near)):
            value = jnp.zeros((freqs, LANES), jnp.float32)
            for f in range(freqs):
                value = jnp.where(which == f, near[f], value)
            waves[i] = value
        at = (1 - (lax.axis_index("gx") & 1)) * (wx - 1)
        for i in range(6):
            for z in range(depth):
                row = i * depth + z
                field = (e, h)[i // 3]
                message[freqs + 1 + row // 8, row % 8 : row % 8 + 1] = field[i % 3, z, pl.ds(at, 1), :]
        for k, layer in enumerate(layers):
            at_z = (1 - ((lax.axis_index("gz") >> k) & 1)) * (depth - 1)
            for i in range(3):
                layer[i] = e[i, at_z]
                layer[3 + i] = h[i, at_z]

    return body


def early_rows(message, freqs, depth, i):
    row = i * depth
    return message[freqs + 1 + row // 8, row % 8 : row % 8 + depth]


def column_kernel(freqs, depth, wx, wy, zbits):
    def body(*refs):
        e, h, message = refs[:3]
        zs = refs[3 : 3 + zbits]
        first, last = refs[3 + zbits :]
        low, high = near_flags(lax.axis_index("gz"), zbits)
        lane = lax.broadcasted_iota(jnp.int32, (1, LANES), 1)
        first[...] = jnp.zeros_like(first)
        last[...] = jnp.zeros_like(last)
        for i, field in enumerate((e[0], e[1], e[2], h[0], h[2])):
            turned = field.reshape(depth * wx, wy).T
            first[i : i + 1] = turned[0:1]
            last[i : i + 1] = turned[wy - 1 :]
        for i, layer in (
            (5, weighted(high, [z[1, 0:wx] for z in zs])),
            (6, weighted(low, [z[2, 0:wx] for z in zs])),
        ):
            turned = layer.T
            first[i : i + 1, 0:wx] = turned[0:1]
            last[i : i + 1, 0:wx] = turned[wy - 1 :]
        for ref, y in ((first, 0), (last, wy - 1)):
            corner = jnp.zeros((1, LANES), jnp.float32)
            side_x, side_y = (early_rows(message, freqs, depth, i)[:, y : y + 1] for i in (0, 1))
            for z in range(depth):
                corner = jnp.where(lane == z, side_x[z : z + 1], corner)
                corner = jnp.where(lane == z * wx + wx - 1, side_y[z : z + 1], corner)
            ref[7:8] = corner

    return body


def total_of(terms, rows):
    value = terms[0][rows]
    for term in terms[1:]:
        value = value + term[rows]
    return value


def merge_y_kernel(count, rows, k, ybits):
    def body(*refs):
        terms, (first, last), outs = refs[:count], refs[count : count + 2], refs[count + 2 :]
        iy = lax.axis_index("gy")
        size = rows // len(outs)
        swaps = (None, k) if len(outs) == 2 else (None, k + 1, k, None)
        for i, (out, swap) in enumerate(zip(outs, swaps)):
            out[0:size] = total_of(terms, slice(i * size, (i + 1) * size))
            if swap is not None:
                upper = ((iy >> swap) & 1).astype(jnp.float32)
                out[size : size + 8] = upper * first[...] + (1.0 - upper) * last[...]

    return body


def halo_at(ref):
    rows = ref.shape[0]
    return ref[rows - 8 : rows]


def merge_x_kernel(count, rows, depth, wx, wy, zbits, ybits, k):
    def body(*refs):
        terms = refs[:count]
        e, h = refs[count : count + 2]
        zs = refs[count + 2 : count + 2 + zbits]
        ys = refs[count + 2 + zbits : count + 2 + zbits + ybits]
        keep, out = refs[count + 3 + zbits + ybits :]
        size = rows // 2
        keep[...] = total_of(terms, slice(0, size))
        out[0:size] = total_of(terms, slice(size, rows))
        zlow, zhigh = near_flags(lax.axis_index("gz"), zbits)
        ylow, yhigh = near_flags(lax.axis_index("gy"), ybits)
        at = (1 - ((lax.axis_index("gx") >> k) & 1)) * (wx - 1)
        for i in range(3):
            for z in range(depth):
                row = size + i * depth + z
                out[row : row + 1] = e[i, z, pl.ds(at, 1), :]
                row = size + (3 + i) * depth + z
                out[row : row + 1] = h[i, z, pl.ds(at, 1), :]
        base = size + 6 * depth
        halos = [halo_at(y) for y in ys]
        out[base : base + 1] = weighted(zhigh, [z[0, pl.ds(at, 1), :] for z in zs])
        out[base + 1 : base + 2] = weighted(zlow, [z[2, pl.ds(at, 1), :] for z in zs])
        out[base + 2 : base + 3] = weighted(yhigh, [y[0:1] for y in halos])
        out[base + 3 : base + 4] = weighted(ylow, [y[1:2] for y in halos])
        out[base + 4 : base + 8] = jnp.zeros((4, LANES), jnp.float32)

    return body


def pole_kernel(depth, wx, wy):
    def body(table_in, e, pole_in, material_in, after, pole_out, base, coef_out, *scratch):
        table, pole, material, new_pole, sems = scratch
        copies = [
            pltpu.make_async_copy(source, target, sems.at[i])
            for i, (source, target) in enumerate(
                ((table_in, table), (material_in, material), (pole_in, pole))
            )
        ]
        for copy in copies:
            copy.start()
        for copy in copies:
            copy.wait()
        kind = material[...]

        def chosen(i):
            value = jnp.full(kind.shape, table[i, NPOLE - 1], jnp.float32)
            for m in range(NPOLE - 1):
                value = jnp.where(kind == m, table[i, m], value)
            return value

        decay, drive, coef = (chosen(i) for i in range(3))
        coef_out[...] = coef
        for i in range(3):
            old = pole[i]
            electric = e[i]
            new = decay * old + drive * electric
            new_pole[i] = new
            base[i] = electric - coef * (0.5 * (new + old))
        copy = pltpu.make_async_copy(new_pole, pole_out, sems.at[0])
        copy.start()
        copy.wait()

    return body


def field_kernel(freqs, depth, wx, wy, xbits, ybits, zbits, side_row):
    def body(*refs):
        e, h, base_e, coef_ref, first, message = refs[:6]
        zs = refs[6 : 6 + zbits]
        ys = refs[6 + zbits : 6 + zbits + ybits]
        xs = [x[x.shape[0] - 6 * depth - 8 :] for x in refs[6 + zbits + ybits : 5 + zbits + ybits + xbits]]
        sides = refs[5 + zbits + ybits + xbits : 5 + 2 * zbits + ybits + xbits]
        e_out, h_out, e_top, h_top, coef_top = refs[5 + 2 * zbits + ybits + xbits :]
        ix, iy, iz = (lax.axis_index(name) for name in ("gx", "gy", "gz"))
        xlow, xhigh = near_flags(ix, xbits)
        ylow, yhigh = near_flags(iy, ybits)
        zlow, zhigh = near_flags(iz, zbits)
        size = depth * wx
        base = 6 * depth
        lane = lax.broadcasted_iota(jnp.int32, (size, wy), 1)
        line = lax.broadcasted_iota(jnp.int32, (size, wy), 0) & (wx - 1)
        inside_x, inside_y, inside_z = (
            (index > 0).astype(jnp.float32) for index in (ix, iy, iz)
        )

        def flat(ref, i):
            return ref[i].reshape(size, wy)

        ex, ey, ez = (flat(e, i) for i in range(3))
        oldx, oldy, oldz = (flat(h, i) for i in range(3))

        def spread(rows):
            return jnp.broadcast_to(rows[:, None, :], (depth, wx, wy)).reshape(size, wy)

        def next_y(value, column):
            rows = value.shape[0]
            return jnp.where(lane[:rows] == wy - 1, column, pltpu.roll(value, wy - 1, 1))

        def next_x(value, rows):
            return jnp.where(line == wx - 1, spread(rows), pltpu.roll(value, size - 1, 0))

        def next_z(value, layer):
            return jnp.concatenate([value[wx:], layer], axis=0)

        def last_y(value, column):
            return jnp.where(lane == 0, column, pltpu.roll(value, 1, 1))

        def last_x(value, rows):
            return jnp.where(line == 0, spread(rows), pltpu.roll(value, 1, 0))

        def last_z(value, layer):
            return jnp.concatenate([layer, value[:-wx]], axis=0)

        ylo = weighted(ylow, [halo_at(y) for y in ys])
        yhi = weighted(yhigh, [halo_at(y) for y in ys])
        above = yhi.T

        def rows_of(flags, i):
            at = slice(i * depth, (i + 1) * depth)
            return weighted(flags, [early_rows(message, freqs, depth, i)] + [x[at] for x in xs])

        def extra_of(flags, early, i):
            return weighted(flags, [early] + [x[base + i : base + i + 1] for x in xs])

        def layer_of(flags, i):
            return weighted(flags, [z[i, 0:wx] for z in zs])

        def side_of(flags, i):
            at = side_row + i
            return weighted(flags, [side[at : at + 1] for side in sides])

        up_x, up_y = layer_of(zhigh, 0), layer_of(zhigh, 1)
        hx = oldx - courant * ((next_y(ez, above[:, 2:3]) - ez) - (next_z(ey, up_y) - ey))
        hy = oldy - courant * (
            (next_z(ex, up_x) - ex) - (next_x(ez, rows_of(xhigh, 2)) - ez)
        )
        hz = oldz - courant * (
            (next_x(ey, rows_of(xhigh, 1)) - ey) - (next_y(ex, above[:, 0:1]) - ex)
        )
        mx, my, mz = (rows_of(xlow, i) for i in range(3))
        up = jnp.concatenate([mx[1:], extra_of(xlow, side_of(zhigh, 0), 0)], axis=0)
        low_hy = rows_of(xlow, 4) - courant * ((up - mx) - (e[2, :, 0, :] - mz))
        corner = xlow[0] * above[0:depth, 7:8]
        for flag, x in zip(xlow[1:], xs):
            tail = x[base : base + 8].T
            picks = [tail[z * wx + wx - 1 : (z + 1) * wx, 2:3] for z in range(depth)]
            corner = corner + flag * jnp.concatenate(picks, axis=0)
        low_hz = rows_of(xlow, 5) - courant * (
            (e[1, :, 0, :] - my) - (next_y(mx, corner) - mx)
        )
        strip = lax.broadcasted_iota(jnp.int32, (1, LANES), 1)
        lx, ly, lz = ylo[0:1], ylo[1:2], ylo[2:3]
        up = jnp.where(
            strip >= size - wx, pltpu.roll(ylo[5:6], size - wx, 1), pltpu.roll(ly, LANES - wx, 1)
        )
        side_hx = ylo[3:4] - courant * ((first[2:3] - lz) - (up - ly))
        corner = xhigh[0] * ylo[7:8]
        for flag, x in zip(xhigh[1:], xs):
            corner = corner + flag * pltpu.roll(x[base + 3 : base + 4], wx - 1, 1)
        right = jnp.where((strip & (wx - 1)) == wx - 1, corner, pltpu.roll(ly, LANES - 1, 1))
        side_hz = ylo[4:5] - courant * ((right - ly) - (first[0:1] - lx))
        both = jnp.concatenate([side_hx, side_hz, jnp.zeros((6, LANES), jnp.float32)], axis=0)
        both = (inside_y * both).T
        bx, by, bz = (layer_of(zlow, i) for i in range(3))
        under_hx = layer_of(zlow, 3) - courant * (
            (next_y(bz, above[0:wx, 6:7]) - bz) - (ey[:wx] - by)
        )
        right = jnp.concatenate([bz[1:], extra_of(xhigh, side_of(zlow, 2), 1)], axis=0)
        under_hy = layer_of(zlow, 4) - courant * ((ex[:wx] - bx) - (right - bz))
        under_hx = inside_z * under_hx
        under_hy = inside_z * under_hy
        low_hy = inside_x * low_hy
        low_hz = inside_x * low_hz
        curl = (
            (hz - last_y(hz, both[:, 1:2])) - (hy - last_z(hy, under_hy)),
            (hx - last_z(hx, under_hx)) - (hz - last_x(hz, low_hz)),
            (hy - last_x(hy, low_hy)) - (hx - last_y(hx, both[:, 0:1])),
        )
        coef = coef_ref[...].reshape(size, wy)
        shape = (depth, wx, wy)
        tail = size - wx
        for i, magnetic in enumerate((hx, hy, hz)):
            value = flat(base_e, i) + coef * curl[i]
            h_out[i] = magnetic.reshape(shape)
            e_out[i] = value.reshape(shape)
            e_top[i] = value[tail:]
            h_top[i] = magnetic[tail:]
        coef_top[...] = coef[tail:]

    return body


def inject_kernel(depth, wx, wy, sy, sz, per, zcut):
    def body(*refs):
        blocks = refs[: 1 << zcut]
        e_top, h_top, coef_top, e_in, h_in, e_out, h_out, e_new, h_new, sems = refs[1 << zcut :]
        ix, iy, iz = (lax.axis_index(name) for name in ("gx", "gy", "gz"))

        @pl.when(iz == sz - 1)
        def _():
            inside_x, inside_y = ((index > 0).astype(jnp.float32) for index in (ix, iy))
            lane = lax.broadcasted_iota(jnp.int32, (wx, wy), 1)
            line = lax.broadcasted_iota(jnp.int32, (wx, wy), 0)
            flip = (
                lax.broadcasted_iota(jnp.int32, (wy, wy), 0)
                + lax.broadcasted_iota(jnp.int32, (wy, wy), 1)
                == wy - 1
            ).astype(jnp.float32)
            flipped = iy < sy // 2

            def straight(value):
                turned = jnp.dot(
                    value, flip, precision=lax.Precision.HIGHEST, preferred_element_type=jnp.float32
                )
                return jnp.where(flipped, turned, value)

            tiles = [straight(ref[...]) for ref in blocks]

            def channel(c):
                start = (c % per) * wx
                return tiles[c // per][start : start + wx]

            electric_x, electric_y, magnetic_x, magnetic_y = (channel(c) for c in range(4))
            before = inside_x * tiles[3 // per][per * wx : per * wx + 1]
            beside = inside_y * blocks[2 // per][per * wx : per * wx + 8].T[0:wx, 1:2]
            last_x = jnp.where(line == 0, before, pltpu.roll(magnetic_y, 1, 0))
            last_y = jnp.where(lane == 0, beside, pltpu.roll(magnetic_x, 1, 1))
            coef = coef_top[...]
            h_new[0] = h_top[0] - courant * magnetic_x
            h_new[1] = h_top[1] - courant * magnetic_y
            h_copy = pltpu.make_async_copy(h_new, h_out.at[0:2, depth - 1], sems.at[1])
            h_copy.start()
            e_new[0] = e_top[0] + coef * (courant * magnetic_y - electric_x)
            e_new[1] = e_top[1] - coef * (courant * magnetic_x + electric_y)
            e_new[2] = e_top[2] + coef * courant * (
                (magnetic_x - last_y) - (magnetic_y - last_x)
            )
            e_copy = pltpu.make_async_copy(e_new, e_out.at[:, depth - 1], sems.at[0])
            e_copy.start()
            h_copy.wait()
            e_copy.wait()

    return body


def in_hbm(*arrays):
    return [pltpu.with_memory_space_constraint(array, pltpu.HBM) for array in arrays]


def in_vmem(*arrays):
    return [pltpu.with_memory_space_constraint(array, pltpu.VMEM) for array in arrays]


def local(
    e_field, h_field, pole_current, material, pole_table, cotangent, cosines, wavenumber, time_phase
):
    depth, wx, wy = material.shape
    sizes = sx, sy, sz = tuple(lax.axis_size(name) for name in ("gx", "gy", "gz"))
    ix, iy, iz = (lax.axis_index(name) for name in ("gx", "gy", "gz"))
    freqs, _, count = cotangent.shape
    scale = 1.0 / math.sqrt(freqs * count * sx * sy * sz)
    assert wy == LANES and depth * wx == LANES and sx > 1 and sy > 1 and sz > 1
    pad = -count % LANES
    if pad:
        cotangent = jnp.pad(cotangent, ((0, 0), (0, 0), (0, pad)))
        cosines = jnp.pad(cosines, ((0, 0), (0, pad)))
    f32 = jnp.float32
    smem = pl.BlockSpec(memory_space=pltpu.SMEM)
    vmem = pl.BlockSpec(memory_space=pltpu.VMEM)
    hbm = pl.BlockSpec(memory_space=pltpu.HBM)
    small = pltpu.CompilerParams(vmem_limit_bytes=8 << 20)
    xslots = sx // 2
    zslots = min(sz, 4)
    per = 4 // zslots
    xbits, ybits, zbits = bits_of(sx), bits_of(sy), bits_of(sz)
    zcut = bits_of(zslots)

    assert 8 % depth == 0
    mine, waves, e_near, h_near, *layers = pl.pallas_call(
        pack_kernel(freqs, depth, wx, zbits),
        out_shape=[
            pltpu.VMEM((freqs + 1 + 6 * depth // 8, 8, LANES), f32),
            pltpu.VMEM((2, freqs, LANES), f32),
            pltpu.VMEM(e_field.shape, f32),
            pltpu.VMEM(h_field.shape, f32),
        ]
        + [pltpu.VMEM((6, wx, wy), f32)] * zbits,
        in_specs=[hbm] * 6,
        out_specs=[vmem] * (4 + zbits),
        scratch_shapes=[
            pltpu.VMEM((2, LANES), f32),
            pltpu.SMEM((freqs,), f32),
            pltpu.SMEM((freqs,), f32),
            pltpu.SemaphoreType.DMA((6,)),
        ],
        compiler_params=small,
        name="pack",
    )(*in_hbm(e_field, h_field, cotangent, cosines, wavenumber, time_phase))
    e_near, h_near = in_vmem(e_near, h_near)
    theirs = exchange(mine, "gx", 1)
    zs = [exchange(layers[k], "gz", (2 << k) - 1) for k in range(zbits)]
    zs = in_vmem(*zs)

    half = sy * wy // 2
    xlevels = max(3, (wx - 1).bit_length())
    ylevels = max(3, (half - 1).bit_length()) + 1
    width = count + pad
    block = per * wx + 8
    part_shape = pltpu.VMEM((zslots // 2, sy, xslots, block, wy), f32)
    assert freqs % 2 == 0
    sums = pltpu.VMEM((4 * xslots * wx + 8, half), f32)
    tables = [
        pltpu.VMEM((xslots, 2, freqs, width), f32),
        pltpu.VMEM((xlevels, 2, freqs, width), f32),
        pltpu.VMEM((ylevels, 2, freqs, width), f32),
    ]
    medium = pltpu.CompilerParams(vmem_limit_bytes=24 << 20)
    waves, mine = in_vmem(waves, mine)
    own = pl.pallas_call(
        source_kernel(freqs, depth, wx, half, sizes, zslots, xslots, scale, zbits, False),
        out_shape=(sums, sums),
        in_specs=[vmem] * 2,
        out_specs=(vmem, vmem),
        scratch_shapes=tables,
        compiler_params=medium,
        name="source_own",
    )(waves, mine)
    with jax.named_scope("source_all"):
        keep, send = pl.pallas_call(
            source_kernel(freqs, depth, wx, half, sizes, zslots, xslots, scale, zbits, True),
            out_shape=(part_shape, part_shape),
            in_specs=[vmem] * (4 + zbits),
            out_specs=(vmem, vmem),
            scratch_shapes=tables + [sums, sums],
            compiler_params=medium,
            name="source_both",
        )(waves, *in_vmem(theirs, *own), *zs)

    strip = pltpu.VMEM((8, LANES), f32)
    first, last = pl.pallas_call(
        column_kernel(freqs, depth, wx, wy, zbits),
        out_shape=(strip, strip),
        in_specs=[vmem] * (3 + zbits),
        out_specs=(vmem, vmem),
        compiler_params=small,
        name="columns",
    )(e_near, h_near, *in_vmem(theirs), *zs)

    whole = jax.ShapeDtypeStruct((3, depth, wx, wy), f32)
    pole_next, base_e, coef = pl.pallas_call(
        pole_kernel(depth, wx, wy),
        out_shape=(whole, pltpu.VMEM(whole.shape, f32), pltpu.VMEM((depth, wx, wy), f32)),
        in_specs=[hbm, vmem, hbm, hbm, vmem],
        out_specs=(hbm, vmem, vmem),
        scratch_shapes=[
            pltpu.SMEM(pole_table.shape, f32),
            pltpu.VMEM(whole.shape, f32),
            pltpu.VMEM((depth, wx, wy), jnp.int32),
            pltpu.VMEM(whole.shape, f32),
            pltpu.SemaphoreType.DMA((3,)),
        ],
        compiler_params=small,
        name="pole",
    )(*in_hbm(pole_table), e_near, *in_hbm(pole_current, material), *in_vmem(first))
    base_e, coef = in_vmem(base_e, coef)

    def flat(value):
        return value.reshape(-1, LANES)

    terms = [keep, exchange(send, "gz", 1)]
    sides = [flat(terms[1])]
    for k in range(1, zbits):
        at = (1 - ((iz >> k) & 1)) * (depth - 1)
        rows = theirs[freqs + 1 :].reshape(6, depth, LANES)
        rows = lax.dynamic_index_in_dim(rows, at, 1, keepdims=False)
        sides.append(exchange(jnp.pad(rows, ((per * wx + 2, 0), (0, 0))), "gz", (2 << k) - 1))
    for k in range(1, zbits):
        part = terms[0] + terms[1]
        mask = (2 << k) - 1
        if k < zcut:
            middle = part.shape[0] // 2
            terms = [part[:middle], exchange(part[middle:], "gz", mask)]
        else:
            terms = [part, exchange(part, "gz", mask)]
    terms = [flat(term) for term in terms]
    rows = sy * xslots * block

    ys = [None] * ybits
    k = 0
    while k < ybits:
        both = k + 1 < ybits
        size = rows // 4 if both else rows // 2
        plain, laden = pltpu.VMEM((size, LANES), f32), pltpu.VMEM((size + 8, LANES), f32)
        shapes = (plain, laden, laden, plain) if both else (plain, laden)
        keep, *away = pl.pallas_call(
            merge_y_kernel(len(terms), rows, k, ybits),
            out_shape=shapes,
            in_specs=[vmem] * (len(terms) + 2),
            out_specs=(vmem,) * len(shapes),
            compiler_params=small,
            name="merge_y",
        )(*in_vmem(*terms, first, last))
        if both:
            ys[k] = exchange(away[1], "gy", (2 << k) - 1)
            other = exchange(away[2], "gy", 2 << k)
            ys[k + 1] = exchange(away[0], "gy", (4 << k) - 1)
            terms = [keep, ys[k], ys[k + 1], other]
            k += 2
        else:
            ys[k] = exchange(away[0], "gy", (2 << k) - 1)
            terms = [keep, ys[k]]
            k += 1
        rows = size
    near = [*zs, *in_vmem(*ys)]
    xs = []
    for k in range(1, xbits):
        keep, away = pl.pallas_call(
            merge_x_kernel(len(terms), rows, depth, wx, wy, zbits, ybits, k),
            out_shape=(
                pltpu.VMEM((rows // 2, LANES), f32),
                pltpu.VMEM((rows // 2 + 6 * depth + 8, LANES), f32),
            ),
            in_specs=[vmem] * (len(terms) + 3 + zbits + ybits),
            out_specs=(vmem, vmem),
            compiler_params=small,
            name="merge_x",
        )(*in_vmem(*terms), e_near, h_near, *near, coef)
        xs.append(exchange(away, "gx", (2 << k) - 1))
        rows //= 2
        terms = [keep, xs[-1]]
    part = sum(term[:rows] for term in terms)

    layer = pltpu.VMEM((3, wx, wy), f32)
    e_next, h_next, e_top, h_top, coef_top = pl.pallas_call(
        field_kernel(freqs, depth, wx, wy, xbits, ybits, zbits, per * wx + 2),
        out_shape=(whole, whole, layer, layer, pltpu.VMEM((wx, wy), f32)),
        in_specs=[vmem] * (5 + xbits + ybits + 2 * zbits),
        out_specs=(vmem,) * 5,
        compiler_params=pltpu.CompilerParams(vmem_limit_bytes=16 << 20),
        name="fields",
    )(e_near, h_near, base_e, coef, *in_vmem(first, theirs), *near, *in_vmem(*xs, *sides))

    top = gray(sz - 1)
    blocks = [part]
    for k in reversed(range(zcut)):
        others = [exchange(value, "gz", (2 << k) - 1) for value in blocks]
        blocks = others + blocks if (top >> k) & 1 else blocks + others
    e_next, h_next = pl.pallas_call(
        inject_kernel(depth, wx, wy, sy, sz, per, zcut),
        out_shape=(whole, whole),
        in_specs=[vmem] * (len(blocks) + 3) + [hbm] * 2,
        out_specs=(hbm, hbm),
        scratch_shapes=[
            pltpu.VMEM((3, wx, wy), f32),
            pltpu.VMEM((2, wx, wy), f32),
            pltpu.SemaphoreType.DMA((2,)),
        ],
        input_output_aliases={len(blocks) + 3: 0, len(blocks) + 4: 1},
        compiler_params=small,
        name="inject",
    )(*in_vmem(*blocks, e_top, h_top, coef_top), e_next, h_next)
    return (e_next, h_next, pole_next)


def solution(mesh):
    in_specs = (
        P(None, "gz", "gx", "gy"),
        P(None, "gz", "gx", "gy"),
        P(None, "gz", "gx", "gy"),
        P("gz", "gx", "gy"),
        P(),
        P(None, None, ("gx", "gy", "gz")),
        P(None, ("gx", "gy", "gz")),
        P(),
        P(),
    )
    out_specs = (P(None, "gz", "gx", "gy"), P(None, "gz", "gx", "gy"), P(None, "gz", "gx", "gy"))
    return jax.shard_map(local, mesh=mesh, in_specs=in_specs, out_specs=out_specs, check_vma=False)
```

```python
import math

import jax
import jax.numpy as jnp
from jax import lax
from jax.experimental import pallas as pl
from jax.experimental.pallas import tpu as pltpu
from jax.sharding import PartitionSpec as P

NPOLE = 4
LANES = 128


courant = 0.5


def exchange(array, axis, mask):
    return lax.ppermute(array, axis, [(i, i ^ mask) for i in range(lax.axis_size(axis))])


def gray(index):
    return index ^ (index >> 1)


def ungray(code, bits):
    index = code
    for step in range(1, bits):
        index = index ^ (code >> step)
    return index


def bits_of(size):
    return size.bit_length() - 1


def cmul(a, b):
    return (a[0] * b[0] - a[1] * b[1], a[0] * b[1] + a[1] * b[0])


def small_turn(angle):
    q = angle * angle
    c = 1.0 + q * (-1 / 2 + q * (1 / 24 + q * (-1 / 720 + q * (1 / 40320))))
    s = angle * (1.0 + q * (-1 / 6 + q * (1 / 120 + q * (-1 / 5040 + q * (1 / 362880)))))
    return c, s


def doubled(turn):
    c, s = turn
    return (c - s) * (c + s), 2.0 * (c * s)


def rotations(base, powers, rows):
    sub = lax.broadcasted_iota(jnp.int32, (8, base[0].shape[-1]), 0)
    value = tuple(jnp.broadcast_to(part, sub.shape) for part in base)
    for k in range(3):
        picked = (sub & (1 << k)) != 0
        value = cmul(value, (jnp.where(picked, powers[k][0], 1.0), jnp.where(picked, powers[k][1], 0.0)))
    blocks = [value]
    k = 3
    while len(blocks) * 8 < rows:
        blocks = blocks + [cmul(block, powers[k]) for block in blocks]
        k += 1
    return tuple(jnp.concatenate([block[i] for block in blocks], axis=0)[:rows] for i in (0, 1))


def split(value):
    high = value.astype(jnp.bfloat16)
    return high, (value - high.astype(jnp.float32)).astype(jnp.bfloat16)


def dot_nt(a, b):
    return lax.dot_general(a, b, (((1,), (1,)), ((), ())), preferred_element_type=jnp.float32)


def source_kernel(freqs, depth, wx, half, sizes, zslots, xslots, scale, zbits, closing):
    sx, sy, sz = sizes
    xbits = max(3, (wx - 1).bit_length())
    ybits = max(3, (half - 1).bit_length())
    per = 4 // zslots
    main = 4 * xslots * wx

    def body(*refs):
        waves, packed = refs[:2]
        if closing:
            old_even, old_odd = refs[2:4]
            keep, send, xbase, xpow, ypow, acc_even, acc_odd = refs[4 + zbits :]
        else:
            acc_even, acc_odd, xbase, xpow, ypow = refs[2:]
        ix, iy, iz = (lax.axis_index(name) for name in ("gx", "gy", "gz"))
        xbit, ybit, zbit = bits_of(sx), bits_of(sy), bits_of(zslots)
        starts = []
        for slot in range(xslots):
            code = gray(ix)
            for k in range(1, xbit):
                code = code ^ (((slot >> (xbit - 1 - k)) & 1) << k)
            starts.append((ungray(code, xbit) * wx).astype(jnp.float32))
        zcode = 0
        for k in range(zbit):
            zcode = zcode * 2 + ((gray(iz) >> k) & 1)
        ycode = gray(iy)
        center = (2 * half - 1) / 2.0
        wave, phase = waves[0], waves[1]
        along_x = wave * packed[freqs, 0:1, :]
        along_y = wave * packed[freqs, 1:2, :]
        origin = along_y * center - phase
        for xr in range(xslots):
            angle = along_x * starts[xr] + origin
            xbase[xr, 0] = jnp.cos(angle)
            xbase[xr, 1] = jnp.sin(angle)
        turn = doubled(small_turn(0.5 * along_x))
        for k in range(xbits):
            xpow[k, 0], xpow[k, 1] = turn
            turn = doubled(turn)
        turn = small_turn(0.5 * along_y)
        for k in range(ybits + 1):
            ypow[k, 0], ypow[k, 1] = turn
            turn = doubled(turn)
        if closing:
            acc_even[...] = old_even[...]
            acc_odd[...] = old_odd[...]
        else:
            acc_even[...] = jnp.zeros_like(acc_even)
            acc_odd[...] = jnp.zeros_like(acc_odd)

        def pair(step, carry):
            firsts, seconds, coses, sines = [], [], [], []
            for n in range(2):
                f = 2 * step + n

                def row(ref, *where):
                    return tuple(ref[(*where, i, pl.ds(f, 1), slice(None))] for i in (0, 1))

                powers = [row(ypow, k) for k in range(ybits + 1)]
                cy, sy_ = rotations(powers[0], powers[1:], half)
                coses.append(cy)
                sines.append(sy_)
                powers = [row(xpow, k) for k in range(xbits)]
                bases = [row(xbase, xr) for xr in range(xslots)]
                turns = [rotations(base, powers, wx) for base in bases]
                first, second = [], []
                for zr in range(zslots):
                    for xr in range(xslots):
                        cx, sx_ = turns[xr]
                        for c2 in range(per):
                            at = 2 * ((zcode ^ zr) * per + c2)
                            p = packed[f, pl.ds(at, 1), :]
                            q = packed[f, pl.ds(at + 1, 1), :]
                            first.append(p * cx - q * sx_)
                            second.append(p * sx_ + q * cx)
                back = (powers[0][0], -powers[0][1])
                p = packed[f, 6:7, :]
                q = packed[f, 7:8, :]
                line = lax.broadcasted_iota(jnp.int32, (16, p.shape[-1]), 0)
                one_first = jnp.zeros(line.shape, jnp.float32)
                one_second = one_first
                for xr in range(xslots):
                    cx, sx_ = cmul(bases[xr], back)
                    one_first = jnp.where(line == xr, p * cx - q * sx_, one_first)
                    one_second = jnp.where(line == xr, p * sx_ + q * cx, one_second)
                firsts.append(jnp.concatenate(first + [one_first], axis=0))
                seconds.append(jnp.concatenate(second + [one_second], axis=0))

            def product(lefts, rights):
                lh, ll = split(jnp.concatenate(lefts, axis=1))
                rh, rl = split(jnp.concatenate(rights, axis=1))
                both = dot_nt(jnp.concatenate([lh, ll], axis=0), rh)
                rows = lh.shape[0]
                return both[:rows] + dot_nt(lh, rl) + both[rows:]

            acc_even[...] += product(firsts, coses)
            acc_odd[...] += product(seconds, sines)
            return carry

        lax.fori_loop(0, freqs // 2, pair, 0, unroll=4)
        if not closing:
            return

        def slot(tile):
            code = gray(tile) ^ ycode
            place = 0
            for k in range(ybit):
                place = place * 2 + ((code >> k) & 1)
            return place

        def place(zr):
            return (keep, zr) if zr < zslots // 2 else (send, zr - zslots // 2)

        extra = per * wx
        for zr in range(zslots):
            ref, z = place(zr)
            for y in range(sy):
                for xr in range(xslots):
                    ref[z, y, xr, extra : extra + 8] = jnp.zeros((8, LANES), jnp.float32)
        at_z = (1 - (iz & 1)) * (depth - 1)
        for i in range(6):
            row = i * depth
            send[0, 0, 0, extra + 2 + i : extra + 3 + i] = packed[
                freqs + 1 + row // 8, pl.ds(row % 8 + at_z, 1), :
            ]
        turned = 2 // per
        spare = 2 % per
        for j in range(sy // 2):
            lanes = slice(j * LANES, (j + 1) * LANES)
            up = slot(sy // 2 + j)
            down = slot(sy // 2 - 1 - j)
            at = 0
            for zr in range(zslots):
                ref, z = place(zr)
                for xr in range(xslots):
                    for c2 in range(per):
                        rows = slice(at * wx, (at + 1) * wx)
                        even = acc_even[rows, lanes] * scale
                        odd = acc_odd[rows, lanes] * scale
                        ref[z, up, xr, c2 * wx : (c2 + 1) * wx] = even - odd
                        ref[z, down, xr, c2 * wx : (c2 + 1) * wx] = even + odd
                        at += 1
            for xr in range(xslots):
                even = acc_even[main + xr : main + xr + 1, lanes] * scale
                odd = acc_odd[main + xr : main + xr + 1, lanes] * scale
                for zr in range(zslots):
                    ref, z = place(zr)
                    ref[z, up, xr, extra : extra + 1] = even - odd
                    ref[z, down, xr, extra : extra + 1] = even + odd
                start = (((zcode ^ turned) * xslots + xr) * per + spare) * wx
                rows = pl.ds(pl.multiple_of(start, wx), wx)
                even = (acc_even[rows, lanes] * scale).T
                odd = (acc_odd[rows, lanes] * scale).T
                lower = slot(sy // 2 - j)
                for zr in range(zslots):
                    ref, z = place(zr)
                    ref[z, lower, xr, extra + 1 : extra + 2, 0:wx] = even[0:1] + odd[0:1]
                if j < sy // 2 - 1:
                    upper = slot(sy // 2 + j + 1)
                    for zr in range(zslots):
                        ref, z = place(zr)
                        ref[z, upper, xr, extra + 1 : extra + 2, 0:wx] = even[LANES - 1 :] - odd[LANES - 1 :]

    return body


def near_flags(index, bits):
    low, high = [], []
    for k in range(bits):
        upper = (index >> k) & 1
        rest = index & ((1 << k) - 1)
        low.append(((upper == 1) & (rest == 0)).astype(jnp.float32))
        high.append(((upper == 0) & (rest == (1 << k) - 1)).astype(jnp.float32))
    return low, high


def weighted(flags, values):
    total = flags[0] * values[0]
    for flag, value in zip(flags[1:], values[1:]):
        total = total + flag * value
    return total


def pack_kernel(freqs, depth, wx, zbits):
    def body(*refs):
        e_in, h_in, cotangent, cosines, wavenumber, time_phase = refs[:6]
        message, waves, e, h = refs[6:10]
        layers = refs[10 : 10 + zbits]
        cos_near, wave_near, phase_near, sems = refs[10 + zbits :]
        copies = [
            pltpu.make_async_copy(source, target, sems.at[i])
            for i, (source, target) in enumerate(
                (
                    (e_in, e),
                    (h_in, h),
                    (cotangent, message.at[0:freqs]),
                    (cosines, cos_near),
                    (wavenumber, wave_near),
                    (time_phase, phase_near),
                )
            )
        ]
        for copy in copies:
            copy.start()
        for copy in copies:
            copy.wait()
        message[freqs, 0:2] = cos_near[...]
        message[freqs, 2:8] = jnp.zeros((6, LANES), jnp.float32)
        which = lax.broadcasted_iota(jnp.int32, (freqs, LANES), 0)
        for i, near in enumerate((wave_near, phase_near)):
            value = jnp.zeros((freqs, LANES), jnp.float32)
            for f in range(freqs):
                value = jnp.where(which == f, near[f], value)
            waves[i] = value
        at = (1 - (lax.axis_index("gx") & 1)) * (wx - 1)
        for i in range(6):
            for z in range(depth):
                row = i * depth + z
                field = (e, h)[i // 3]
                message[freqs + 1 + row // 8, row % 8 : row % 8 + 1] = field[i % 3, z, pl.ds(at, 1), :]
        for k, layer in enumerate(layers):
            at_z = (1 - ((lax.axis_index("gz") >> k) & 1)) * (depth - 1)
            for i in range(3):
                layer[i] = e[i, at_z]
                layer[3 + i] = h[i, at_z]

    return body


def early_rows(message, freqs, depth, i):
    row = i * depth
    return message[freqs + 1 + row // 8, row % 8 : row % 8 + depth]


def column_kernel(freqs, depth, wx, wy, zbits):
    def body(*refs):
        e, h, message = refs[:3]
        zs = refs[3 : 3 + zbits]
        first, last = refs[3 + zbits :]
        low, high = near_flags(lax.axis_index("gz"), zbits)
        lane = lax.broadcasted_iota(jnp.int32, (1, LANES), 1)
        first[...] = jnp.zeros_like(first)
        last[...] = jnp.zeros_like(last)
        for i, field in enumerate((e[0], e[1], e[2], h[0], h[2])):
            turned = field.reshape(depth * wx, wy).T
            first[i : i + 1] = turned[0:1]
            last[i : i + 1] = turned[wy - 1 :]
        for i, layer in (
            (5, weighted(high, [z[1, 0:wx] for z in zs])),
            (6, weighted(low, [z[2, 0:wx] for z in zs])),
        ):
            turned = layer.T
            first[i : i + 1, 0:wx] = turned[0:1]
            last[i : i + 1, 0:wx] = turned[wy - 1 :]
        for ref, y in ((first, 0), (last, wy - 1)):
            corner = jnp.zeros((1, LANES), jnp.float32)
            side_x, side_y = (early_rows(message, freqs, depth, i)[:, y : y + 1] for i in (0, 1))
            for z in range(depth):
                corner = jnp.where(lane == z, side_x[z : z + 1], corner)
                corner = jnp.where(lane == z * wx + wx - 1, side_y[z : z + 1], corner)
            ref[7:8] = corner

    return body


def total_of(terms, rows):
    value = terms[0][rows]
    for term in terms[1:]:
        value = value + term[rows]
    return value


def merge_y_kernel(count, rows, k, ybits):
    def body(*refs):
        terms, (first, last), outs = refs[:count], refs[count : count + 2], refs[count + 2 :]
        iy = lax.axis_index("gy")
        size = rows // len(outs)
        swaps = (None, k) if len(outs) == 2 else (None, k + 1, k, None)
        for i, (out, swap) in enumerate(zip(outs, swaps)):
            out[0:size] = total_of(terms, slice(i * size, (i + 1) * size))
            if swap is not None:
                upper = ((iy >> swap) & 1).astype(jnp.float32)
                out[size : size + 8] = upper * first[...] + (1.0 - upper) * last[...]

    return body


def halo_at(ref):
    rows = ref.shape[0]
    return ref[rows - 8 : rows]


def merge_x_kernel(count, rows, depth, wx, wy, zbits, ybits, k):
    def body(*refs):
        terms = refs[:count]
        e, h = refs[count : count + 2]
        zs = refs[count + 2 : count + 2 + zbits]
        ys = refs[count + 2 + zbits : count + 2 + zbits + ybits]
        keep, out = refs[count + 3 + zbits + ybits :]
        size = rows // 2
        keep[...] = total_of(terms, slice(0, size))
        out[0:size] = total_of(terms, slice(size, rows))
        zlow, zhigh = near_flags(lax.axis_index("gz"), zbits)
        ylow, yhigh = near_flags(lax.axis_index("gy"), ybits)
        at = (1 - ((lax.axis_index("gx") >> k) & 1)) * (wx - 1)
        for i in range(3):
            for z in range(depth):
                row = size + i * depth + z
                out[row : row + 1] = e[i, z, pl.ds(at, 1), :]
                row = size + (3 + i) * depth + z
                out[row : row + 1] = h[i, z, pl.ds(at, 1), :]
        base = size + 6 * depth
        halos = [halo_at(y) for y in ys]
        out[base : base + 1] = weighted(zhigh, [z[0, pl.ds(at, 1), :] for z in zs])
        out[base + 1 : base + 2] = weighted(zlow, [z[2, pl.ds(at, 1), :] for z in zs])
        out[base + 2 : base + 3] = weighted(yhigh, [y[0:1] for y in halos])
        out[base + 3 : base + 4] = weighted(ylow, [y[1:2] for y in halos])
        out[base + 4 : base + 8] = jnp.zeros((4, LANES), jnp.float32)

    return body


def pole_kernel(depth, wx, wy):
    def body(table_in, e, pole_in, material_in, after, pole_out, base, coef_out, *scratch):
        table, pole, material, new_pole, sems = scratch
        copies = [
            pltpu.make_async_copy(source, target, sems.at[i])
            for i, (source, target) in enumerate(
                ((table_in, table), (material_in, material), (pole_in, pole))
            )
        ]
        for copy in copies:
            copy.start()
        for copy in copies:
            copy.wait()
        kind = material[...]

        def chosen(i):
            value = jnp.full(kind.shape, table[i, NPOLE - 1], jnp.float32)
            for m in range(NPOLE - 1):
                value = jnp.where(kind == m, table[i, m], value)
            return value

        decay, drive, coef = (chosen(i) for i in range(3))
        coef_out[...] = coef
        for i in range(3):
            old = pole[i]
            electric = e[i]
            new = decay * old + drive * electric
            new_pole[i] = new
            base[i] = electric - coef * (0.5 * (new + old))
        copy = pltpu.make_async_copy(new_pole, pole_out, sems.at[0])
        copy.start()
        copy.wait()

    return body


def field_kernel(freqs, depth, wx, wy, xbits, ybits, zbits, side_row):
    def body(*refs):
        e, h, base_e, coef_ref, first, message = refs[:6]
        zs = refs[6 : 6 + zbits]
        ys = refs[6 + zbits : 6 + zbits + ybits]
        xs = [x[x.shape[0] - 6 * depth - 8 :] for x in refs[6 + zbits + ybits : 5 + zbits + ybits + xbits]]
        sides = refs[5 + zbits + ybits + xbits : 5 + 2 * zbits + ybits + xbits]
        e_out, h_out, e_top, h_top, coef_top = refs[5 + 2 * zbits + ybits + xbits :]
        ix, iy, iz = (lax.axis_index(name) for name in ("gx", "gy", "gz"))
        xlow, xhigh = near_flags(ix, xbits)
        ylow, yhigh = near_flags(iy, ybits)
        zlow, zhigh = near_flags(iz, zbits)
        size = depth * wx
        base = 6 * depth
        lane = lax.broadcasted_iota(jnp.int32, (size, wy), 1)
        line = lax.broadcasted_iota(jnp.int32, (size, wy), 0) & (wx - 1)
        inside_x, inside_y, inside_z = (
            (index > 0).astype(jnp.float32) for index in (ix, iy, iz)
        )

        def flat(ref, i):
            return ref[i].reshape(size, wy)

        ex, ey, ez = (flat(e, i) for i in range(3))
        oldx, oldy, oldz = (flat(h, i) for i in range(3))

        def spread(rows):
            return jnp.broadcast_to(rows[:, None, :], (depth, wx, wy)).reshape(size, wy)

        def next_y(value, column):
            rows = value.shape[0]
            return jnp.where(lane[:rows] == wy - 1, column, pltpu.roll(value, wy - 1, 1))

        def next_x(value, rows):
            return jnp.where(line == wx - 1, spread(rows), pltpu.roll(value, size - 1, 0))

        def next_z(value, layer):
            return jnp.concatenate([value[wx:], layer], axis=0)

        def last_y(value, column):
            return jnp.where(lane == 0, column, pltpu.roll(value, 1, 1))

        def last_x(value, rows):
            return jnp.where(line == 0, spread(rows), pltpu.roll(value, 1, 0))

        def last_z(value, layer):
            return jnp.concatenate([layer, value[:-wx]], axis=0)

        ylo = weighted(ylow, [halo_at(y) for y in ys])
        yhi = weighted(yhigh, [halo_at(y) for y in ys])
        above = yhi.T

        def rows_of(flags, i):
            at = slice(i * depth, (i + 1) * depth)
            return weighted(flags, [early_rows(message, freqs, depth, i)] + [x[at] for x in xs])

        def extra_of(flags, early, i):
            return weighted(flags, [early] + [x[base + i : base + i + 1] for x in xs])

        def layer_of(flags, i):
            return weighted(flags, [z[i, 0:wx] for z in zs])

        def side_of(flags, i):
            at = side_row + i
            return weighted(flags, [side[at : at + 1] for side in sides])

        up_x, up_y = layer_of(zhigh, 0), layer_of(zhigh, 1)
        hx = oldx - courant * ((next_y(ez, above[:, 2:3]) - ez) - (next_z(ey, up_y) - ey))
        hy = oldy - courant * (
            (next_z(ex, up_x) - ex) - (next_x(ez, rows_of(xhigh, 2)) - ez)
        )
        hz = oldz - courant * (
            (next_x(ey, rows_of(xhigh, 1)) - ey) - (next_y(ex, above[:, 0:1]) - ex)
        )
        mx, my, mz = (rows_of(xlow, i) for i in range(3))
        up = jnp.concatenate([mx[1:], extra_of(xlow, side_of(zhigh, 0), 0)], axis=0)
        low_hy = rows_of(xlow, 4) - courant * ((up - mx) - (e[2, :, 0, :] - mz))
        corner = xlow[0] * above[0:depth, 7:8]
        for flag, x in zip(xlow[1:], xs):
            tail = x[base : base + 8].T
            picks = [tail[z * wx + wx - 1 : (z + 1) * wx, 2:3] for z in range(depth)]
            corner = corner + flag * jnp.concatenate(picks, axis=0)
        low_hz = rows_of(xlow, 5) - courant * (
            (e[1, :, 0, :] - my) - (next_y(mx, corner) - mx)
        )
        strip = lax.broadcasted_iota(jnp.int32, (1, LANES), 1)
        lx, ly, lz = ylo[0:1], ylo[1:2], ylo[2:3]
        up = jnp.where(
            strip >= size - wx, pltpu.roll(ylo[5:6], size - wx, 1), pltpu.roll(ly, LANES - wx, 1)
        )
        side_hx = ylo[3:4] - courant * ((first[2:3] - lz) - (up - ly))
        corner = xhigh[0] * ylo[7:8]
        for flag, x in zip(xhigh[1:], xs):
            corner = corner + flag * pltpu.roll(x[base + 3 : base + 4], wx - 1, 1)
        right = jnp.where((strip & (wx - 1)) == wx - 1, corner, pltpu.roll(ly, LANES - 1, 1))
        side_hz = ylo[4:5] - courant * ((right - ly) - (first[0:1] - lx))
        both = jnp.concatenate([side_hx, side_hz, jnp.zeros((6, LANES), jnp.float32)], axis=0)
        both = (inside_y * both).T
        bx, by, bz = (layer_of(zlow, i) for i in range(3))
        under_hx = layer_of(zlow, 3) - courant * (
            (next_y(bz, above[0:wx, 6:7]) - bz) - (ey[:wx] - by)
        )
        right = jnp.concatenate([bz[1:], extra_of(xhigh, side_of(zlow, 2), 1)], axis=0)
        under_hy = layer_of(zlow, 4) - courant * ((ex[:wx] - bx) - (right - bz))
        under_hx = inside_z * under_hx
        under_hy = inside_z * under_hy
        low_hy = inside_x * low_hy
        low_hz = inside_x * low_hz
        curl = (
            (hz - last_y(hz, both[:, 1:2])) - (hy - last_z(hy, under_hy)),
            (hx - last_z(hx, under_hx)) - (hz - last_x(hz, low_hz)),
            (hy - last_x(hy, low_hy)) - (hx - last_y(hx, both[:, 0:1])),
        )
        coef = coef_ref[...].reshape(size, wy)
        shape = (depth, wx, wy)
        tail = size - wx
        for i, magnetic in enumerate((hx, hy, hz)):
            value = flat(base_e, i) + coef * curl[i]
            h_out[i] = magnetic.reshape(shape)
            e_out[i] = value.reshape(shape)
            e_top[i] = value[tail:]
            h_top[i] = magnetic[tail:]
        coef_top[...] = coef[tail:]

    return body


def inject_kernel(depth, wx, wy, sy, sz, per, zcut):
    def body(*refs):
        blocks = refs[: 1 << zcut]
        e_top, h_top, coef_top, e_in, h_in, e_out, h_out, e_new, h_new, sems = refs[1 << zcut :]
        ix, iy, iz = (lax.axis_index(name) for name in ("gx", "gy", "gz"))

        @pl.when(iz == sz - 1)
        def _():
            inside_x, inside_y = ((index > 0).astype(jnp.float32) for index in (ix, iy))
            lane = lax.broadcasted_iota(jnp.int32, (wx, wy), 1)
            line = lax.broadcasted_iota(jnp.int32, (wx, wy), 0)
            flip = (
                lax.broadcasted_iota(jnp.int32, (wy, wy), 0)
                + lax.broadcasted_iota(jnp.int32, (wy, wy), 1)
                == wy - 1
            ).astype(jnp.float32)
            flipped = iy < sy // 2

            def straight(value):
                turned = jnp.dot(
                    value, flip, precision=lax.Precision.HIGHEST, preferred_element_type=jnp.float32
                )
                return jnp.where(flipped, turned, value)

            tiles = [straight(ref[...]) for ref in blocks]

            def channel(c):
                start = (c % per) * wx
                return tiles[c // per][start : start + wx]

            electric_x, electric_y, magnetic_x, magnetic_y = (channel(c) for c in range(4))
            before = inside_x * tiles[3 // per][per * wx : per * wx + 1]
            beside = inside_y * blocks[2 // per][per * wx : per * wx + 8].T[0:wx, 1:2]
            last_x = jnp.where(line == 0, before, pltpu.roll(magnetic_y, 1, 0))
            last_y = jnp.where(lane == 0, beside, pltpu.roll(magnetic_x, 1, 1))
            coef = coef_top[...]
            h_new[0] = h_top[0] - courant * magnetic_x
            h_new[1] = h_top[1] - courant * magnetic_y
            h_copy = pltpu.make_async_copy(h_new, h_out.at[0:2, depth - 1], sems.at[1])
            h_copy.start()
            e_new[0] = e_top[0] + coef * (courant * magnetic_y - electric_x)
            e_new[1] = e_top[1] - coef * (courant * magnetic_x + electric_y)
            e_new[2] = e_top[2] + coef * courant * (
                (magnetic_x - last_y) - (magnetic_y - last_x)
            )
            e_copy = pltpu.make_async_copy(e_new, e_out.at[:, depth - 1], sems.at[0])
            e_copy.start()
            h_copy.wait()
            e_copy.wait()

    return body


def in_hbm(*arrays):
    return [pltpu.with_memory_space_constraint(array, pltpu.HBM) for array in arrays]


def in_vmem(*arrays):
    return [pltpu.with_memory_space_constraint(array, pltpu.VMEM) for array in arrays]


def local(
    e_field, h_field, pole_current, material, pole_table, cotangent, cosines, wavenumber, time_phase
):
    depth, wx, wy = material.shape
    sizes = sx, sy, sz = tuple(lax.axis_size(name) for name in ("gx", "gy", "gz"))
    ix, iy, iz = (lax.axis_index(name) for name in ("gx", "gy", "gz"))
    freqs, _, count = cotangent.shape
    scale = 1.0 / math.sqrt(freqs * count * sx * sy * sz)
    assert wy == LANES and depth * wx == LANES and sx > 1 and sy > 1 and sz > 1
    pad = -count % LANES
    if pad:
        cotangent = jnp.pad(cotangent, ((0, 0), (0, 0), (0, pad)))
        cosines = jnp.pad(cosines, ((0, 0), (0, pad)))
    f32 = jnp.float32
    smem = pl.BlockSpec(memory_space=pltpu.SMEM)
    vmem = pl.BlockSpec(memory_space=pltpu.VMEM)
    hbm = pl.BlockSpec(memory_space=pltpu.HBM)
    small = pltpu.CompilerParams(vmem_limit_bytes=8 << 20)
    xslots = sx // 2
    zslots = min(sz, 4)
    per = 4 // zslots
    xbits, ybits, zbits = bits_of(sx), bits_of(sy), bits_of(sz)
    zcut = bits_of(zslots)

    assert 8 % depth == 0
    mine, waves, e_near, h_near, *layers = pl.pallas_call(
        pack_kernel(freqs, depth, wx, zbits),
        out_shape=[
            pltpu.VMEM((freqs + 1 + 6 * depth // 8, 8, LANES), f32),
            pltpu.VMEM((2, freqs, LANES), f32),
            pltpu.VMEM(e_field.shape, f32),
            pltpu.VMEM(h_field.shape, f32),
        ]
        + [pltpu.VMEM((6, wx, wy), f32)] * zbits,
        in_specs=[hbm] * 6,
        out_specs=[vmem] * (4 + zbits),
        scratch_shapes=[
            pltpu.VMEM((2, LANES), f32),
            pltpu.SMEM((freqs,), f32),
            pltpu.SMEM((freqs,), f32),
            pltpu.SemaphoreType.DMA((6,)),
        ],
        compiler_params=small,
        name="pack",
    )(*in_hbm(e_field, h_field, cotangent, cosines, wavenumber, time_phase))
    e_near, h_near = in_vmem(e_near, h_near)
    theirs = exchange(mine, "gx", 1)
    zs = [exchange(layers[k], "gz", (2 << k) - 1) for k in range(zbits)]
    zs = in_vmem(*zs)

    half = sy * wy // 2
    xlevels = max(3, (wx - 1).bit_length())
    ylevels = max(3, (half - 1).bit_length()) + 1
    width = count + pad
    block = per * wx + 8
    part_shape = pltpu.VMEM((zslots // 2, sy, xslots, block, wy), f32)
    assert freqs % 2 == 0
    sums = pltpu.VMEM((4 * xslots * wx + 16, half), f32)
    tables = [
        pltpu.VMEM((xslots, 2, freqs, width), f32),
        pltpu.VMEM((xlevels, 2, freqs, width), f32),
        pltpu.VMEM((ylevels, 2, freqs, width), f32),
    ]
    medium = pltpu.CompilerParams(vmem_limit_bytes=24 << 20)
    waves, mine = in_vmem(waves, mine)
    own = pl.pallas_call(
        source_kernel(freqs, depth, wx, half, sizes, zslots, xslots, scale, zbits, False),
        out_shape=(sums, sums),
        in_specs=[vmem] * 2,
        out_specs=(vmem, vmem),
        scratch_shapes=tables,
        compiler_params=medium,
        name="source_own",
    )(waves, mine)
    with jax.named_scope("source_all"):
        keep, send = pl.pallas_call(
            source_kernel(freqs, depth, wx, half, sizes, zslots, xslots, scale, zbits, True),
            out_shape=(part_shape, part_shape),
            in_specs=[vmem] * (4 + zbits),
            out_specs=(vmem, vmem),
            scratch_shapes=tables + [sums, sums],
            compiler_params=medium,
            name="source_both",
        )(waves, *in_vmem(theirs, *own), *zs)

    strip = pltpu.VMEM((8, LANES), f32)
    first, last = pl.pallas_call(
        column_kernel(freqs, depth, wx, wy, zbits),
        out_shape=(strip, strip),
        in_specs=[vmem] * (3 + zbits),
        out_specs=(vmem, vmem),
        compiler_params=small,
        name="columns",
    )(e_near, h_near, *in_vmem(theirs), *zs)

    whole = jax.ShapeDtypeStruct((3, depth, wx, wy), f32)
    pole_next, base_e, coef = pl.pallas_call(
        pole_kernel(depth, wx, wy),
        out_shape=(whole, pltpu.VMEM(whole.shape, f32), pltpu.VMEM((depth, wx, wy), f32)),
        in_specs=[hbm, vmem, hbm, hbm, vmem],
        out_specs=(hbm, vmem, vmem),
        scratch_shapes=[
            pltpu.SMEM(pole_table.shape, f32),
            pltpu.VMEM(whole.shape, f32),
            pltpu.VMEM((depth, wx, wy), jnp.int32),
            pltpu.VMEM(whole.shape, f32),
            pltpu.SemaphoreType.DMA((3,)),
        ],
        compiler_params=small,
        name="pole",
    )(*in_hbm(pole_table), e_near, *in_hbm(pole_current, material), *in_vmem(first))
    base_e, coef = in_vmem(base_e, coef)

    def flat(value):
        return value.reshape(-1, LANES)

    terms = [keep, exchange(send, "gz", 1)]
    sides = [flat(terms[1])]
    for k in range(1, zbits):
        at = (1 - ((iz >> k) & 1)) * (depth - 1)
        rows = theirs[freqs + 1 :].reshape(6, depth, LANES)
        rows = lax.dynamic_index_in_dim(rows, at, 1, keepdims=False)
        sides.append(exchange(jnp.pad(rows, ((per * wx + 2, 0), (0, 0))), "gz", (2 << k) - 1))
    for k in range(1, zbits):
        part = terms[0] + terms[1]
        mask = (2 << k) - 1
        if k < zcut:
            middle = part.shape[0] // 2
            terms = [part[:middle], exchange(part[middle:], "gz", mask)]
        else:
            terms = [part, exchange(part, "gz", mask)]
    terms = [flat(term) for term in terms]
    rows = sy * xslots * block

    ys = [None] * ybits
    k = 0
    while k < ybits:
        both = k + 1 < ybits
        size = rows // 4 if both else rows // 2
        plain, laden = pltpu.VMEM((size, LANES), f32), pltpu.VMEM((size + 8, LANES), f32)
        shapes = (plain, laden, laden, plain) if both else (plain, laden)
        keep, *away = pl.pallas_call(
            merge_y_kernel(len(terms), rows, k, ybits),
            out_shape=shapes,
            in_specs=[vmem] * (len(terms) + 2),
            out_specs=(vmem,) * len(shapes),
            compiler_params=small,
            name="merge_y",
        )(*in_vmem(*terms, first, last))
        if both:
            ys[k] = exchange(away[1], "gy", (2 << k) - 1)
            other = exchange(away[2], "gy", 2 << k)
            ys[k + 1] = exchange(away[0], "gy", (4 << k) - 1)
            terms = [keep, ys[k], ys[k + 1], other]
            k += 2
        else:
            ys[k] = exchange(away[0], "gy", (2 << k) - 1)
            terms = [keep, ys[k]]
            k += 1
        rows = size
    near = [*zs, *in_vmem(*ys)]
    xs = []
    for k in range(1, xbits):
        keep, away = pl.pallas_call(
            merge_x_kernel(len(terms), rows, depth, wx, wy, zbits, ybits, k),
            out_shape=(
                pltpu.VMEM((rows // 2, LANES), f32),
                pltpu.VMEM((rows // 2 + 6 * depth + 8, LANES), f32),
            ),
            in_specs=[vmem] * (len(terms) + 3 + zbits + ybits),
            out_specs=(vmem, vmem),
            compiler_params=small,
            name="merge_x",
        )(*in_vmem(*terms), e_near, h_near, *near, coef)
        xs.append(exchange(away, "gx", (2 << k) - 1))
        rows //= 2
        terms = [keep, xs[-1]]
    part = sum(term[:rows] for term in terms)

    layer = pltpu.VMEM((3, wx, wy), f32)
    e_next, h_next, e_top, h_top, coef_top = pl.pallas_call(
        field_kernel(freqs, depth, wx, wy, xbits, ybits, zbits, per * wx + 2),
        out_shape=(whole, whole, layer, layer, pltpu.VMEM((wx, wy), f32)),
        in_specs=[vmem] * (5 + xbits + ybits + 2 * zbits),
        out_specs=(vmem,) * 5,
        compiler_params=pltpu.CompilerParams(vmem_limit_bytes=16 << 20),
        name="fields",
    )(e_near, h_near, base_e, coef, *in_vmem(first, theirs), *near, *in_vmem(*xs, *sides))

    top = gray(sz - 1)
    blocks = [part]
    for k in reversed(range(zcut)):
        others = [exchange(value, "gz", (2 << k) - 1) for value in blocks]
        blocks = others + blocks if (top >> k) & 1 else blocks + others
    e_next, h_next = pl.pallas_call(
        inject_kernel(depth, wx, wy, sy, sz, per, zcut),
        out_shape=(whole, whole),
        in_specs=[vmem] * (len(blocks) + 3) + [hbm] * 2,
        out_specs=(hbm, hbm),
        scratch_shapes=[
            pltpu.VMEM((3, wx, wy), f32),
            pltpu.VMEM((2, wx, wy), f32),
            pltpu.SemaphoreType.DMA((2,)),
        ],
        input_output_aliases={len(blocks) + 3: 0, len(blocks) + 4: 1},
        compiler_params=small,
        name="inject",
    )(*in_vmem(*blocks, e_top, h_top, coef_top), e_next, h_next)
    return (e_next, h_next, pole_next)


def solution(mesh):
    in_specs = (
        P(None, "gz", "gx", "gy"),
        P(None, "gz", "gx", "gy"),
        P(None, "gz", "gx", "gy"),
        P("gz", "gx", "gy"),
        P(),
        P(None, None, ("gx", "gy", "gz")),
        P(None, ("gx", "gy", "gz")),
        P(),
        P(),
    )
    out_specs = (P(None, "gz", "gx", "gy"), P(None, "gz", "gx", "gy"), P(None, "gz", "gx", "gy"))
    return jax.shard_map(local, mesh=mesh, in_specs=in_specs, out_specs=out_specs, check_vma=False)
```

```python
import math

import jax
import jax.numpy as jnp
from jax import lax
from jax.experimental import pallas as pl
from jax.experimental.pallas import tpu as pltpu
from jax.sharding import PartitionSpec as P

NPOLE = 4
LANES = 128


courant = 0.5


def exchange(array, axis, mask):
    return lax.ppermute(array, axis, [(i, i ^ mask) for i in range(lax.axis_size(axis))])


def gray(index):
    return index ^ (index >> 1)


def ungray(code, bits):
    index = code
    for step in range(1, bits):
        index = index ^ (code >> step)
    return index


def bits_of(size):
    return size.bit_length() - 1


def cmul(a, b):
    return (a[0] * b[0] - a[1] * b[1], a[0] * b[1] + a[1] * b[0])


def small_turn(angle):
    q = angle * angle
    c = 1.0 + q * (-1 / 2 + q * (1 / 24 + q * (-1 / 720 + q * (1 / 40320))))
    s = angle * (1.0 + q * (-1 / 6 + q * (1 / 120 + q * (-1 / 5040 + q * (1 / 362880)))))
    return c, s


def doubled(turn):
    c, s = turn
    return (c - s) * (c + s), 2.0 * (c * s)


def rotations(base, powers, rows):
    sub = lax.broadcasted_iota(jnp.int32, (8, base[0].shape[-1]), 0)
    value = tuple(jnp.broadcast_to(part, sub.shape) for part in base)
    for k in range(3):
        picked = (sub & (1 << k)) != 0
        value = cmul(value, (jnp.where(picked, powers[k][0], 1.0), jnp.where(picked, powers[k][1], 0.0)))
    blocks = [value]
    k = 3
    while len(blocks) * 8 < rows:
        blocks = blocks + [cmul(block, powers[k]) for block in blocks]
        k += 1
    return tuple(jnp.concatenate([block[i] for block in blocks], axis=0)[:rows] for i in (0, 1))


def split(value):
    high = value.astype(jnp.bfloat16)
    return high, (value - high.astype(jnp.float32)).astype(jnp.bfloat16)


def dot_nt(a, b):
    return lax.dot_general(a, b, (((1,), (1,)), ((), ())), preferred_element_type=jnp.float32)


def source_kernel(freqs, depth, wx, half, sizes, zslots, xslots, scale, zbits, closing):
    sx, sy, sz = sizes
    xbits = max(3, (wx - 1).bit_length())
    ybits = max(3, (half - 1).bit_length())
    per = 4 // zslots
    main = 4 * xslots * wx

    def body(*refs):
        waves, packed = refs[:2]
        if closing:
            old_even, old_odd = refs[2:4]
            keep, send, xbase, xpow, ypow, acc_even, acc_odd = refs[4 + zbits :]
        else:
            e_in, h_in, acc_even, acc_odd, e_near, h_near, xbase, xpow, ypow, sems = refs[2:]
            copies = [
                pltpu.make_async_copy(source, target, sems.at[i])
                for i, (source, target) in enumerate(((e_in, e_near), (h_in, h_near)))
            ]
            for copy in copies:
                copy.start()
        ix, iy, iz = (lax.axis_index(name) for name in ("gx", "gy", "gz"))
        xbit, ybit, zbit = bits_of(sx), bits_of(sy), bits_of(zslots)
        starts = []
        for slot in range(xslots):
            code = gray(ix)
            for k in range(1, xbit):
                code = code ^ (((slot >> (xbit - 1 - k)) & 1) << k)
            starts.append((ungray(code, xbit) * wx).astype(jnp.float32))
        zcode = 0
        for k in range(zbit):
            zcode = zcode * 2 + ((gray(iz) >> k) & 1)
        ycode = gray(iy)
        center = (2 * half - 1) / 2.0
        wave, phase = waves[0], waves[1]
        along_x = wave * packed[freqs, 0:1, :]
        along_y = wave * packed[freqs, 1:2, :]
        origin = along_y * center - phase
        for xr in range(xslots):
            angle = along_x * starts[xr] + origin
            xbase[xr, 0] = jnp.cos(angle)
            xbase[xr, 1] = jnp.sin(angle)
        turn = doubled(small_turn(0.5 * along_x))
        for k in range(xbits):
            xpow[k, 0], xpow[k, 1] = turn
            turn = doubled(turn)
        turn = small_turn(0.5 * along_y)
        for k in range(ybits + 1):
            ypow[k, 0], ypow[k, 1] = turn
            turn = doubled(turn)
        if closing:
            acc_even[...] = old_even[...]
            acc_odd[...] = old_odd[...]
        else:
            acc_even[...] = jnp.zeros_like(acc_even)
            acc_odd[...] = jnp.zeros_like(acc_odd)

        def pair(step, carry):
            firsts, seconds, coses, sines = [], [], [], []
            for n in range(2):
                f = 2 * step + n

                def row(ref, *where):
                    return tuple(ref[(*where, i, pl.ds(f, 1), slice(None))] for i in (0, 1))

                powers = [row(ypow, k) for k in range(ybits + 1)]
                cy, sy_ = rotations(powers[0], powers[1:], half)
                coses.append(cy)
                sines.append(sy_)
                powers = [row(xpow, k) for k in range(xbits)]
                bases = [row(xbase, xr) for xr in range(xslots)]
                turns = [rotations(base, powers, wx) for base in bases]
                first, second = [], []
                for zr in range(zslots):
                    for xr in range(xslots):
                        cx, sx_ = turns[xr]
                        for c2 in range(per):
                            at = 2 * ((zcode ^ zr) * per + c2)
                            p = packed[f, pl.ds(at, 1), :]
                            q = packed[f, pl.ds(at + 1, 1), :]
                            first.append(p * cx - q * sx_)
                            second.append(p * sx_ + q * cx)
                back = (powers[0][0], -powers[0][1])
                p = packed[f, 6:7, :]
                q = packed[f, 7:8, :]
                line = lax.broadcasted_iota(jnp.int32, (16, p.shape[-1]), 0)
                one_first = jnp.zeros(line.shape, jnp.float32)
                one_second = one_first
                for xr in range(xslots):
                    cx, sx_ = cmul(bases[xr], back)
                    one_first = jnp.where(line == xr, p * cx - q * sx_, one_first)
                    one_second = jnp.where(line == xr, p * sx_ + q * cx, one_second)
                firsts.append(jnp.concatenate(first + [one_first], axis=0))
                seconds.append(jnp.concatenate(second + [one_second], axis=0))

            def product(lefts, rights):
                lh, ll = split(jnp.concatenate(lefts, axis=1))
                rh, rl = split(jnp.concatenate(rights, axis=1))
                both = dot_nt(jnp.concatenate([lh, ll], axis=0), rh)
                rows = lh.shape[0]
                return both[:rows] + dot_nt(lh, rl) + both[rows:]

            acc_even[...] += product(firsts, coses)
            acc_odd[...] += product(seconds, sines)
            return carry

        lax.fori_loop(0, freqs // 2, pair, 0, unroll=4)
        if not closing:
            for copy in copies:
                copy.wait()
            return

        def slot(tile):
            code = gray(tile) ^ ycode
            place = 0
            for k in range(ybit):
                place = place * 2 + ((code >> k) & 1)
            return place

        def place(zr):
            return (keep, zr) if zr < zslots // 2 else (send, zr - zslots // 2)

        extra = per * wx
        for zr in range(zslots):
            ref, z = place(zr)
            for y in range(sy):
                for xr in range(xslots):
                    ref[z, y, xr, extra : extra + 8] = jnp.zeros((8, LANES), jnp.float32)
        at_z = (1 - (iz & 1)) * (depth - 1)
        for i in range(6):
            row = i * depth
            send[0, 0, 0, extra + 2 + i : extra + 3 + i] = packed[
                freqs + 1 + row // 8, pl.ds(row % 8 + at_z, 1), :
            ]
        turned = 2 // per
        spare = 2 % per
        for j in range(sy // 2):
            lanes = slice(j * LANES, (j + 1) * LANES)
            up = slot(sy // 2 + j)
            down = slot(sy // 2 - 1 - j)
            at = 0
            for zr in range(zslots):
                ref, z = place(zr)
                for xr in range(xslots):
                    for c2 in range(per):
                        rows = slice(at * wx, (at + 1) * wx)
                        even = acc_even[rows, lanes] * scale
                        odd = acc_odd[rows, lanes] * scale
                        ref[z, up, xr, c2 * wx : (c2 + 1) * wx] = even - odd
                        ref[z, down, xr, c2 * wx : (c2 + 1) * wx] = even + odd
                        at += 1
            for xr in range(xslots):
                even = acc_even[main + xr : main + xr + 1, lanes] * scale
                odd = acc_odd[main + xr : main + xr + 1, lanes] * scale
                for zr in range(zslots):
                    ref, z = place(zr)
                    ref[z, up, xr, extra : extra + 1] = even - odd
                    ref[z, down, xr, extra : extra + 1] = even + odd
                start = (((zcode ^ turned) * xslots + xr) * per + spare) * wx
                rows = pl.ds(pl.multiple_of(start, wx), wx)
                even = (acc_even[rows, lanes] * scale).T
                odd = (acc_odd[rows, lanes] * scale).T
                lower = slot(sy // 2 - j)
                for zr in range(zslots):
                    ref, z = place(zr)
                    ref[z, lower, xr, extra + 1 : extra + 2, 0:wx] = even[0:1] + odd[0:1]
                if j < sy // 2 - 1:
                    upper = slot(sy // 2 + j + 1)
                    for zr in range(zslots):
                        ref, z = place(zr)
                        ref[z, upper, xr, extra + 1 : extra + 2, 0:wx] = even[LANES - 1 :] - odd[LANES - 1 :]

    return body


def near_flags(index, bits):
    low, high = [], []
    for k in range(bits):
        upper = (index >> k) & 1
        rest = index & ((1 << k) - 1)
        low.append(((upper == 1) & (rest == 0)).astype(jnp.float32))
        high.append(((upper == 0) & (rest == (1 << k) - 1)).astype(jnp.float32))
    return low, high


def weighted(flags, values):
    total = flags[0] * values[0]
    for flag, value in zip(flags[1:], values[1:]):
        total = total + flag * value
    return total


def pack_kernel(freqs, depth, wx, zbits):
    def body(*refs):
        e_in, h_in, cotangent, cosines, wavenumber, time_phase, message, waves = refs[:8]
        layers = refs[8 : 8 + zbits]
        edge, cos_near, wave_near, phase_near, sems = refs[8 + zbits :]
        upper = lax.axis_index("gx") & 1
        tile = pl.ds(pl.multiple_of((1 - upper) * (wx - 8), 8), 8)
        pairs = [
            (cotangent, message.at[0:freqs]),
            (e_in.at[:, :, tile], edge.at[0:3]),
            (h_in.at[:, :, tile], edge.at[3:6]),
            (cosines, cos_near),
            (wavenumber, wave_near),
            (time_phase, phase_near),
        ]
        for k, layer in enumerate(layers):
            at = (1 - ((lax.axis_index("gz") >> k) & 1)) * (depth - 1)
            pairs += [(e_in.at[:, at], layer.at[0:3]), (h_in.at[:, at], layer.at[3:6])]
        copies = [
            pltpu.make_async_copy(source, target, sems.at[i])
            for i, (source, target) in enumerate(pairs)
        ]
        for copy in copies:
            copy.start()
        for copy in copies:
            copy.wait()
        message[freqs, 0:2] = cos_near[...]
        message[freqs, 2:8] = jnp.zeros((6, LANES), jnp.float32)
        which = lax.broadcasted_iota(jnp.int32, (freqs, LANES), 0)
        for i, near in enumerate((wave_near, phase_near)):
            value = jnp.zeros((freqs, LANES), jnp.float32)
            for f in range(freqs):
                value = jnp.where(which == f, near[f], value)
            waves[i] = value
        at = (1 - upper) * 7
        for i in range(6):
            for z in range(depth):
                row = i * depth + z
                message[freqs + 1 + row // 8, row % 8 : row % 8 + 1] = edge[i, z, pl.ds(at, 1), :]

    return body


def early_rows(message, freqs, depth, i):
    row = i * depth
    return message[freqs + 1 + row // 8, row % 8 : row % 8 + depth]


def column_kernel(freqs, depth, wx, wy, zbits):
    def body(*refs):
        e, h, message = refs[:3]
        zs = refs[3 : 3 + zbits]
        first, last = refs[3 + zbits :]
        low, high = near_flags(lax.axis_index("gz"), zbits)
        lane = lax.broadcasted_iota(jnp.int32, (1, LANES), 1)
        first[...] = jnp.zeros_like(first)
        last[...] = jnp.zeros_like(last)
        for i, field in enumerate((e[0], e[1], e[2], h[0], h[2])):
            turned = field.reshape(depth * wx, wy).T
            first[i : i + 1] = turned[0:1]
            last[i : i + 1] = turned[wy - 1 :]
        for i, layer in (
            (5, weighted(high, [z[1, 0:wx] for z in zs])),
            (6, weighted(low, [z[2, 0:wx] for z in zs])),
        ):
            turned = layer.T
            first[i : i + 1, 0:wx] = turned[0:1]
            last[i : i + 1, 0:wx] = turned[wy - 1 :]
        for ref, y in ((first, 0), (last, wy - 1)):
            corner = jnp.zeros((1, LANES), jnp.float32)
            side_x, side_y = (early_rows(message, freqs, depth, i)[:, y : y + 1] for i in (0, 1))
            for z in range(depth):
                corner = jnp.where(lane == z, side_x[z : z + 1], corner)
                corner = jnp.where(lane == z * wx + wx - 1, side_y[z : z + 1], corner)
            ref[7:8] = corner

    return body


def total_of(terms, rows):
    value = terms[0][rows]
    for term in terms[1:]:
        value = value + term[rows]
    return value


def merge_y_kernel(count, rows, k, ybits):
    def body(*refs):
        terms, (first, last), outs = refs[:count], refs[count : count + 2], refs[count + 2 :]
        iy = lax.axis_index("gy")
        size = rows // len(outs)
        swaps = (None, k) if len(outs) == 2 else (None, k + 1, k, None)
        for i, (out, swap) in enumerate(zip(outs, swaps)):
            out[0:size] = total_of(terms, slice(i * size, (i + 1) * size))
            if swap is not None:
                upper = ((iy >> swap) & 1).astype(jnp.float32)
                out[size : size + 8] = upper * first[...] + (1.0 - upper) * last[...]

    return body


def halo_at(ref):
    rows = ref.shape[0]
    return ref[rows - 8 : rows]


def merge_x_kernel(count, rows, depth, wx, wy, zbits, ybits, k):
    def body(*refs):
        terms = refs[:count]
        e, h = refs[count : count + 2]
        zs = refs[count + 2 : count + 2 + zbits]
        ys = refs[count + 2 + zbits : count + 2 + zbits + ybits]
        keep, out = refs[count + 3 + zbits + ybits :]
        size = rows // 2
        keep[...] = total_of(terms, slice(0, size))
        out[0:size] = total_of(terms, slice(size, rows))
        zlow, zhigh = near_flags(lax.axis_index("gz"), zbits)
        ylow, yhigh = near_flags(lax.axis_index("gy"), ybits)
        at = (1 - ((lax.axis_index("gx") >> k) & 1)) * (wx - 1)
        for i in range(3):
            for z in range(depth):
                row = size + i * depth + z
                out[row : row + 1] = e[i, z, pl.ds(at, 1), :]
                row = size + (3 + i) * depth + z
                out[row : row + 1] = h[i, z, pl.ds(at, 1), :]
        base = size + 6 * depth
        halos = [halo_at(y) for y in ys]
        out[base : base + 1] = weighted(zhigh, [z[0, pl.ds(at, 1), :] for z in zs])
        out[base + 1 : base + 2] = weighted(zlow, [z[2, pl.ds(at, 1), :] for z in zs])
        out[base + 2 : base + 3] = weighted(yhigh, [y[0:1] for y in halos])
        out[base + 3 : base + 4] = weighted(ylow, [y[1:2] for y in halos])
        out[base + 4 : base + 8] = jnp.zeros((4, LANES), jnp.float32)

    return body


def pole_kernel(depth, wx, wy):
    def body(table_in, e, pole_in, material_in, after, pole_out, base, coef_out, *scratch):
        table, pole, material, new_pole, sems = scratch
        copies = [
            pltpu.make_async_copy(source, target, sems.at[i])
            for i, (source, target) in enumerate(
                ((table_in, table), (material_in, material), (pole_in, pole))
            )
        ]
        for copy in copies:
            copy.start()
        for copy in copies:
            copy.wait()
        kind = material[...]

        def chosen(i):
            value = jnp.full(kind.shape, table[i, NPOLE - 1], jnp.float32)
            for m in range(NPOLE - 1):
                value = jnp.where(kind == m, table[i, m], value)
            return value

        decay, drive, coef = (chosen(i) for i in range(3))
        coef_out[...] = coef
        for i in range(3):
            old = pole[i]
            electric = e[i]
            new = decay * old + drive * electric
            new_pole[i] = new
            base[i] = electric - coef * (0.5 * (new + old))
        copy = pltpu.make_async_copy(new_pole, pole_out, sems.at[0])
        copy.start()
        copy.wait()

    return body


def field_kernel(freqs, depth, wx, wy, xbits, ybits, zbits, side_row):
    def body(*refs):
        e, h, base_e, coef_ref, first, message = refs[:6]
        zs = refs[6 : 6 + zbits]
        ys = refs[6 + zbits : 6 + zbits + ybits]
        xs = [x[x.shape[0] - 6 * depth - 8 :] for x in refs[6 + zbits + ybits : 5 + zbits + ybits + xbits]]
        sides = refs[5 + zbits + ybits + xbits : 5 + 2 * zbits + ybits + xbits]
        e_out, h_out = refs[5 + 2 * zbits + ybits + xbits :]
        ix, iy, iz = (lax.axis_index(name) for name in ("gx", "gy", "gz"))
        xlow, xhigh = near_flags(ix, xbits)
        ylow, yhigh = near_flags(iy, ybits)
        zlow, zhigh = near_flags(iz, zbits)
        size = depth * wx
        base = 6 * depth
        lane = lax.broadcasted_iota(jnp.int32, (size, wy), 1)
        line = lax.broadcasted_iota(jnp.int32, (size, wy), 0) & (wx - 1)
        inside_x, inside_y, inside_z = (
            (index > 0).astype(jnp.float32) for index in (ix, iy, iz)
        )

        def flat(ref, i):
            return ref[i].reshape(size, wy)

        ex, ey, ez = (flat(e, i) for i in range(3))
        oldx, oldy, oldz = (flat(h, i) for i in range(3))

        def spread(rows):
            return jnp.broadcast_to(rows[:, None, :], (depth, wx, wy)).reshape(size, wy)

        def next_y(value, column):
            rows = value.shape[0]
            return jnp.where(lane[:rows] == wy - 1, column, pltpu.roll(value, wy - 1, 1))

        def next_x(value, rows):
            return jnp.where(line == wx - 1, spread(rows), pltpu.roll(value, size - 1, 0))

        def next_z(value, layer):
            return jnp.concatenate([value[wx:], layer], axis=0)

        def last_y(value, column):
            return jnp.where(lane == 0, column, pltpu.roll(value, 1, 1))

        def last_x(value, rows):
            return jnp.where(line == 0, spread(rows), pltpu.roll(value, 1, 0))

        def last_z(value, layer):
            return jnp.concatenate([layer, value[:-wx]], axis=0)

        ylo = weighted(ylow, [halo_at(y) for y in ys])
        yhi = weighted(yhigh, [halo_at(y) for y in ys])
        above = yhi.T

        def rows_of(flags, i):
            at = slice(i * depth, (i + 1) * depth)
            return weighted(flags, [early_rows(message, freqs, depth, i)] + [x[at] for x in xs])

        def extra_of(flags, early, i):
            return weighted(flags, [early] + [x[base + i : base + i + 1] for x in xs])

        def layer_of(flags, i):
            return weighted(flags, [z[i, 0:wx] for z in zs])

        def side_of(flags, i):
            at = side_row + i
            return weighted(flags, [side[at : at + 1] for side in sides])

        up_x, up_y = layer_of(zhigh, 0), layer_of(zhigh, 1)
        hx = oldx - courant * ((next_y(ez, above[:, 2:3]) - ez) - (next_z(ey, up_y) - ey))
        hy = oldy - courant * (
            (next_z(ex, up_x) - ex) - (next_x(ez, rows_of(xhigh, 2)) - ez)
        )
        hz = oldz - courant * (
            (next_x(ey, rows_of(xhigh, 1)) - ey) - (next_y(ex, above[:, 0:1]) - ex)
        )
        mx, my, mz = (rows_of(xlow, i) for i in range(3))
        up = jnp.concatenate([mx[1:], extra_of(xlow, side_of(zhigh, 0), 0)], axis=0)
        low_hy = rows_of(xlow, 4) - courant * ((up - mx) - (e[2, :, 0, :] - mz))
        corner = xlow[0] * above[0:depth, 7:8]
        for flag, x in zip(xlow[1:], xs):
            tail = x[base : base + 8].T
            picks = [tail[z * wx + wx - 1 : (z + 1) * wx, 2:3] for z in range(depth)]
            corner = corner + flag * jnp.concatenate(picks, axis=0)
        low_hz = rows_of(xlow, 5) - courant * (
            (e[1, :, 0, :] - my) - (next_y(mx, corner) - mx)
        )
        strip = lax.broadcasted_iota(jnp.int32, (1, LANES), 1)
        lx, ly, lz = ylo[0:1], ylo[1:2], ylo[2:3]
        up = jnp.where(
            strip >= size - wx, pltpu.roll(ylo[5:6], size - wx, 1), pltpu.roll(ly, LANES - wx, 1)
        )
        side_hx = ylo[3:4] - courant * ((first[2:3] - lz) - (up - ly))
        corner = xhigh[0] * ylo[7:8]
        for flag, x in zip(xhigh[1:], xs):
            corner = corner + flag * pltpu.roll(x[base + 3 : base + 4], wx - 1, 1)
        right = jnp.where((strip & (wx - 1)) == wx - 1, corner, pltpu.roll(ly, LANES - 1, 1))
        side_hz = ylo[4:5] - courant * ((right - ly) - (first[0:1] - lx))
        both = jnp.concatenate([side_hx, side_hz, jnp.zeros((6, LANES), jnp.float32)], axis=0)
        both = (inside_y * both).T
        bx, by, bz = (layer_of(zlow, i) for i in range(3))
        under_hx = layer_of(zlow, 3) - courant * (
            (next_y(bz, above[0:wx, 6:7]) - bz) - (ey[:wx] - by)
        )
        right = jnp.concatenate([bz[1:], extra_of(xhigh, side_of(zlow, 2), 1)], axis=0)
        under_hy = layer_of(zlow, 4) - courant * ((ex[:wx] - bx) - (right - bz))
        under_hx = inside_z * under_hx
        under_hy = inside_z * under_hy
        low_hy = inside_x * low_hy
        low_hz = inside_x * low_hz
        curl = (
            (hz - last_y(hz, both[:, 1:2])) - (hy - last_z(hy, under_hy)),
            (hx - last_z(hx, under_hx)) - (hz - last_x(hz, low_hz)),
            (hy - last_x(hy, low_hy)) - (hx - last_y(hx, both[:, 0:1])),
        )
        coef = coef_ref[...].reshape(size, wy)
        shape = (depth, wx, wy)
        for i, magnetic in enumerate((hx, hy, hz)):
            value = flat(base_e, i) + coef * curl[i]
            h_out[i] = magnetic.reshape(shape)
            e_out[i] = value.reshape(shape)

    return body


def inject_kernel(depth, wx, wy, sy, sz, per, zcut):
    def body(*refs):
        blocks = refs[: 1 << zcut]
        e_near, h_near, coef_ref, e_out, h_out, e_new, h_new, sems = refs[1 << zcut :]
        last = depth - 1
        others = slice(0, last)
        copies = [
            pltpu.make_async_copy(e_near.at[:, others], e_out.at[:, others], sems.at[0]),
            pltpu.make_async_copy(h_near.at[:, others], h_out.at[:, others], sems.at[1]),
            pltpu.make_async_copy(h_near.at[2, last], h_out.at[2, last], sems.at[2]),
        ]
        for copy in copies:
            copy.start()
        h_copy = pltpu.make_async_copy(h_new, h_out.at[0:2, last], sems.at[3])
        e_copy = pltpu.make_async_copy(e_new, e_out.at[:, last], sems.at[4])
        ix, iy, iz = (lax.axis_index(name) for name in ("gx", "gy", "gz"))

        @pl.when(iz == sz - 1)
        def _():
            inside_x, inside_y = ((index > 0).astype(jnp.float32) for index in (ix, iy))
            lane = lax.broadcasted_iota(jnp.int32, (wx, wy), 1)
            line = lax.broadcasted_iota(jnp.int32, (wx, wy), 0)
            flip = (
                lax.broadcasted_iota(jnp.int32, (wy, wy), 0)
                + lax.broadcasted_iota(jnp.int32, (wy, wy), 1)
                == wy - 1
            ).astype(jnp.float32)
            flipped = iy < sy // 2

            def straight(value):
                turned = jnp.dot(
                    value, flip, precision=lax.Precision.HIGHEST, preferred_element_type=jnp.float32
                )
                return jnp.where(flipped, turned, value)

            tiles = [straight(ref[...]) for ref in blocks]

            def channel(c):
                start = (c % per) * wx
                return tiles[c // per][start : start + wx]

            electric_x, electric_y, magnetic_x, magnetic_y = (channel(c) for c in range(4))
            before = inside_x * tiles[3 // per][per * wx : per * wx + 1]
            beside = inside_y * blocks[2 // per][per * wx : per * wx + 8].T[0:wx, 1:2]
            last_x = jnp.where(line == 0, before, pltpu.roll(magnetic_y, 1, 0))
            last_y = jnp.where(lane == 0, beside, pltpu.roll(magnetic_x, 1, 1))
            coef = coef_ref[last]
            h_new[0] = h_near[0, last] - courant * magnetic_x
            h_new[1] = h_near[1, last] - courant * magnetic_y
            e_new[0] = e_near[0, last] + coef * (courant * magnetic_y - electric_x)
            e_new[1] = e_near[1, last] - coef * (courant * magnetic_x + electric_y)
            e_new[2] = e_near[2, last] + coef * courant * (
                (magnetic_x - last_y) - (magnetic_y - last_x)
            )

        @pl.when(iz != sz - 1)
        def _():
            for i in range(3):
                e_new[i] = e_near[i, last]
            for i in range(2):
                h_new[i] = h_near[i, last]

        h_copy.start()
        e_copy.start()
        for copy in (*copies, h_copy, e_copy):
            copy.wait()

    return body


def in_hbm(*arrays):
    return [pltpu.with_memory_space_constraint(array, pltpu.HBM) for array in arrays]


def in_vmem(*arrays):
    return [pltpu.with_memory_space_constraint(array, pltpu.VMEM) for array in arrays]


def local(
    e_field, h_field, pole_current, material, pole_table, cotangent, cosines, wavenumber, time_phase
):
    depth, wx, wy = material.shape
    sizes = sx, sy, sz = tuple(lax.axis_size(name) for name in ("gx", "gy", "gz"))
    ix, iy, iz = (lax.axis_index(name) for name in ("gx", "gy", "gz"))
    freqs, _, count = cotangent.shape
    scale = 1.0 / math.sqrt(freqs * count * sx * sy * sz)
    assert wy == LANES and depth * wx == LANES and sx > 1 and sy > 1 and sz > 1
    pad = -count % LANES
    if pad:
        cotangent = jnp.pad(cotangent, ((0, 0), (0, 0), (0, pad)))
        cosines = jnp.pad(cosines, ((0, 0), (0, pad)))
    f32 = jnp.float32
    smem = pl.BlockSpec(memory_space=pltpu.SMEM)
    vmem = pl.BlockSpec(memory_space=pltpu.VMEM)
    hbm = pl.BlockSpec(memory_space=pltpu.HBM)
    small = pltpu.CompilerParams(vmem_limit_bytes=8 << 20)
    xslots = sx // 2
    zslots = min(sz, 4)
    per = 4 // zslots
    xbits, ybits, zbits = bits_of(sx), bits_of(sy), bits_of(sz)
    zcut = bits_of(zslots)

    assert 8 % depth == 0
    mine, waves, *layers = pl.pallas_call(
        pack_kernel(freqs, depth, wx, zbits),
        out_shape=[
            pltpu.VMEM((freqs + 1 + 6 * depth // 8, 8, LANES), f32),
            pltpu.VMEM((2, freqs, LANES), f32),
        ]
        + [pltpu.VMEM((6, wx, wy), f32)] * zbits,
        in_specs=[hbm] * 6,
        out_specs=[vmem] * (2 + zbits),
        scratch_shapes=[
            pltpu.VMEM((6, depth, 8, LANES), f32),
            pltpu.VMEM((2, LANES), f32),
            pltpu.SMEM((freqs,), f32),
            pltpu.SMEM((freqs,), f32),
            pltpu.SemaphoreType.DMA((6 + 2 * zbits,)),
        ],
        compiler_params=small,
        name="pack",
    )(*in_hbm(e_field, h_field, cotangent, cosines, wavenumber, time_phase))
    theirs = exchange(mine, "gx", 1)
    zs = [exchange(layers[k], "gz", (2 << k) - 1) for k in range(zbits)]
    zs = in_vmem(*zs)

    half = sy * wy // 2
    xlevels = max(3, (wx - 1).bit_length())
    ylevels = max(3, (half - 1).bit_length()) + 1
    width = count + pad
    block = per * wx + 8
    part_shape = pltpu.VMEM((zslots // 2, sy, xslots, block, wy), f32)
    assert freqs % 2 == 0
    sums = pltpu.VMEM((4 * xslots * wx + 16, half), f32)
    tables = [
        pltpu.VMEM((xslots, 2, freqs, width), f32),
        pltpu.VMEM((xlevels, 2, freqs, width), f32),
        pltpu.VMEM((ylevels, 2, freqs, width), f32),
    ]
    medium = pltpu.CompilerParams(vmem_limit_bytes=24 << 20)
    waves, mine = in_vmem(waves, mine)
    *own, e_near, h_near = pl.pallas_call(
        source_kernel(freqs, depth, wx, half, sizes, zslots, xslots, scale, zbits, False),
        out_shape=(sums, sums, pltpu.VMEM(e_field.shape, f32), pltpu.VMEM(h_field.shape, f32)),
        in_specs=[vmem, vmem, hbm, hbm],
        out_specs=(vmem,) * 4,
        scratch_shapes=tables + [pltpu.SemaphoreType.DMA((2,))],
        compiler_params=medium,
        name="source_own",
    )(waves, mine, *in_hbm(e_field, h_field))
    e_near, h_near = in_vmem(e_near, h_near)
    with jax.named_scope("source_all"):
        keep, send = pl.pallas_call(
            source_kernel(freqs, depth, wx, half, sizes, zslots, xslots, scale, zbits, True),
            out_shape=(part_shape, part_shape),
            in_specs=[vmem] * (4 + zbits),
            out_specs=(vmem, vmem),
            scratch_shapes=tables + [sums, sums],
            compiler_params=medium,
            name="source_both",
        )(waves, *in_vmem(theirs, *own), *zs)

    strip = pltpu.VMEM((8, LANES), f32)
    first, last = pl.pallas_call(
        column_kernel(freqs, depth, wx, wy, zbits),
        out_shape=(strip, strip),
        in_specs=[vmem] * (3 + zbits),
        out_specs=(vmem, vmem),
        compiler_params=small,
        name="columns",
    )(e_near, h_near, *in_vmem(theirs), *zs)

    whole = jax.ShapeDtypeStruct((3, depth, wx, wy), f32)
    pole_next, base_e, coef = pl.pallas_call(
        pole_kernel(depth, wx, wy),
        out_shape=(whole, pltpu.VMEM(whole.shape, f32), pltpu.VMEM((depth, wx, wy), f32)),
        in_specs=[hbm, vmem, hbm, hbm, vmem],
        out_specs=(hbm, vmem, vmem),
        scratch_shapes=[
            pltpu.SMEM(pole_table.shape, f32),
            pltpu.VMEM(whole.shape, f32),
            pltpu.VMEM((depth, wx, wy), jnp.int32),
            pltpu.VMEM(whole.shape, f32),
            pltpu.SemaphoreType.DMA((3,)),
        ],
        compiler_params=small,
        name="pole",
    )(*in_hbm(pole_table), e_near, *in_hbm(pole_current, material), *in_vmem(first))
    base_e, coef = in_vmem(base_e, coef)

    def flat(value):
        return value.reshape(-1, LANES)

    terms = [keep, exchange(send, "gz", 1)]
    sides = [flat(terms[1])]
    for k in range(1, zbits):
        at = (1 - ((iz >> k) & 1)) * (depth - 1)
        rows = theirs[freqs + 1 :].reshape(6, depth, LANES)
        rows = lax.dynamic_index_in_dim(rows, at, 1, keepdims=False)
        sides.append(exchange(jnp.pad(rows, ((per * wx + 2, 0), (0, 0))), "gz", (2 << k) - 1))
    for k in range(1, zbits):
        part = terms[0] + terms[1]
        mask = (2 << k) - 1
        if k < zcut:
            middle = part.shape[0] // 2
            terms = [part[:middle], exchange(part[middle:], "gz", mask)]
        else:
            terms = [part, exchange(part, "gz", mask)]
    terms = [flat(term) for term in terms]
    rows = sy * xslots * block

    ys = [None] * ybits
    k = 0
    while k < ybits:
        both = k + 1 < ybits
        size = rows // 4 if both else rows // 2
        plain, laden = pltpu.VMEM((size, LANES), f32), pltpu.VMEM((size + 8, LANES), f32)
        shapes = (plain, laden, laden, plain) if both else (plain, laden)
        keep, *away = pl.pallas_call(
            merge_y_kernel(len(terms), rows, k, ybits),
            out_shape=shapes,
            in_specs=[vmem] * (len(terms) + 2),
            out_specs=(vmem,) * len(shapes),
            compiler_params=small,
            name="merge_y",
        )(*in_vmem(*terms, first, last))
        if both:
            ys[k] = exchange(away[1], "gy", (2 << k) - 1)
            other = exchange(away[2], "gy", 2 << k)
            ys[k + 1] = exchange(away[0], "gy", (4 << k) - 1)
            terms = [keep, ys[k], ys[k + 1], other]
            k += 2
        else:
            ys[k] = exchange(away[0], "gy", (2 << k) - 1)
            terms = [keep, ys[k]]
            k += 1
        rows = size
    near = [*zs, *in_vmem(*ys)]
    xs = []
    for k in range(1, xbits):
        keep, away = pl.pallas_call(
            merge_x_kernel(len(terms), rows, depth, wx, wy, zbits, ybits, k),
            out_shape=(
                pltpu.VMEM((rows // 2, LANES), f32),
                pltpu.VMEM((rows // 2 + 6 * depth + 8, LANES), f32),
            ),
            in_specs=[vmem] * (len(terms) + 3 + zbits + ybits),
            out_specs=(vmem, vmem),
            compiler_params=small,
            name="merge_x",
        )(*in_vmem(*terms), e_near, h_near, *near, coef)
        xs.append(exchange(away, "gx", (2 << k) - 1))
        rows //= 2
        terms = [keep, xs[-1]]
    part = sum(term[:rows] for term in terms)

    e_most, h_most = pl.pallas_call(
        field_kernel(freqs, depth, wx, wy, xbits, ybits, zbits, per * wx + 2),
        out_shape=(pltpu.VMEM(whole.shape, f32), pltpu.VMEM(whole.shape, f32)),
        in_specs=[vmem] * (5 + xbits + ybits + 2 * zbits),
        out_specs=(vmem,) * 2,
        compiler_params=pltpu.CompilerParams(vmem_limit_bytes=16 << 20),
        name="fields",
    )(e_near, h_near, base_e, coef, *in_vmem(first, theirs), *near, *in_vmem(*xs, *sides))

    top = gray(sz - 1)
    blocks = [part]
    for k in reversed(range(zcut)):
        others = [exchange(value, "gz", (2 << k) - 1) for value in blocks]
        blocks = others + blocks if (top >> k) & 1 else blocks + others
    e_next, h_next = pl.pallas_call(
        inject_kernel(depth, wx, wy, sy, sz, per, zcut),
        out_shape=(whole, whole),
        in_specs=[vmem] * (len(blocks) + 3),
        out_specs=(hbm, hbm),
        scratch_shapes=[
            pltpu.VMEM((3, wx, wy), f32),
            pltpu.VMEM((2, wx, wy), f32),
            pltpu.SemaphoreType.DMA((5,)),
        ],
        compiler_params=small,
        name="inject",
    )(*in_vmem(*blocks, e_most, h_most), coef)
    return (e_next, h_next, pole_next)


def solution(mesh):
    in_specs = (
        P(None, "gz", "gx", "gy"),
        P(None, "gz", "gx", "gy"),
        P(None, "gz", "gx", "gy"),
        P("gz", "gx", "gy"),
        P(),
        P(None, None, ("gx", "gy", "gz")),
        P(None, ("gx", "gy", "gz")),
        P(),
        P(),
    )
    out_specs = (P(None, "gz", "gx", "gy"), P(None, "gz", "gx", "gy"), P(None, "gz", "gx", "gy"))
    return jax.shard_map(local, mesh=mesh, in_specs=in_specs, out_specs=out_specs, check_vma=False)
```

```python
import math

import jax
import jax.numpy as jnp
from jax import lax
from jax.experimental import pallas as pl
from jax.experimental.pallas import tpu as pltpu
from jax.sharding import PartitionSpec as P

NPOLE = 4
LANES = 128


courant = 0.5


def exchange(array, axis, mask):
    return lax.ppermute(array, axis, [(i, i ^ mask) for i in range(lax.axis_size(axis))])


def gray(index):
    return index ^ (index >> 1)


def ungray(code, bits):
    index = code
    for step in range(1, bits):
        index = index ^ (code >> step)
    return index


def bits_of(size):
    return size.bit_length() - 1


def cmul(a, b):
    return (a[0] * b[0] - a[1] * b[1], a[0] * b[1] + a[1] * b[0])


def small_turn(angle):
    q = angle * angle
    c = 1.0 + q * (-1 / 2 + q * (1 / 24 + q * (-1 / 720 + q * (1 / 40320))))
    s = angle * (1.0 + q * (-1 / 6 + q * (1 / 120 + q * (-1 / 5040 + q * (1 / 362880)))))
    return c, s


def doubled(turn):
    c, s = turn
    return (c - s) * (c + s), 2.0 * (c * s)


def tree_levels(rows):
    levels = 0
    while 3 ** (levels + 1) * 8 <= rows:
        levels += 1
    return levels


def turn_table(first, unit, rows):
    powers = [unit]
    for _ in range(2):
        powers.append(doubled(powers[-1]))
    step = doubled(powers[-1])
    for level in range(max(1, tree_levels(rows))):
        powers.append(step)
        if level < tree_levels(rows):
            first = cmul(first, step)
        step = cmul(step, doubled(step))
    return [first, *powers]


def turn_count(rows):
    return 4 + max(1, tree_levels(rows))


def both_ways(value, turn):
    cc, ss = value[0] * turn[0], value[1] * turn[1]
    cs, sc = value[0] * turn[1], value[1] * turn[0]
    return (cc - ss, sc + cs), (cc + ss, sc - cs)


def rotations(table, rows):
    base, powers = table[0], table[1:]
    sub = lax.broadcasted_iota(jnp.int32, (8, base[0].shape[-1]), 0)
    value = tuple(jnp.broadcast_to(part, sub.shape) for part in base)
    for k in range(3):
        picked = (sub & (1 << k)) != 0
        value = cmul(value, (jnp.where(picked, powers[k][0], 1.0), jnp.where(picked, powers[k][1], 0.0)))
    blocks = [value]
    last = 0
    for level in range(tree_levels(rows)):
        last = level
        pairs = [both_ways(block, powers[3 + level]) for block in blocks]
        blocks = [pair[1] for pair in pairs] + blocks + [pair[0] for pair in pairs]
    while len(blocks) * 8 < rows:
        blocks.append(cmul(blocks[len(blocks) - 3**last], powers[3 + last]))
    return tuple(jnp.concatenate([block[i] for block in blocks], axis=0)[:rows] for i in (0, 1))


def split(value):
    high = value.astype(jnp.bfloat16)
    return high, (value - high.astype(jnp.float32)).astype(jnp.bfloat16)


def dot_nt(a, b):
    return lax.dot_general(a, b, (((1,), (1,)), ((), ())), preferred_element_type=jnp.float32)


def source_kernel(freqs, depth, wx, half, sizes, zslots, xslots, scale, zbits, closing):
    sx, sy, sz = sizes
    per = 4 // zslots
    main = 4 * xslots * wx

    def body(*refs):
        waves, packed = refs[:2]
        if closing:
            old_even, old_odd = refs[2:4]
            keep, send, xback, xturn, yturn, acc_even, acc_odd = refs[4 + zbits :]
        else:
            e_in, h_in, acc_even, acc_odd, e_near, h_near, xback, xturn, yturn, sems = refs[2:]
            copies = [
                pltpu.make_async_copy(source, target, sems.at[i])
                for i, (source, target) in enumerate(((e_in, e_near), (h_in, h_near)))
            ]
            for copy in copies:
                copy.start()
        ix, iy, iz = (lax.axis_index(name) for name in ("gx", "gy", "gz"))
        xbit, ybit, zbit = bits_of(sx), bits_of(sy), bits_of(zslots)
        starts = []
        for slot in range(xslots):
            code = gray(ix)
            for k in range(1, xbit):
                code = code ^ (((slot >> (xbit - 1 - k)) & 1) << k)
            starts.append((ungray(code, xbit) * wx).astype(jnp.float32))
        zcode = 0
        for k in range(zbit):
            zcode = zcode * 2 + ((gray(iz) >> k) & 1)
        ycode = gray(iy)
        center = (2 * half - 1) / 2.0
        wave, phase = waves[0], waves[1]
        along_x = wave * packed[freqs, 0:1, :]
        along_y = wave * packed[freqs, 1:2, :]
        origin = along_y * center - phase
        unit = doubled(small_turn(0.5 * along_x))
        for xr in range(xslots):
            angle = along_x * starts[xr] + origin
            first = jnp.cos(angle), jnp.sin(angle)
            xback[xr, 0], xback[xr, 1] = cmul(first, (unit[0], -unit[1]))
            for k, turn in enumerate(turn_table(first, unit, wx)):
                xturn[xr, k, 0], xturn[xr, k, 1] = turn
        first = small_turn(0.5 * along_y)
        for k, turn in enumerate(turn_table(first, doubled(first), half)):
            yturn[k, 0], yturn[k, 1] = turn
        if closing:
            acc_even[...] = old_even[...]
            acc_odd[...] = old_odd[...]
        else:
            acc_even[...] = jnp.zeros_like(acc_even)
            acc_odd[...] = jnp.zeros_like(acc_odd)

        def pair(step, carry):
            firsts, seconds, coses, sines = [], [], [], []
            for n in range(2):
                f = 2 * step + n

                def row(ref, *where):
                    return tuple(ref[(*where, i, pl.ds(f, 1), slice(None))] for i in (0, 1))

                cy, sy_ = rotations([row(yturn, k) for k in range(turn_count(half))], half)
                coses.append(cy)
                sines.append(sy_)
                turns = [
                    rotations([row(xturn, xr, k) for k in range(turn_count(wx))], wx)
                    for xr in range(xslots)
                ]
                first, second = [], []
                for zr in range(zslots):
                    for xr in range(xslots):
                        cx, sx_ = turns[xr]
                        for c2 in range(per):
                            at = 2 * ((zcode ^ zr) * per + c2)
                            p = packed[f, pl.ds(at, 1), :]
                            q = packed[f, pl.ds(at + 1, 1), :]
                            first.append(p * cx - q * sx_)
                            second.append(p * sx_ + q * cx)
                p = packed[f, 6:7, :]
                q = packed[f, 7:8, :]
                line = lax.broadcasted_iota(jnp.int32, (16, p.shape[-1]), 0)
                one_first = jnp.zeros(line.shape, jnp.float32)
                one_second = one_first
                for xr in range(xslots):
                    cx, sx_ = row(xback, xr)
                    one_first = jnp.where(line == xr, p * cx - q * sx_, one_first)
                    one_second = jnp.where(line == xr, p * sx_ + q * cx, one_second)
                firsts.append(jnp.concatenate(first + [one_first], axis=0))
                seconds.append(jnp.concatenate(second + [one_second], axis=0))

            def product(lefts, rights):
                lh, ll = split(jnp.concatenate(lefts, axis=1))
                rh, rl = split(jnp.concatenate(rights, axis=1))
                both = dot_nt(jnp.concatenate([lh, ll], axis=0), rh)
                rows = lh.shape[0]
                return both[:rows] + dot_nt(lh, rl) + both[rows:]

            acc_even[...] += product(firsts, coses)
            acc_odd[...] += product(seconds, sines)
            return carry

        lax.fori_loop(0, freqs // 2, pair, 0, unroll=4)
        if not closing:
            for copy in copies:
                copy.wait()
            return

        def slot(tile):
            code = gray(tile) ^ ycode
            place = 0
            for k in range(ybit):
                place = place * 2 + ((code >> k) & 1)
            return place

        def place(zr):
            return (keep, zr) if zr < zslots // 2 else (send, zr - zslots // 2)

        extra = xslots * per * wx
        for zr in range(zslots):
            ref, z = place(zr)
            for y in range(sy):
                ref[z, y, extra : extra + 8] = jnp.zeros((8, LANES), jnp.float32)
        at_z = (1 - (iz & 1)) * (depth - 1)
        for i in range(6):
            row = i * depth
            spot = extra + 4 + i % 4
            send[0, i // 4, spot : spot + 1] = packed[
                freqs + 1 + row // 8, pl.ds(row % 8 + at_z, 1), :
            ]
        turned = 2 // per
        spare = 2 % per
        for j in range(sy // 2):
            lanes = slice(j * LANES, (j + 1) * LANES)
            up = slot(sy // 2 + j)
            down = slot(sy // 2 - 1 - j)
            at = 0
            for zr in range(zslots):
                ref, z = place(zr)
                for xr in range(xslots):
                    for c2 in range(per):
                        rows = slice(at * wx, (at + 1) * wx)
                        even = acc_even[rows, lanes] * scale
                        odd = acc_odd[rows, lanes] * scale
                        into = slice((xr * per + c2) * wx, (xr * per + c2 + 1) * wx)
                        ref[z, up, into] = even - odd
                        ref[z, down, into] = even + odd
                        at += 1
            for xr in range(xslots):
                even = acc_even[main + xr : main + xr + 1, lanes] * scale
                odd = acc_odd[main + xr : main + xr + 1, lanes] * scale
                for zr in range(zslots):
                    ref, z = place(zr)
                    ref[z, up, extra + 2 * xr : extra + 2 * xr + 1] = even - odd
                    ref[z, down, extra + 2 * xr : extra + 2 * xr + 1] = even + odd
                start = (((zcode ^ turned) * xslots + xr) * per + spare) * wx
                rows = pl.ds(pl.multiple_of(start, wx), wx)
                even = (acc_even[rows, lanes] * scale).T
                odd = (acc_odd[rows, lanes] * scale).T
                lower = slot(sy // 2 - j)
                line = slice(extra + 2 * xr + 1, extra + 2 * xr + 2)
                for zr in range(zslots):
                    ref, z = place(zr)
                    ref[z, lower, line, 0:wx] = even[0:1] + odd[0:1]
                if j < sy // 2 - 1:
                    upper = slot(sy // 2 + j + 1)
                    for zr in range(zslots):
                        ref, z = place(zr)
                        ref[z, upper, line, 0:wx] = even[LANES - 1 :] - odd[LANES - 1 :]

    return body


def near_flags(index, bits):
    low, high = [], []
    for k in range(bits):
        upper = (index >> k) & 1
        rest = index & ((1 << k) - 1)
        low.append(((upper == 1) & (rest == 0)).astype(jnp.float32))
        high.append(((upper == 0) & (rest == (1 << k) - 1)).astype(jnp.float32))
    return low, high


def weighted(flags, values):
    total = flags[0] * values[0]
    for flag, value in zip(flags[1:], values[1:]):
        total = total + flag * value
    return total


def pack_kernel(freqs, depth, wx, zbits):
    def body(*refs):
        e_in, h_in, cotangent, cosines, wavenumber, time_phase, message, waves = refs[:8]
        layers = refs[8 : 8 + zbits]
        edge, cos_near, wave_near, phase_near, sems = refs[8 + zbits :]
        upper = lax.axis_index("gx") & 1
        tile = pl.ds(pl.multiple_of((1 - upper) * (wx - 8), 8), 8)
        pairs = [
            (cotangent, message.at[0:freqs]),
            (e_in.at[:, :, tile], edge.at[0:3]),
            (h_in.at[:, :, tile], edge.at[3:6]),
            (cosines, cos_near),
            (wavenumber, wave_near),
            (time_phase, phase_near),
        ]
        for k, layer in enumerate(layers):
            at = (1 - ((lax.axis_index("gz") >> k) & 1)) * (depth - 1)
            pairs += [(e_in.at[:, at], layer.at[0:3]), (h_in.at[:, at], layer.at[3:6])]
        copies = [
            pltpu.make_async_copy(source, target, sems.at[i])
            for i, (source, target) in enumerate(pairs)
        ]
        for copy in copies:
            copy.start()
        for copy in copies:
            copy.wait()
        message[freqs, 0:2] = cos_near[...]
        message[freqs, 2:8] = jnp.zeros((6, LANES), jnp.float32)
        which = lax.broadcasted_iota(jnp.int32, (freqs, LANES), 0)
        for i, near in enumerate((wave_near, phase_near)):
            value = jnp.zeros((freqs, LANES), jnp.float32)
            for f in range(freqs):
                value = jnp.where(which == f, near[f], value)
            waves[i] = value
        at = (1 - upper) * 7
        for i in range(6):
            for z in range(depth):
                row = i * depth + z
                message[freqs + 1 + row // 8, row % 8 : row % 8 + 1] = edge[i, z, pl.ds(at, 1), :]

    return body


def early_rows(message, freqs, depth, i):
    row = i * depth
    return message[freqs + 1 + row // 8, row % 8 : row % 8 + depth]


def column_kernel(freqs, depth, wx, wy, zbits):
    def body(*refs):
        e, h, message = refs[:3]
        zs = refs[3 : 3 + zbits]
        first, last = refs[3 + zbits :]
        low, high = near_flags(lax.axis_index("gz"), zbits)
        lane = lax.broadcasted_iota(jnp.int32, (1, LANES), 1)
        first[...] = jnp.zeros_like(first)
        last[...] = jnp.zeros_like(last)
        for i, field in enumerate((e[0], e[1], e[2], h[0], h[2])):
            turned = field.reshape(depth * wx, wy).T
            first[i : i + 1] = turned[0:1]
            last[i : i + 1] = turned[wy - 1 :]
        for i, layer in (
            (5, weighted(high, [z[1, 0:wx] for z in zs])),
            (6, weighted(low, [z[2, 0:wx] for z in zs])),
        ):
            turned = layer.T
            first[i : i + 1, 0:wx] = turned[0:1]
            last[i : i + 1, 0:wx] = turned[wy - 1 :]
        for ref, y in ((first, 0), (last, wy - 1)):
            corner = jnp.zeros((1, LANES), jnp.float32)
            side_x, side_y = (early_rows(message, freqs, depth, i)[:, y : y + 1] for i in (0, 1))
            for z in range(depth):
                corner = jnp.where(lane == z, side_x[z : z + 1], corner)
                corner = jnp.where(lane == z * wx + wx - 1, side_y[z : z + 1], corner)
            ref[7:8] = corner

    return body


def total_of(terms, rows):
    value = terms[0][rows]
    for term in terms[1:]:
        value = value + term[rows]
    return value


def merge_y_kernel(count, rows, k, ybits):
    def body(*refs):
        terms, (first, last), outs = refs[:count], refs[count : count + 2], refs[count + 2 :]
        iy = lax.axis_index("gy")
        size = rows // len(outs)
        swaps = (None, k) if len(outs) == 2 else (None, k + 1, k, None)
        for i, (out, swap) in enumerate(zip(outs, swaps)):
            out[0:size] = total_of(terms, slice(i * size, (i + 1) * size))
            if swap is not None:
                upper = ((iy >> swap) & 1).astype(jnp.float32)
                out[size : size + 8] = upper * first[...] + (1.0 - upper) * last[...]

    return body


def halo_at(ref):
    rows = ref.shape[0]
    return ref[rows - 8 : rows]


def merge_x_kernel(count, rows, depth, wx, zbits, ybits, slots, k):
    def body(*refs):
        terms = refs[:count]
        e, h = refs[count : count + 2]
        zs = refs[count + 2 : count + 2 + zbits]
        ys = refs[count + 2 + zbits : count + 2 + zbits + ybits]
        keep, out = refs[count + 3 + zbits + ybits :]
        half = (rows - 8) // 2
        size = half + 8
        keep[0:half] = total_of(terms, slice(0, half))
        out[0:half] = total_of(terms, slice(half, rows - 8))
        extra = total_of(terms, slice(rows - 8, rows))
        keep[half:size] = extra
        out[half:size] = pltpu.roll(extra, 8 - slots, 0)
        zlow, zhigh = near_flags(lax.axis_index("gz"), zbits)
        ylow, yhigh = near_flags(lax.axis_index("gy"), ybits)
        at = (1 - ((lax.axis_index("gx") >> k) & 1)) * (wx - 1)
        for i in range(3):
            for z in range(depth):
                row = size + i * depth + z
                out[row : row + 1] = e[i, z, pl.ds(at, 1), :]
                if i > 0:
                    row = size + (2 + i) * depth + z
                    out[row : row + 1] = h[i, z, pl.ds(at, 1), :]
        base = size + 5 * depth
        halos = [halo_at(y) for y in ys]
        out[base : base + 1] = weighted(zhigh, [z[0, pl.ds(at, 1), :] for z in zs])
        out[base + 1 : base + 2] = weighted(zlow, [z[2, pl.ds(at, 1), :] for z in zs])
        out[base + 2 : base + 3] = weighted(yhigh, [y[0:1] for y in halos])
        out[base + 3 : base + 4] = weighted(ylow, [y[1:2] for y in halos])

    return body


def pole_kernel(depth, wx, wy):
    def body(table_in, e, pole_in, material_in, after, pole_out, base, coef_out, *scratch):
        table, pole, material, new_pole, sems = scratch
        copies = [
            pltpu.make_async_copy(source, target, sems.at[i])
            for i, (source, target) in enumerate(
                ((table_in, table), (material_in, material), (pole_in, pole))
            )
        ]
        for copy in copies:
            copy.start()
        for copy in copies:
            copy.wait()
        kind = material[...]

        def chosen(i):
            value = jnp.full(kind.shape, table[i, NPOLE - 1], jnp.float32)
            for m in range(NPOLE - 1):
                value = jnp.where(kind == m, table[i, m], value)
            return value

        decay, drive, coef = (chosen(i) for i in range(3))
        coef_out[...] = coef
        for i in range(3):
            old = pole[i]
            electric = e[i]
            new = decay * old + drive * electric
            new_pole[i] = new
            base[i] = electric - coef * (0.5 * (new + old))
        copy = pltpu.make_async_copy(new_pole, pole_out, sems.at[0])
        copy.start()
        copy.wait()

    return body


def field_kernel(freqs, depth, wx, wy, xbits, ybits, zbits, side_rows):
    def body(*refs):
        e, h, base_e, coef_ref, first, message = refs[:6]
        zs = refs[6 : 6 + zbits]
        ys = refs[6 + zbits : 6 + zbits + ybits]
        xs = [x[x.shape[0] - 5 * depth - 4 :] for x in refs[6 + zbits + ybits : 5 + zbits + ybits + xbits]]
        sides = refs[5 + zbits + ybits + xbits : 5 + 2 * zbits + ybits + xbits]
        e_out, h_out = refs[5 + 2 * zbits + ybits + xbits :]
        ix, iy, iz = (lax.axis_index(name) for name in ("gx", "gy", "gz"))
        xlow, xhigh = near_flags(ix, xbits)
        ylow, yhigh = near_flags(iy, ybits)
        zlow, zhigh = near_flags(iz, zbits)
        size = depth * wx
        base = 5 * depth
        lane = lax.broadcasted_iota(jnp.int32, (size, wy), 1)
        line = lax.broadcasted_iota(jnp.int32, (size, wy), 0) & (wx - 1)
        inside_x, inside_y, inside_z = (
            (index > 0).astype(jnp.float32) for index in (ix, iy, iz)
        )

        def flat(ref, i):
            return ref[i].reshape(size, wy)

        ex, ey, ez = (flat(e, i) for i in range(3))
        oldx, oldy, oldz = (flat(h, i) for i in range(3))

        def spread(rows):
            return jnp.broadcast_to(rows[:, None, :], (depth, wx, wy)).reshape(size, wy)

        def next_y(value, column):
            rows = value.shape[0]
            return jnp.where(lane[:rows] == wy - 1, column, pltpu.roll(value, wy - 1, 1))

        def next_x(value, rows):
            return jnp.where(line == wx - 1, spread(rows), pltpu.roll(value, size - 1, 0))

        def next_z(value, layer):
            return jnp.concatenate([value[wx:], layer], axis=0)

        def last_y(value, column):
            return jnp.where(lane == 0, column, pltpu.roll(value, 1, 1))

        def last_x(value, rows):
            return jnp.where(line == 0, spread(rows), pltpu.roll(value, 1, 0))

        def last_z(value, layer):
            return jnp.concatenate([layer, value[:-wx]], axis=0)

        ylo = weighted(ylow, [halo_at(y) for y in ys])
        yhi = weighted(yhigh, [halo_at(y) for y in ys])
        above = yhi.T

        def rows_of(flags, i):
            line = i if i < 3 else i - 1
            at = slice(line * depth, (line + 1) * depth)
            return weighted(flags, [early_rows(message, freqs, depth, i)] + [x[at] for x in xs])

        def extra_of(flags, early, i):
            return weighted(flags, [early] + [x[base + i : base + i + 1] for x in xs])

        def layer_of(flags, i):
            return weighted(flags, [z[i, 0:wx] for z in zs])

        def side_of(flags, i):
            ats = [rows[i] for rows in side_rows]
            return weighted(flags, [side[at : at + 1] for at, side in zip(ats, sides)])

        up_x, up_y = layer_of(zhigh, 0), layer_of(zhigh, 1)
        hx = oldx - courant * ((next_y(ez, above[:, 2:3]) - ez) - (next_z(ey, up_y) - ey))
        hy = oldy - courant * (
            (next_z(ex, up_x) - ex) - (next_x(ez, rows_of(xhigh, 2)) - ez)
        )
        hz = oldz - courant * (
            (next_x(ey, rows_of(xhigh, 1)) - ey) - (next_y(ex, above[:, 0:1]) - ex)
        )
        mx, my, mz = (rows_of(xlow, i) for i in range(3))
        up = jnp.concatenate([mx[1:], extra_of(xlow, side_of(zhigh, 0), 0)], axis=0)
        low_hy = rows_of(xlow, 4) - courant * ((up - mx) - (e[2, :, 0, :] - mz))
        corner = xlow[0] * above[0:depth, 7:8]
        for flag, x in zip(xlow[1:], xs):
            tail = x[base : base + 8].T
            picks = [tail[z * wx + wx - 1 : (z + 1) * wx, 2:3] for z in range(depth)]
            corner = corner + flag * jnp.concatenate(picks, axis=0)
        low_hz = rows_of(xlow, 5) - courant * (
            (e[1, :, 0, :] - my) - (next_y(mx, corner) - mx)
        )
        strip = lax.broadcasted_iota(jnp.int32, (1, LANES), 1)
        lx, ly, lz = ylo[0:1], ylo[1:2], ylo[2:3]
        up = jnp.where(
            strip >= size - wx, pltpu.roll(ylo[5:6], size - wx, 1), pltpu.roll(ly, LANES - wx, 1)
        )
        side_hx = ylo[3:4] - courant * ((first[2:3] - lz) - (up - ly))
        corner = xhigh[0] * ylo[7:8]
        for flag, x in zip(xhigh[1:], xs):
            corner = corner + flag * pltpu.roll(x[base + 3 : base + 4], wx - 1, 1)
        right = jnp.where((strip & (wx - 1)) == wx - 1, corner, pltpu.roll(ly, LANES - 1, 1))
        side_hz = ylo[4:5] - courant * ((right - ly) - (first[0:1] - lx))
        both = jnp.concatenate([side_hx, side_hz, jnp.zeros((6, LANES), jnp.float32)], axis=0)
        both = (inside_y * both).T
        bx, by, bz = (layer_of(zlow, i) for i in range(3))
        under_hx = layer_of(zlow, 3) - courant * (
            (next_y(bz, above[0:wx, 6:7]) - bz) - (ey[:wx] - by)
        )
        right = jnp.concatenate([bz[1:], extra_of(xhigh, side_of(zlow, 2), 1)], axis=0)
        under_hy = layer_of(zlow, 4) - courant * ((ex[:wx] - bx) - (right - bz))
        under_hx = inside_z * under_hx
        under_hy = inside_z * under_hy
        low_hy = inside_x * low_hy
        low_hz = inside_x * low_hz
        curl = (
            (hz - last_y(hz, both[:, 1:2])) - (hy - last_z(hy, under_hy)),
            (hx - last_z(hx, under_hx)) - (hz - last_x(hz, low_hz)),
            (hy - last_x(hy, low_hy)) - (hx - last_y(hx, both[:, 0:1])),
        )
        coef = coef_ref[...].reshape(size, wy)
        shape = (depth, wx, wy)
        for i, magnetic in enumerate((hx, hy, hz)):
            value = flat(base_e, i) + coef * curl[i]
            h_out[i] = magnetic.reshape(shape)
            e_out[i] = value.reshape(shape)

    return body


def inject_kernel(depth, wx, wy, sy, sz, per, zcut):
    def body(*refs):
        blocks = refs[: 1 << zcut]
        e_near, h_near, coef_ref, e_out, h_out, e_new, h_new, sems = refs[1 << zcut :]
        last = depth - 1
        others = slice(0, last)
        copies = [
            pltpu.make_async_copy(e_near.at[:, others], e_out.at[:, others], sems.at[0]),
            pltpu.make_async_copy(h_near.at[:, others], h_out.at[:, others], sems.at[1]),
            pltpu.make_async_copy(h_near.at[2, last], h_out.at[2, last], sems.at[2]),
        ]
        for copy in copies:
            copy.start()
        h_copy = pltpu.make_async_copy(h_new, h_out.at[0:2, last], sems.at[3])
        e_copy = pltpu.make_async_copy(e_new, e_out.at[:, last], sems.at[4])
        ix, iy, iz = (lax.axis_index(name) for name in ("gx", "gy", "gz"))

        @pl.when(iz == sz - 1)
        def _():
            inside_x, inside_y = ((index > 0).astype(jnp.float32) for index in (ix, iy))
            lane = lax.broadcasted_iota(jnp.int32, (wx, wy), 1)
            line = lax.broadcasted_iota(jnp.int32, (wx, wy), 0)
            flip = (
                lax.broadcasted_iota(jnp.int32, (wy, wy), 0)
                + lax.broadcasted_iota(jnp.int32, (wy, wy), 1)
                == wy - 1
            ).astype(jnp.float32)
            flipped = iy < sy // 2

            def straight(value):
                turned = jnp.dot(
                    value, flip, precision=lax.Precision.HIGHEST, preferred_element_type=jnp.float32
                )
                return jnp.where(flipped, turned, value)

            tiles = [straight(ref[...]) for ref in blocks]

            def channel(c):
                start = (c % per) * wx
                return tiles[c // per][start : start + wx]

            electric_x, electric_y, magnetic_x, magnetic_y = (channel(c) for c in range(4))
            before = inside_x * tiles[3 // per][per * wx : per * wx + 1]
            beside = inside_y * blocks[2 // per][per * wx : per * wx + 8].T[0:wx, 1:2]
            last_x = jnp.where(line == 0, before, pltpu.roll(magnetic_y, 1, 0))
            last_y = jnp.where(lane == 0, beside, pltpu.roll(magnetic_x, 1, 1))
            coef = coef_ref[last]
            h_new[0] = h_near[0, last] - courant * magnetic_x
            h_new[1] = h_near[1, last] - courant * magnetic_y
            e_new[0] = e_near[0, last] + coef * (courant * magnetic_y - electric_x)
            e_new[1] = e_near[1, last] - coef * (courant * magnetic_x + electric_y)
            e_new[2] = e_near[2, last] + coef * courant * (
                (magnetic_x - last_y) - (magnetic_y - last_x)
            )

        @pl.when(iz != sz - 1)
        def _():
            for i in range(3):
                e_new[i] = e_near[i, last]
            for i in range(2):
                h_new[i] = h_near[i, last]

        h_copy.start()
        e_copy.start()
        for copy in (*copies, h_copy, e_copy):
            copy.wait()

    return body


def in_hbm(*arrays):
    return [pltpu.with_memory_space_constraint(array, pltpu.HBM) for array in arrays]


def in_vmem(*arrays):
    return [pltpu.with_memory_space_constraint(array, pltpu.VMEM) for array in arrays]


def local(
    e_field, h_field, pole_current, material, pole_table, cotangent, cosines, wavenumber, time_phase
):
    depth, wx, wy = material.shape
    sizes = sx, sy, sz = tuple(lax.axis_size(name) for name in ("gx", "gy", "gz"))
    ix, iy, iz = (lax.axis_index(name) for name in ("gx", "gy", "gz"))
    freqs, _, count = cotangent.shape
    scale = 1.0 / math.sqrt(freqs * count * sx * sy * sz)
    assert wy == LANES and depth * wx == LANES and 1 < sx <= 4 and sy > 1 and sz > 1
    pad = -count % LANES
    if pad:
        cotangent = jnp.pad(cotangent, ((0, 0), (0, 0), (0, pad)))
        cosines = jnp.pad(cosines, ((0, 0), (0, pad)))
    f32 = jnp.float32
    smem = pl.BlockSpec(memory_space=pltpu.SMEM)
    vmem = pl.BlockSpec(memory_space=pltpu.VMEM)
    hbm = pl.BlockSpec(memory_space=pltpu.HBM)
    small = pltpu.CompilerParams(vmem_limit_bytes=8 << 20)
    xslots = sx // 2
    zslots = min(sz, 4)
    per = 4 // zslots
    xbits, ybits, zbits = bits_of(sx), bits_of(sy), bits_of(sz)
    zcut = bits_of(zslots)

    assert 8 % depth == 0
    mine, waves, *layers = pl.pallas_call(
        pack_kernel(freqs, depth, wx, zbits),
        out_shape=[
            pltpu.VMEM((freqs + 1 + 6 * depth // 8, 8, LANES), f32),
            pltpu.VMEM((2, freqs, LANES), f32),
        ]
        + [pltpu.VMEM((6, wx, wy), f32)] * zbits,
        in_specs=[hbm] * 6,
        out_specs=[vmem] * (2 + zbits),
        scratch_shapes=[
            pltpu.VMEM((6, depth, 8, LANES), f32),
            pltpu.VMEM((2, LANES), f32),
            pltpu.SMEM((freqs,), f32),
            pltpu.SMEM((freqs,), f32),
            pltpu.SemaphoreType.DMA((6 + 2 * zbits,)),
        ],
        compiler_params=small,
        name="pack",
    )(*in_hbm(e_field, h_field, cotangent, cosines, wavenumber, time_phase))
    theirs = exchange(mine, "gx", 1)
    zs = [exchange(layers[k], "gz", (2 << k) - 1) for k in range(zbits)]
    zs = in_vmem(*zs)

    half = sy * wy // 2
    width = count + pad
    block = xslots * per * wx + 8
    part_shape = pltpu.VMEM((zslots // 2, sy, block, wy), f32)
    assert freqs % 2 == 0
    sums = pltpu.VMEM((4 * xslots * wx + 16, half), f32)
    tables = [
        pltpu.VMEM((xslots, 2, freqs, width), f32),
        pltpu.VMEM((xslots, turn_count(wx), 2, freqs, width), f32),
        pltpu.VMEM((turn_count(half), 2, freqs, width), f32),
    ]
    medium = pltpu.CompilerParams(vmem_limit_bytes=24 << 20)
    waves, mine = in_vmem(waves, mine)
    *own, e_near, h_near = pl.pallas_call(
        source_kernel(freqs, depth, wx, half, sizes, zslots, xslots, scale, zbits, False),
        out_shape=(sums, sums, pltpu.VMEM(e_field.shape, f32), pltpu.VMEM(h_field.shape, f32)),
        in_specs=[vmem, vmem, hbm, hbm],
        out_specs=(vmem,) * 4,
        scratch_shapes=tables + [pltpu.SemaphoreType.DMA((2,))],
        compiler_params=medium,
        name="source_own",
    )(waves, mine, *in_hbm(e_field, h_field))
    e_near, h_near = in_vmem(e_near, h_near)
    with jax.named_scope("source_all"):
        keep, send = pl.pallas_call(
            source_kernel(freqs, depth, wx, half, sizes, zslots, xslots, scale, zbits, True),
            out_shape=(part_shape, part_shape),
            in_specs=[vmem] * (4 + zbits),
            out_specs=(vmem, vmem),
            scratch_shapes=tables + [sums, sums],
            compiler_params=medium,
            name="source_both",
        )(waves, *in_vmem(theirs, *own), *zs)

    strip = pltpu.VMEM((8, LANES), f32)
    first, last = pl.pallas_call(
        column_kernel(freqs, depth, wx, wy, zbits),
        out_shape=(strip, strip),
        in_specs=[vmem] * (3 + zbits),
        out_specs=(vmem, vmem),
        compiler_params=small,
        name="columns",
    )(e_near, h_near, *in_vmem(theirs), *zs)

    whole = jax.ShapeDtypeStruct((3, depth, wx, wy), f32)
    pole_next, base_e, coef = pl.pallas_call(
        pole_kernel(depth, wx, wy),
        out_shape=(whole, pltpu.VMEM(whole.shape, f32), pltpu.VMEM((depth, wx, wy), f32)),
        in_specs=[hbm, vmem, hbm, hbm, vmem],
        out_specs=(hbm, vmem, vmem),
        scratch_shapes=[
            pltpu.SMEM(pole_table.shape, f32),
            pltpu.VMEM(whole.shape, f32),
            pltpu.VMEM((depth, wx, wy), jnp.int32),
            pltpu.VMEM(whole.shape, f32),
            pltpu.SemaphoreType.DMA((3,)),
        ],
        compiler_params=small,
        name="pole",
    )(*in_hbm(pole_table), e_near, *in_hbm(pole_current, material), *in_vmem(first))
    base_e, coef = in_vmem(base_e, coef)

    def flat(value):
        return value.reshape(-1, LANES)

    terms = [keep, exchange(send, "gz", 1)]
    sides = [flat(terms[1])]
    side_rows = [[(i // 4) * block + block - 4 + i % 4 for i in range(6)]]
    for k in range(1, zbits):
        at = (1 - ((iz >> k) & 1)) * (depth - 1)
        rows = theirs[freqs + 1 :].reshape(6, depth, LANES)
        rows = lax.dynamic_index_in_dim(rows, at, 1, keepdims=False)
        sides.append(exchange(jnp.pad(rows, ((0, 2), (0, 0))), "gz", (2 << k) - 1))
        side_rows.append(list(range(6)))
    for k in range(1, zbits):
        part = terms[0] + terms[1]
        mask = (2 << k) - 1
        if k < zcut:
            middle = part.shape[0] // 2
            terms = [part[:middle], exchange(part[middle:], "gz", mask)]
        else:
            terms = [part, exchange(part, "gz", mask)]
    terms = [flat(term) for term in terms]
    rows = sy * block

    ys = [None] * ybits
    k = 0
    while k < ybits:
        both = k + 1 < ybits
        size = rows // 4 if both else rows // 2
        plain, laden = pltpu.VMEM((size, LANES), f32), pltpu.VMEM((size + 8, LANES), f32)
        shapes = (plain, laden, laden, plain) if both else (plain, laden)
        keep, *away = pl.pallas_call(
            merge_y_kernel(len(terms), rows, k, ybits),
            out_shape=shapes,
            in_specs=[vmem] * (len(terms) + 2),
            out_specs=(vmem,) * len(shapes),
            compiler_params=small,
            name="merge_y",
        )(*in_vmem(*terms, first, last))
        if both:
            ys[k] = exchange(away[1], "gy", (2 << k) - 1)
            other = exchange(away[2], "gy", 2 << k)
            ys[k + 1] = exchange(away[0], "gy", (4 << k) - 1)
            terms = [keep, ys[k], ys[k + 1], other]
            k += 2
        else:
            ys[k] = exchange(away[0], "gy", (2 << k) - 1)
            terms = [keep, ys[k]]
            k += 1
        rows = size
    near = [*zs, *in_vmem(*ys)]
    xs = []
    slots = xslots
    for k in range(1, xbits):
        size = (rows - 8) // 2 + 8
        keep, away = pl.pallas_call(
            merge_x_kernel(len(terms), rows, depth, wx, zbits, ybits, slots, k),
            out_shape=(
                pltpu.VMEM((size, LANES), f32),
                pltpu.VMEM((size + 5 * depth + 4, LANES), f32),
            ),
            in_specs=[vmem] * (len(terms) + 3 + zbits + ybits),
            out_specs=(vmem, vmem),
            compiler_params=small,
            name="merge_x",
        )(*in_vmem(*terms), e_near, h_near, *near, coef)
        xs.append(exchange(away, "gx", (2 << k) - 1))
        rows = size
        slots //= 2
        terms = [keep, xs[-1]]
    part = sum(term[:rows] for term in terms)

    e_most, h_most = pl.pallas_call(
        field_kernel(freqs, depth, wx, wy, xbits, ybits, zbits, side_rows),
        out_shape=(pltpu.VMEM(whole.shape, f32), pltpu.VMEM(whole.shape, f32)),
        in_specs=[vmem] * (5 + xbits + ybits + 2 * zbits),
        out_specs=(vmem,) * 2,
        compiler_params=pltpu.CompilerParams(vmem_limit_bytes=16 << 20),
        name="fields",
    )(e_near, h_near, base_e, coef, *in_vmem(first, theirs), *near, *in_vmem(*xs, *sides))

    top = gray(sz - 1)
    blocks = [part]
    for k in reversed(range(zcut)):
        others = [exchange(value, "gz", (2 << k) - 1) for value in blocks]
        blocks = others + blocks if (top >> k) & 1 else blocks + others
    e_next, h_next = pl.pallas_call(
        inject_kernel(depth, wx, wy, sy, sz, per, zcut),
        out_shape=(whole, whole),
        in_specs=[vmem] * (len(blocks) + 3),
        out_specs=(hbm, hbm),
        scratch_shapes=[
            pltpu.VMEM((3, wx, wy), f32),
            pltpu.VMEM((2, wx, wy), f32),
            pltpu.SemaphoreType.DMA((5,)),
        ],
        compiler_params=small,
        name="inject",
    )(*in_vmem(*blocks, e_most, h_most), coef)
    return (e_next, h_next, pole_next)


def solution(mesh):
    in_specs = (
        P(None, "gz", "gx", "gy"),
        P(None, "gz", "gx", "gy"),
        P(None, "gz", "gx", "gy"),
        P("gz", "gx", "gy"),
        P(),
        P(None, None, ("gx", "gy", "gz")),
        P(None, ("gx", "gy", "gz")),
        P(),
        P(),
    )
    out_specs = (P(None, "gz", "gx", "gy"), P(None, "gz", "gx", "gy"), P(None, "gz", "gx", "gy"))
    return jax.shard_map(local, mesh=mesh, in_specs=in_specs, out_specs=out_specs, check_vma=False)
```

```python
import math

import jax
import jax.numpy as jnp
from jax import lax
from jax.experimental import pallas as pl
from jax.experimental.pallas import tpu as pltpu
from jax.sharding import PartitionSpec as P


NPOLE = 4
LANES = 128


courant = 0.5


def exchange(array, axis, mask):
    return lax.ppermute(array, axis, [(i, i ^ mask) for i in range(lax.axis_size(axis))])


def gray(index):
    return index ^ (index >> 1)


def ungray(code, bits):
    index = code
    for step in range(1, bits):
        index = index ^ (code >> step)
    return index


def bits_of(size):
    return size.bit_length() - 1


def cmul(a, b):
    return (a[0] * b[0] - a[1] * b[1], a[0] * b[1] + a[1] * b[0])


def small_turn(angle):
    q = angle * angle
    c = 1.0 + q * (-1 / 2 + q * (1 / 24 + q * (-1 / 720 + q * (1 / 40320))))
    s = angle * (1.0 + q * (-1 / 6 + q * (1 / 120 + q * (-1 / 5040 + q * (1 / 362880)))))
    return c, s


def doubled(turn):
    c, s = turn
    return (c - s) * (c + s), 2.0 * (c * s)


def tree_levels(rows):
    levels = 0
    while 3 ** (levels + 1) * 8 <= rows:
        levels += 1
    return levels


def turn_table(first, unit, rows):
    powers = [unit]
    for _ in range(2):
        powers.append(doubled(powers[-1]))
    step = doubled(powers[-1])
    for level in range(max(1, tree_levels(rows))):
        powers.append(step)
        if level < tree_levels(rows):
            first = cmul(first, step)
        step = cmul(step, doubled(step))
    return [first, *powers]


def turn_count(rows):
    return 4 + max(1, tree_levels(rows))


def both_ways(value, turn):
    cc, ss = value[0] * turn[0], value[1] * turn[1]
    cs, sc = value[0] * turn[1], value[1] * turn[0]
    return (cc - ss, sc + cs), (cc + ss, sc - cs)


def rotations(table, rows):
    base, powers = table[0], table[1:]
    sub = lax.broadcasted_iota(jnp.int32, (8, base[0].shape[-1]), 0)
    value = tuple(jnp.broadcast_to(part, sub.shape) for part in base)
    for k in range(3):
        picked = (sub & (1 << k)) != 0
        value = cmul(value, (jnp.where(picked, powers[k][0], 1.0), jnp.where(picked, powers[k][1], 0.0)))
    blocks = [value]
    last = 0
    for level in range(tree_levels(rows)):
        last = level
        pairs = [both_ways(block, powers[3 + level]) for block in blocks]
        blocks = [pair[1] for pair in pairs] + blocks + [pair[0] for pair in pairs]
    while len(blocks) * 8 < rows:
        blocks.append(cmul(blocks[len(blocks) - 3**last], powers[3 + last]))
    return tuple(jnp.concatenate([block[i] for block in blocks], axis=0)[:rows] for i in (0, 1))


def split(value):
    high = value.astype(jnp.bfloat16)
    return high, (value - high.astype(jnp.float32)).astype(jnp.bfloat16)


def dot_nt(a, b):
    return lax.dot_general(a, b, (((1,), (1,)), ((), ())), preferred_element_type=jnp.float32)


def source_kernel(freqs, depth, wx, half, sizes, zslots, xslots, scale, zbits, closing):
    sx, sy, _ = sizes
    per = 4 // zslots
    main = 4 * xslots * wx

    def body(*refs):
        waves, packed = refs[:2]
        if closing:
            old_even, old_odd = refs[2:4]
            keep, send, xback, xturn, yturn, acc_even, acc_odd = refs[4 + zbits :]
        else:
            e_in, h_in, acc_even, acc_odd, e_near, h_near, xback, xturn, yturn, sems = refs[2:]
            copies = [
                pltpu.make_async_copy(source, target, sems.at[i])
                for i, (source, target) in enumerate(((e_in, e_near), (h_in, h_near)))
            ]
            for copy in copies:
                copy.start()
        ix, iy, iz = (lax.axis_index(name) for name in ("gx", "gy", "gz"))
        xbit, ybit, zbit = bits_of(sx), bits_of(sy), bits_of(zslots)
        starts = []
        for slot in range(xslots):
            code = gray(ix)
            for k in range(1, xbit):
                code = code ^ (((slot >> (xbit - 1 - k)) & 1) << k)
            starts.append((ungray(code, xbit) * wx).astype(jnp.float32))
        zcode = 0
        for k in range(zbit):
            zcode = zcode * 2 + ((gray(iz) >> k) & 1)
        ycode = gray(iy)
        center = (2 * half - 1) / 2.0
        wave, phase = waves[0], waves[1]
        along_x = wave * packed[freqs, 0:1, :]
        along_y = wave * packed[freqs, 1:2, :]
        origin = along_y * center - phase
        unit = doubled(small_turn(0.5 * along_x))
        for xr in range(xslots):
            angle = along_x * starts[xr] + origin
            first = jnp.cos(angle), jnp.sin(angle)
            xback[xr, 0], xback[xr, 1] = cmul(first, (unit[0], -unit[1]))
            for k, turn in enumerate(turn_table(first, unit, wx)):
                xturn[xr, k, 0], xturn[xr, k, 1] = turn
        first = small_turn(0.5 * along_y)
        for k, turn in enumerate(turn_table(first, doubled(first), half)):
            yturn[k, 0], yturn[k, 1] = turn
        if closing:
            acc_even[...] = old_even[...]
            acc_odd[...] = old_odd[...]
        else:
            acc_even[...] = jnp.zeros_like(acc_even)
            acc_odd[...] = jnp.zeros_like(acc_odd)

        def pair(step, carry):
            firsts, seconds, coses, sines = [], [], [], []
            for n in range(2):
                f = 2 * step + n

                def row(ref, *where):
                    return tuple(ref[(*where, i, pl.ds(f, 1), slice(None))] for i in (0, 1))

                cy, sy_ = rotations([row(yturn, k) for k in range(turn_count(half))], half)
                coses.append(cy)
                sines.append(sy_)
                turns = [
                    rotations([row(xturn, xr, k) for k in range(turn_count(wx))], wx)
                    for xr in range(xslots)
                ]
                first, second = [], []
                for zr in range(zslots):
                    for xr in range(xslots):
                        cx, sx_ = turns[xr]
                        for c2 in range(per):
                            at = 2 * ((zcode ^ zr) * per + c2)
                            p = packed[f, pl.ds(at, 1), :]
                            q = packed[f, pl.ds(at + 1, 1), :]
                            first.append(p * cx - q * sx_)
                            second.append(p * sx_ + q * cx)
                p = packed[f, 6:7, :]
                q = packed[f, 7:8, :]
                line = lax.broadcasted_iota(jnp.int32, (16, p.shape[-1]), 0)
                one_first = jnp.zeros(line.shape, jnp.float32)
                one_second = one_first
                for xr in range(xslots):
                    cx, sx_ = row(xback, xr)
                    one_first = jnp.where(line == xr, p * cx - q * sx_, one_first)
                    one_second = jnp.where(line == xr, p * sx_ + q * cx, one_second)
                firsts.append(jnp.concatenate(first + [one_first], axis=0))
                seconds.append(jnp.concatenate(second + [one_second], axis=0))

            def product(lefts, rights):
                lh, ll = split(jnp.concatenate(lefts, axis=1))
                rh, rl = split(jnp.concatenate(rights, axis=1))
                both = dot_nt(jnp.concatenate([lh, ll], axis=0), rh)
                rows = lh.shape[0]
                return both[:rows] + dot_nt(lh, rl) + both[rows:]

            acc_even[...] += product(firsts, coses)
            acc_odd[...] += product(seconds, sines)
            return carry

        lax.fori_loop(0, freqs // 2, pair, 0, unroll=4)
        if not closing:
            for copy in copies:
                copy.wait()
            return

        def slot(tile):
            code = gray(tile) ^ ycode
            place = 0
            for k in range(ybit):
                place = place * 2 + ((code >> k) & 1)
            return place

        def place(zr):
            return (keep, zr) if zr < zslots // 2 else (send, zr - zslots // 2)

        extra = xslots * per * wx
        for zr in range(zslots):
            ref, z = place(zr)
            for y in range(sy):
                ref[z, y, extra : extra + 8] = jnp.zeros((8, LANES), jnp.float32)
        at_z = (1 - (iz & 1)) * (depth - 1)
        for i in range(6):
            row = i * depth
            spot = extra + 4 + i % 4
            send[0, i // 4, spot : spot + 1] = packed[
                freqs + 1 + row // 8, pl.ds(row % 8 + at_z, 1), :
            ]
        turned = 2 // per
        spare = 2 % per
        for j in range(sy // 2):
            lanes = slice(j * LANES, (j + 1) * LANES)
            up = slot(sy // 2 + j)
            down = slot(sy // 2 - 1 - j)
            at = 0
            for zr in range(zslots):
                ref, z = place(zr)
                for xr in range(xslots):
                    for c2 in range(per):
                        rows = slice(at * wx, (at + 1) * wx)
                        even = acc_even[rows, lanes] * scale
                        odd = acc_odd[rows, lanes] * scale
                        into = slice((xr * per + c2) * wx, (xr * per + c2 + 1) * wx)
                        ref[z, up, into] = even - odd
                        ref[z, down, into] = even + odd
                        at += 1
            for xr in range(xslots):
                even = acc_even[main + xr : main + xr + 1, lanes] * scale
                odd = acc_odd[main + xr : main + xr + 1, lanes] * scale
                for zr in range(zslots):
                    ref, z = place(zr)
                    ref[z, up, extra + 2 * xr : extra + 2 * xr + 1] = even - odd
                    ref[z, down, extra + 2 * xr : extra + 2 * xr + 1] = even + odd
                start = (((zcode ^ turned) * xslots + xr) * per + spare) * wx
                rows = pl.ds(pl.multiple_of(start, wx), wx)
                even = (acc_even[rows, lanes] * scale).T
                odd = (acc_odd[rows, lanes] * scale).T
                lower = slot(sy // 2 - j)
                line = slice(extra + 2 * xr + 1, extra + 2 * xr + 2)
                for zr in range(zslots):
                    ref, z = place(zr)
                    ref[z, lower, line, 0:wx] = even[0:1] + odd[0:1]
                if j < sy // 2 - 1:
                    upper = slot(sy // 2 + j + 1)
                    for zr in range(zslots):
                        ref, z = place(zr)
                        ref[z, upper, line, 0:wx] = even[LANES - 1 :] - odd[LANES - 1 :]

    return body


def near_flags(index, bits):
    low, high = [], []
    for k in range(bits):
        upper = (index >> k) & 1
        rest = index & ((1 << k) - 1)
        low.append(((upper == 1) & (rest == 0)).astype(jnp.float32))
        high.append(((upper == 0) & (rest == (1 << k) - 1)).astype(jnp.float32))
    return low, high


def weighted(flags, values):
    total = flags[0] * values[0]
    for flag, value in zip(flags[1:], values[1:]):
        total = total + flag * value
    return total


def pack_kernel(freqs, depth, wx, zbits):
    def body(*refs):
        e_in, h_in, cotangent, cosines, wavenumber, time_phase, message, waves = refs[:8]
        layers = refs[8 : 8 + zbits]
        edge, cos_near, wave_near, phase_near, sems = refs[8 + zbits :]
        upper = lax.axis_index("gx") & 1
        tile = pl.ds(pl.multiple_of((1 - upper) * (wx - 8), 8), 8)
        pairs = [
            (cotangent, message.at[0:freqs]),
            (e_in.at[:, :, tile], edge.at[0:3]),
            (h_in.at[:, :, tile], edge.at[3:6]),
            (cosines, cos_near),
            (wavenumber, wave_near),
            (time_phase, phase_near),
        ]
        for k, layer in enumerate(layers):
            at = (1 - ((lax.axis_index("gz") >> k) & 1)) * (depth - 1)
            pairs += [(e_in.at[:, at], layer.at[0:3]), (h_in.at[:, at], layer.at[3:6])]
        copies = [
            pltpu.make_async_copy(source, target, sems.at[i])
            for i, (source, target) in enumerate(pairs)
        ]
        for copy in copies:
            copy.start()
        for copy in copies:
            copy.wait()
        message[freqs, 0:2] = cos_near[...]
        message[freqs, 2:8] = jnp.zeros((6, LANES), jnp.float32)
        which = lax.broadcasted_iota(jnp.int32, (freqs, LANES), 0)
        for i, near in enumerate((wave_near, phase_near)):
            value = jnp.zeros((freqs, LANES), jnp.float32)
            for f in range(freqs):
                value = jnp.where(which == f, near[f], value)
            waves[i] = value
        at = (1 - upper) * 7
        for i in range(6):
            for z in range(depth):
                row = i * depth + z
                message[freqs + 1 + row // 8, row % 8 : row % 8 + 1] = edge[i, z, pl.ds(at, 1), :]

    return body


def early_rows(message, freqs, depth, i):
    row = i * depth
    return message[freqs + 1 + row // 8, row % 8 : row % 8 + depth]


def column_kernel(freqs, depth, wx, wy, zbits):
    def body(*refs):
        e, h, message = refs[:3]
        zs = refs[3 : 3 + zbits]
        first, last = refs[3 + zbits :]
        low, high = near_flags(lax.axis_index("gz"), zbits)
        lane = lax.broadcasted_iota(jnp.int32, (1, LANES), 1)
        first[...] = jnp.zeros_like(first)
        last[...] = jnp.zeros_like(last)
        for i, field in enumerate((e[0], e[1], e[2], h[0], h[2])):
            turned = field.reshape(depth * wx, wy).T
            first[i : i + 1] = turned[0:1]
            last[i : i + 1] = turned[wy - 1 :]
        for i, layer in (
            (5, weighted(high, [z[1, 0:wx] for z in zs])),
            (6, weighted(low, [z[2, 0:wx] for z in zs])),
        ):
            turned = layer.T
            first[i : i + 1, 0:wx] = turned[0:1]
            last[i : i + 1, 0:wx] = turned[wy - 1 :]
        for ref, y in ((first, 0), (last, wy - 1)):
            corner = jnp.zeros((1, LANES), jnp.float32)
            side_x, side_y = (early_rows(message, freqs, depth, i)[:, y : y + 1] for i in (0, 1))
            for z in range(depth):
                corner = jnp.where(lane == z, side_x[z : z + 1], corner)
                corner = jnp.where(lane == z * wx + wx - 1, side_y[z : z + 1], corner)
            ref[7:8] = corner

    return body


def total_of(terms, rows):
    value = terms[0][rows]
    for term in terms[1:]:
        value = value + term[rows]
    return value


def merge_y_kernel(count, rows, k):
    def body(*refs):
        terms, (first, last), outs = refs[:count], refs[count : count + 2], refs[count + 2 :]
        iy = lax.axis_index("gy")
        size = rows // len(outs)
        swaps = (None, k) if len(outs) == 2 else (None, k + 1, k, None)
        for i, (out, swap) in enumerate(zip(outs, swaps)):
            out[0:size] = total_of(terms, slice(i * size, (i + 1) * size))
            if swap is not None:
                upper = ((iy >> swap) & 1).astype(jnp.float32)
                out[size : size + 8] = upper * first[...] + (1.0 - upper) * last[...]

    return body


def halo_at(ref):
    rows = ref.shape[0]
    return ref[rows - 8 : rows]


def merge_x_kernel(count, rows, depth, wx, zbits, ybits, slots, k):
    def body(*refs):
        terms = refs[:count]
        e, h = refs[count : count + 2]
        zs = refs[count + 2 : count + 2 + zbits]
        ys = refs[count + 2 + zbits : count + 2 + zbits + ybits]
        keep, out = refs[count + 3 + zbits + ybits :]
        half = (rows - 8) // 2
        size = half + 8
        keep[0:half] = total_of(terms, slice(0, half))
        out[0:half] = total_of(terms, slice(half, rows - 8))
        extra = total_of(terms, slice(rows - 8, rows))
        keep[half:size] = extra
        out[half:size] = pltpu.roll(extra, 8 - slots, 0)
        zlow, zhigh = near_flags(lax.axis_index("gz"), zbits)
        ylow, yhigh = near_flags(lax.axis_index("gy"), ybits)
        at = (1 - ((lax.axis_index("gx") >> k) & 1)) * (wx - 1)
        for i in range(3):
            for z in range(depth):
                row = size + i * depth + z
                out[row : row + 1] = e[i, z, pl.ds(at, 1), :]
                if i > 0:
                    row = size + (2 + i) * depth + z
                    out[row : row + 1] = h[i, z, pl.ds(at, 1), :]
        base = size + 5 * depth
        halos = [halo_at(y) for y in ys]
        out[base : base + 1] = weighted(zhigh, [z[0, pl.ds(at, 1), :] for z in zs])
        out[base + 1 : base + 2] = weighted(zlow, [z[2, pl.ds(at, 1), :] for z in zs])
        out[base + 2 : base + 3] = weighted(yhigh, [y[0:1] for y in halos])
        out[base + 3 : base + 4] = weighted(ylow, [y[1:2] for y in halos])

    return body


def pole_kernel():
    def body(table_in, e, pole_in, material_in, after, pole_out, base, coef_out, *scratch):
        table, pole, material, new_pole, sems = scratch
        copies = [
            pltpu.make_async_copy(source, target, sems.at[i])
            for i, (source, target) in enumerate(
                ((table_in, table), (material_in, material), (pole_in, pole))
            )
        ]
        for copy in copies:
            copy.start()
        for copy in copies:
            copy.wait()
        kind = material[...]

        def chosen(i):
            value = jnp.full(kind.shape, table[i, NPOLE - 1], jnp.float32)
            for m in range(NPOLE - 1):
                value = jnp.where(kind == m, table[i, m], value)
            return value

        decay, drive, coef = (chosen(i) for i in range(3))
        coef_out[...] = coef
        for i in range(3):
            old = pole[i]
            electric = e[i]
            new = decay * old + drive * electric
            new_pole[i] = new
            base[i] = electric - coef * (0.5 * (new + old))
        copy = pltpu.make_async_copy(new_pole, pole_out, sems.at[0])
        copy.start()
        copy.wait()

    return body


def field_kernel(freqs, depth, wx, wy, xbits, ybits, zbits, side_rows):
    def body(*refs):
        e, h, base_e, coef_ref, first, message = refs[:6]
        zs = refs[6 : 6 + zbits]
        ys = refs[6 + zbits : 6 + zbits + ybits]
        xs = [x[x.shape[0] - 5 * depth - 4 :] for x in refs[6 + zbits + ybits : 5 + zbits + ybits + xbits]]
        sides = refs[5 + zbits + ybits + xbits : 5 + 2 * zbits + ybits + xbits]
        e_out, h_out = refs[5 + 2 * zbits + ybits + xbits :]
        ix, iy, iz = (lax.axis_index(name) for name in ("gx", "gy", "gz"))
        xlow, xhigh = near_flags(ix, xbits)
        ylow, yhigh = near_flags(iy, ybits)
        zlow, zhigh = near_flags(iz, zbits)
        size = depth * wx
        base = 5 * depth
        lane = lax.broadcasted_iota(jnp.int32, (size, wy), 1)
        line = lax.broadcasted_iota(jnp.int32, (size, wy), 0) & (wx - 1)
        inside_x, inside_y, inside_z = (
            (index > 0).astype(jnp.float32) for index in (ix, iy, iz)
        )

        def flat(ref, i):
            return ref[i].reshape(size, wy)

        ex, ey, ez = (flat(e, i) for i in range(3))
        oldx, oldy, oldz = (flat(h, i) for i in range(3))

        def spread(rows):
            return jnp.broadcast_to(rows[:, None, :], (depth, wx, wy)).reshape(size, wy)

        def next_y(value, column):
            rows = value.shape[0]
            return jnp.where(lane[:rows] == wy - 1, column, pltpu.roll(value, wy - 1, 1))

        def next_x(value, rows):
            return jnp.where(line == wx - 1, spread(rows), pltpu.roll(value, size - 1, 0))

        def next_z(value, layer):
            return jnp.concatenate([value[wx:], layer], axis=0)

        def last_y(value, column):
            return jnp.where(lane == 0, column, pltpu.roll(value, 1, 1))

        def last_x(value, rows):
            return jnp.where(line == 0, spread(rows), pltpu.roll(value, 1, 0))

        def last_z(value, layer):
            return jnp.concatenate([layer, value[:-wx]], axis=0)

        ylo = weighted(ylow, [halo_at(y) for y in ys])
        yhi = weighted(yhigh, [halo_at(y) for y in ys])
        above = yhi.T

        def rows_of(flags, i):
            line = i if i < 3 else i - 1
            at = slice(line * depth, (line + 1) * depth)
            return weighted(flags, [early_rows(message, freqs, depth, i)] + [x[at] for x in xs])

        def extra_of(flags, early, i):
            return weighted(flags, [early] + [x[base + i : base + i + 1] for x in xs])

        def layer_of(flags, i):
            return weighted(flags, [z[i, 0:wx] for z in zs])

        def side_of(flags, i):
            ats = [rows[i] for rows in side_rows]
            return weighted(flags, [side[at : at + 1] for at, side in zip(ats, sides)])

        up_x, up_y = layer_of(zhigh, 0), layer_of(zhigh, 1)
        hx = oldx - courant * ((next_y(ez, above[:, 2:3]) - ez) - (next_z(ey, up_y) - ey))
        hy = oldy - courant * (
            (next_z(ex, up_x) - ex) - (next_x(ez, rows_of(xhigh, 2)) - ez)
        )
        hz = oldz - courant * (
            (next_x(ey, rows_of(xhigh, 1)) - ey) - (next_y(ex, above[:, 0:1]) - ex)
        )
        mx, my, mz = (rows_of(xlow, i) for i in range(3))
        up = jnp.concatenate([mx[1:], extra_of(xlow, side_of(zhigh, 0), 0)], axis=0)
        low_hy = rows_of(xlow, 4) - courant * ((up - mx) - (e[2, :, 0, :] - mz))
        corner = xlow[0] * above[0:depth, 7:8]
        for flag, x in zip(xlow[1:], xs):
            tail = x[base : base + 8].T
            picks = [tail[z * wx + wx - 1 : (z + 1) * wx, 2:3] for z in range(depth)]
            corner = corner + flag * jnp.concatenate(picks, axis=0)
        low_hz = rows_of(xlow, 5) - courant * (
            (e[1, :, 0, :] - my) - (next_y(mx, corner) - mx)
        )
        strip = lax.broadcasted_iota(jnp.int32, (1, LANES), 1)
        lx, ly, lz = ylo[0:1], ylo[1:2], ylo[2:3]
        up = jnp.where(
            strip >= size - wx, pltpu.roll(ylo[5:6], size - wx, 1), pltpu.roll(ly, LANES - wx, 1)
        )
        side_hx = ylo[3:4] - courant * ((first[2:3] - lz) - (up - ly))
        corner = xhigh[0] * ylo[7:8]
        for flag, x in zip(xhigh[1:], xs):
            corner = corner + flag * pltpu.roll(x[base + 3 : base + 4], wx - 1, 1)
        right = jnp.where((strip & (wx - 1)) == wx - 1, corner, pltpu.roll(ly, LANES - 1, 1))
        side_hz = ylo[4:5] - courant * ((right - ly) - (first[0:1] - lx))
        both = jnp.concatenate([side_hx, side_hz, jnp.zeros((6, LANES), jnp.float32)], axis=0)
        both = (inside_y * both).T
        bx, by, bz = (layer_of(zlow, i) for i in range(3))
        under_hx = layer_of(zlow, 3) - courant * (
            (next_y(bz, above[0:wx, 6:7]) - bz) - (ey[:wx] - by)
        )
        right = jnp.concatenate([bz[1:], extra_of(xhigh, side_of(zlow, 2), 1)], axis=0)
        under_hy = layer_of(zlow, 4) - courant * ((ex[:wx] - bx) - (right - bz))
        under_hx = inside_z * under_hx
        under_hy = inside_z * under_hy
        low_hy = inside_x * low_hy
        low_hz = inside_x * low_hz
        curl = (
            (hz - last_y(hz, both[:, 1:2])) - (hy - last_z(hy, under_hy)),
            (hx - last_z(hx, under_hx)) - (hz - last_x(hz, low_hz)),
            (hy - last_x(hy, low_hy)) - (hx - last_y(hx, both[:, 0:1])),
        )
        coef = coef_ref[...].reshape(size, wy)
        shape = (depth, wx, wy)
        for i, magnetic in enumerate((hx, hy, hz)):
            value = flat(base_e, i) + coef * curl[i]
            h_out[i] = magnetic.reshape(shape)
            e_out[i] = value.reshape(shape)

    return body


def inject_kernel(depth, wx, wy, sy, sz, per, zcut):
    def body(*refs):
        blocks = refs[: 1 << zcut]
        e_near, h_near, coef_ref, e_out, h_out, e_new, h_new, sems = refs[1 << zcut :]
        last = depth - 1
        others = slice(0, last)
        copies = [
            pltpu.make_async_copy(e_near.at[:, others], e_out.at[:, others], sems.at[0]),
            pltpu.make_async_copy(h_near.at[:, others], h_out.at[:, others], sems.at[1]),
            pltpu.make_async_copy(h_near.at[2, last], h_out.at[2, last], sems.at[2]),
        ]
        for copy in copies:
            copy.start()
        h_copy = pltpu.make_async_copy(h_new, h_out.at[0:2, last], sems.at[3])
        e_copy = pltpu.make_async_copy(e_new, e_out.at[:, last], sems.at[4])
        ix, iy, iz = (lax.axis_index(name) for name in ("gx", "gy", "gz"))

        @pl.when(iz == sz - 1)
        def _():
            inside_x, inside_y = ((index > 0).astype(jnp.float32) for index in (ix, iy))
            lane = lax.broadcasted_iota(jnp.int32, (wx, wy), 1)
            line = lax.broadcasted_iota(jnp.int32, (wx, wy), 0)
            flip = (
                lax.broadcasted_iota(jnp.int32, (wy, wy), 0)
                + lax.broadcasted_iota(jnp.int32, (wy, wy), 1)
                == wy - 1
            ).astype(jnp.float32)
            flipped = iy < sy // 2

            def straight(value):
                turned = jnp.dot(
                    value, flip, precision=lax.Precision.HIGHEST, preferred_element_type=jnp.float32
                )
                return jnp.where(flipped, turned, value)

            tiles = [straight(ref[...]) for ref in blocks]

            def channel(c):
                start = (c % per) * wx
                return tiles[c // per][start : start + wx]

            electric_x, electric_y, magnetic_x, magnetic_y = (channel(c) for c in range(4))
            before = inside_x * tiles[3 // per][per * wx : per * wx + 1]
            beside = inside_y * blocks[2 // per][per * wx : per * wx + 8].T[0:wx, 1:2]
            last_x = jnp.where(line == 0, before, pltpu.roll(magnetic_y, 1, 0))
            last_y = jnp.where(lane == 0, beside, pltpu.roll(magnetic_x, 1, 1))
            coef = coef_ref[last]
            h_new[0] = h_near[0, last] - courant * magnetic_x
            h_new[1] = h_near[1, last] - courant * magnetic_y
            e_new[0] = e_near[0, last] + coef * (courant * magnetic_y - electric_x)
            e_new[1] = e_near[1, last] - coef * (courant * magnetic_x + electric_y)
            e_new[2] = e_near[2, last] + coef * courant * (
                (magnetic_x - last_y) - (magnetic_y - last_x)
            )

        @pl.when(iz != sz - 1)
        def _():
            for i in range(3):
                e_new[i] = e_near[i, last]
            for i in range(2):
                h_new[i] = h_near[i, last]

        h_copy.start()
        e_copy.start()
        for copy in (*copies, h_copy, e_copy):
            copy.wait()

    return body


def in_hbm(*arrays):
    return [pltpu.with_memory_space_constraint(array, pltpu.HBM) for array in arrays]


def in_vmem(*arrays):
    return [pltpu.with_memory_space_constraint(array, pltpu.VMEM) for array in arrays]


def local(
    e_field, h_field, pole_current, material, pole_table, cotangent, cosines, wavenumber, time_phase
):
    depth, wx, wy = material.shape
    sizes = sx, sy, sz = tuple(lax.axis_size(name) for name in ("gx", "gy", "gz"))
    _, _, iz = (lax.axis_index(name) for name in ("gx", "gy", "gz"))
    freqs, _, count = cotangent.shape
    scale = 1.0 / math.sqrt(freqs * count * sx * sy * sz)
    assert wy == LANES and depth * wx == LANES and 1 < sx <= 4 and sy > 1 and sz > 1
    pad = -count % LANES
    if pad:
        cotangent = jnp.pad(cotangent, ((0, 0), (0, 0), (0, pad)))
        cosines = jnp.pad(cosines, ((0, 0), (0, pad)))
    f32 = jnp.float32
    smem = pl.BlockSpec(memory_space=pltpu.SMEM)
    vmem = pl.BlockSpec(memory_space=pltpu.VMEM)
    hbm = pl.BlockSpec(memory_space=pltpu.HBM)
    small = pltpu.CompilerParams(vmem_limit_bytes=8 << 20)
    xslots = sx // 2
    zslots = min(sz, 4)
    per = 4 // zslots
    xbits, ybits, zbits = bits_of(sx), bits_of(sy), bits_of(sz)
    zcut = bits_of(zslots)

    assert 8 % depth == 0
    mine, waves, *layers = pl.pallas_call(
        pack_kernel(freqs, depth, wx, zbits),
        out_shape=[
            pltpu.VMEM((freqs + 1 + 6 * depth // 8, 8, LANES), f32),
            pltpu.VMEM((2, freqs, LANES), f32),
        ]
        + [pltpu.VMEM((6, wx, wy), f32)] * zbits,
        in_specs=[hbm] * 6,
        out_specs=[vmem] * (2 + zbits),
        scratch_shapes=[
            pltpu.VMEM((6, depth, 8, LANES), f32),
            pltpu.VMEM((2, LANES), f32),
            pltpu.SMEM((freqs,), f32),
            pltpu.SMEM((freqs,), f32),
            pltpu.SemaphoreType.DMA((6 + 2 * zbits,)),
        ],
        compiler_params=small,
        name="pack",
    )(*in_hbm(e_field, h_field, cotangent, cosines, wavenumber, time_phase))
    theirs = exchange(mine, "gx", 1)
    zs = [exchange(layers[k], "gz", (2 << k) - 1) for k in range(zbits)]
    zs = in_vmem(*zs)

    half = sy * wy // 2
    width = count + pad
    block = xslots * per * wx + 8
    part_shape = pltpu.VMEM((zslots // 2, sy, block, wy), f32)
    assert freqs % 2 == 0
    sums = pltpu.VMEM((4 * xslots * wx + 16, half), f32)
    tables = [
        pltpu.VMEM((xslots, 2, freqs, width), f32),
        pltpu.VMEM((xslots, turn_count(wx), 2, freqs, width), f32),
        pltpu.VMEM((turn_count(half), 2, freqs, width), f32),
    ]
    medium = pltpu.CompilerParams(vmem_limit_bytes=24 << 20)
    waves, mine = in_vmem(waves, mine)
    *own, e_near, h_near = pl.pallas_call(
        source_kernel(freqs, depth, wx, half, sizes, zslots, xslots, scale, zbits, False),
        out_shape=(sums, sums, pltpu.VMEM(e_field.shape, f32), pltpu.VMEM(h_field.shape, f32)),
        in_specs=[vmem, vmem, hbm, hbm],
        out_specs=(vmem,) * 4,
        scratch_shapes=tables + [pltpu.SemaphoreType.DMA((2,))],
        compiler_params=medium,
        name="source_own",
    )(waves, mine, *in_hbm(e_field, h_field))
    e_near, h_near = in_vmem(e_near, h_near)
    keep, send = pl.pallas_call(
        source_kernel(freqs, depth, wx, half, sizes, zslots, xslots, scale, zbits, True),
        out_shape=(part_shape, part_shape),
        in_specs=[vmem] * (4 + zbits),
        out_specs=(vmem, vmem),
        scratch_shapes=tables + [sums, sums],
        compiler_params=medium,
        name="source_both",
    )(waves, *in_vmem(theirs, *own), *zs)

    strip = pltpu.VMEM((8, LANES), f32)
    first, last = pl.pallas_call(
        column_kernel(freqs, depth, wx, wy, zbits),
        out_shape=(strip, strip),
        in_specs=[vmem] * (3 + zbits),
        out_specs=(vmem, vmem),
        compiler_params=small,
        name="columns",
    )(e_near, h_near, *in_vmem(theirs), *zs)

    whole = jax.ShapeDtypeStruct((3, depth, wx, wy), f32)
    pole_next, base_e, coef = pl.pallas_call(
        pole_kernel(),
        out_shape=(whole, pltpu.VMEM(whole.shape, f32), pltpu.VMEM((depth, wx, wy), f32)),
        in_specs=[hbm, vmem, hbm, hbm, vmem],
        out_specs=(hbm, vmem, vmem),
        scratch_shapes=[
            pltpu.SMEM(pole_table.shape, f32),
            pltpu.VMEM(whole.shape, f32),
            pltpu.VMEM((depth, wx, wy), jnp.int32),
            pltpu.VMEM(whole.shape, f32),
            pltpu.SemaphoreType.DMA((3,)),
        ],
        compiler_params=small,
        name="pole",
    )(*in_hbm(pole_table), e_near, *in_hbm(pole_current, material), *in_vmem(first))
    base_e, coef = in_vmem(base_e, coef)

    def flat(value):
        return value.reshape(-1, LANES)

    terms = [keep, exchange(send, "gz", 1)]
    sides = [flat(terms[1])]
    side_rows = [[(i // 4) * block + block - 4 + i % 4 for i in range(6)]]
    for k in range(1, zbits):
        at = (1 - ((iz >> k) & 1)) * (depth - 1)
        rows = theirs[freqs + 1 :].reshape(6, depth, LANES)
        rows = lax.dynamic_index_in_dim(rows, at, 1, keepdims=False)
        sides.append(exchange(jnp.pad(rows, ((0, 2), (0, 0))), "gz", (2 << k) - 1))
        side_rows.append(list(range(6)))
    for k in range(1, zbits):
        part = terms[0] + terms[1]
        mask = (2 << k) - 1
        if k < zcut:
            middle = part.shape[0] // 2
            terms = [part[:middle], exchange(part[middle:], "gz", mask)]
        else:
            terms = [part, exchange(part, "gz", mask)]
    terms = [flat(term) for term in terms]
    rows = sy * block

    ys = [None] * ybits
    k = 0
    while k < ybits:
        both = k + 1 < ybits
        size = rows // 4 if both else rows // 2
        plain, laden = pltpu.VMEM((size, LANES), f32), pltpu.VMEM((size + 8, LANES), f32)
        shapes = (plain, laden, laden, plain) if both else (plain, laden)
        keep, *away = pl.pallas_call(
            merge_y_kernel(len(terms), rows, k),
            out_shape=shapes,
            in_specs=[vmem] * (len(terms) + 2),
            out_specs=(vmem,) * len(shapes),
            compiler_params=small,
            name="merge_y",
        )(*in_vmem(*terms, first, last))
        if both:
            ys[k] = exchange(away[1], "gy", (2 << k) - 1)
            other = exchange(away[2], "gy", 2 << k)
            ys[k + 1] = exchange(away[0], "gy", (4 << k) - 1)
            terms = [keep, ys[k], ys[k + 1], other]
            k += 2
        else:
            ys[k] = exchange(away[0], "gy", (2 << k) - 1)
            terms = [keep, ys[k]]
            k += 1
        rows = size
    near = [*zs, *in_vmem(*ys)]
    xs = []
    slots = xslots
    for k in range(1, xbits):
        size = (rows - 8) // 2 + 8
        keep, away = pl.pallas_call(
            merge_x_kernel(len(terms), rows, depth, wx, zbits, ybits, slots, k),
            out_shape=(
                pltpu.VMEM((size, LANES), f32),
                pltpu.VMEM((size + 5 * depth + 4, LANES), f32),
            ),
            in_specs=[vmem] * (len(terms) + 3 + zbits + ybits),
            out_specs=(vmem, vmem),
            compiler_params=small,
            name="merge_x",
        )(*in_vmem(*terms), e_near, h_near, *near, coef)
        xs.append(exchange(away, "gx", (2 << k) - 1))
        rows = size
        slots //= 2
        terms = [keep, xs[-1]]
    part = sum(term[:rows] for term in terms)

    e_most, h_most = pl.pallas_call(
        field_kernel(freqs, depth, wx, wy, xbits, ybits, zbits, side_rows),
        out_shape=(pltpu.VMEM(whole.shape, f32), pltpu.VMEM(whole.shape, f32)),
        in_specs=[vmem] * (5 + xbits + ybits + 2 * zbits),
        out_specs=(vmem,) * 2,
        compiler_params=pltpu.CompilerParams(vmem_limit_bytes=16 << 20),
        name="fields",
    )(e_near, h_near, base_e, coef, *in_vmem(first, theirs), *near, *in_vmem(*xs, *sides))

    top = gray(sz - 1)
    blocks = [part]
    for k in reversed(range(zcut)):
        others = [exchange(value, "gz", (2 << k) - 1) for value in blocks]
        blocks = others + blocks if (top >> k) & 1 else blocks + others
    e_next, h_next = pl.pallas_call(
        inject_kernel(depth, wx, wy, sy, sz, per, zcut),
        out_shape=(whole, whole),
        in_specs=[vmem] * (len(blocks) + 3),
        out_specs=(hbm, hbm),
        scratch_shapes=[
            pltpu.VMEM((3, wx, wy), f32),
            pltpu.VMEM((2, wx, wy), f32),
            pltpu.SemaphoreType.DMA((5,)),
        ],
        compiler_params=small,
        name="inject",
    )(*in_vmem(*blocks, e_most, h_most), coef)
    return (e_next, h_next, pole_next)


def solution(mesh):
    in_specs = (
        P(None, "gz", "gx", "gy"),
        P(None, "gz", "gx", "gy"),
        P(None, "gz", "gx", "gy"),
        P("gz", "gx", "gy"),
        P(),
        P(None, None, ("gx", "gy", "gz")),
        P(None, ("gx", "gy", "gz")),
        P(),
        P(),
    )
    out_specs = (P(None, "gz", "gx", "gy"), P(None, "gz", "gx", "gy"), P(None, "gz", "gx", "gy"))
    return jax.shard_map(
        local, mesh=mesh, in_specs=in_specs, out_specs=out_specs, check_vma=False
    )
```

```python
import math

import jax
import jax.numpy as jnp
from jax import lax
from jax.experimental import pallas as pl
from jax.experimental.pallas import tpu as pltpu
from jax.sharding import PartitionSpec as P


NPOLE = 4
LANES = 128


courant = 0.5


def exchange(array, axis, mask):
    return lax.ppermute(array, axis, [(i, i ^ mask) for i in range(lax.axis_size(axis))])


def gray(index):
    return index ^ (index >> 1)


def bits_of(size):
    return size.bit_length() - 1


def cmul(a, b):
    return (a[0] * b[0] - a[1] * b[1], a[0] * b[1] + a[1] * b[0])


def small_turn(angle):
    q = angle * angle
    c = 1.0 + q * (-1 / 2 + q * (1 / 24 + q * (-1 / 720 + q * (1 / 40320))))
    s = angle * (1.0 + q * (-1 / 6 + q * (1 / 120 + q * (-1 / 5040 + q * (1 / 362880)))))
    return c, s


def doubled(turn):
    c, s = turn
    return (c - s) * (c + s), 2.0 * (c * s)


def tree_levels(rows):
    levels = 0
    while 3 ** (levels + 1) * 8 <= rows:
        levels += 1
    return levels


def turn_table(first, unit, rows):
    powers = [unit]
    for _ in range(2):
        powers.append(doubled(powers[-1]))
    step = doubled(powers[-1])
    for level in range(max(1, tree_levels(rows))):
        powers.append(step)
        if level < tree_levels(rows):
            first = cmul(first, step)
        step = cmul(step, doubled(step))
    return [first, *powers]


def turn_count(rows):
    return 4 + max(1, tree_levels(rows))


def both_ways(value, turn):
    cc, ss = value[0] * turn[0], value[1] * turn[1]
    cs, sc = value[0] * turn[1], value[1] * turn[0]
    return (cc - ss, sc + cs), (cc + ss, sc - cs)


def rotations(table, rows):
    base, powers = table[0], table[1:]
    sub = lax.broadcasted_iota(jnp.int32, (8, base[0].shape[-1]), 0)
    value = tuple(jnp.broadcast_to(part, sub.shape) for part in base)
    for k in range(3):
        picked = (sub & (1 << k)) != 0
        value = cmul(value, (jnp.where(picked, powers[k][0], 1.0), jnp.where(picked, powers[k][1], 0.0)))
    blocks = [value]
    last = 0
    for level in range(tree_levels(rows)):
        last = level
        pairs = [both_ways(block, powers[3 + level]) for block in blocks]
        blocks = [pair[1] for pair in pairs] + blocks + [pair[0] for pair in pairs]
    while len(blocks) * 8 < rows:
        blocks.append(cmul(blocks[len(blocks) - 3**last], powers[3 + last]))
    return tuple(jnp.concatenate([block[i] for block in blocks], axis=0)[:rows] for i in (0, 1))


def split(value):
    high = value.astype(jnp.bfloat16)
    return high, (value - high.astype(jnp.float32)).astype(jnp.bfloat16)


def dot_nt(a, b):
    return lax.dot_general(a, b, (((1,), (1,)), ((), ())), preferred_element_type=jnp.float32)


def source_kernel(freqs, depth, wx, half, sizes, zslots, xslots, scale, zbits, closing):
    sx, sy, _ = sizes
    per = 4 // zslots
    main = 4 * xslots * wx

    def body(*refs):
        waves, packed = refs[:2]
        if closing:
            old_even, old_odd = refs[2:4]
            keep, send, xback, xturn, yturn, acc_even, acc_odd = refs[4 + zbits :]
        else:
            e_in, h_in, acc_even, acc_odd, e_near, h_near, xback, xturn, yturn, sems = refs[2:]
            copies = [
                pltpu.make_async_copy(source, target, sems.at[i])
                for i, (source, target) in enumerate(((e_in, e_near), (h_in, h_near)))
            ]
            for copy in copies:
                copy.start()
        ix, iy, iz = (lax.axis_index(name) for name in ("gx", "gy", "gz"))
        xbit, ybit, zbit = bits_of(sx), bits_of(sy), bits_of(zslots)
        starts = []
        for slot in range(xslots):
            code = ix
            for k in range(1, xbit):
                code = code ^ (((slot >> (xbit - 1 - k)) & 1) << k)
            starts.append((code * wx).astype(jnp.float32))
        zcode = 0
        for k in range(zbit):
            zcode = zcode * 2 + ((gray(iz) >> k) & 1)
        ycode = gray(iy)
        center = (2 * half - 1) / 2.0
        wave, phase = waves[0], waves[1]
        along_x = wave * packed[freqs, 0:1, :]
        along_y = wave * packed[freqs, 1:2, :]
        origin = along_y * center - phase
        unit = doubled(small_turn(0.5 * along_x))
        for xr in range(xslots):
            angle = along_x * starts[xr] + origin
            first = jnp.cos(angle), jnp.sin(angle)
            xback[xr, 0], xback[xr, 1] = cmul(first, (unit[0], -unit[1]))
            for k, turn in enumerate(turn_table(first, unit, wx)):
                xturn[xr, k, 0], xturn[xr, k, 1] = turn
        first = small_turn(0.5 * along_y)
        for k, turn in enumerate(turn_table(first, doubled(first), half)):
            yturn[k, 0], yturn[k, 1] = turn
        if closing:
            acc_even[...] = old_even[...]
            acc_odd[...] = old_odd[...]
        else:
            acc_even[...] = jnp.zeros_like(acc_even)
            acc_odd[...] = jnp.zeros_like(acc_odd)

        def pair(step, carry):
            firsts, seconds, coses, sines = [], [], [], []
            for n in range(2):
                f = 2 * step + n

                def row(ref, *where):
                    return tuple(ref[(*where, i, pl.ds(f, 1), slice(None))] for i in (0, 1))

                cy, sy_ = rotations([row(yturn, k) for k in range(turn_count(half))], half)
                coses.append(cy)
                sines.append(sy_)
                turns = [
                    rotations([row(xturn, xr, k) for k in range(turn_count(wx))], wx)
                    for xr in range(xslots)
                ]
                first, second = [], []
                for zr in range(zslots):
                    for xr in range(xslots):
                        cx, sx_ = turns[xr]
                        for c2 in range(per):
                            at = 2 * ((zcode ^ zr) * per + c2)
                            p = packed[f, pl.ds(at, 1), :]
                            q = packed[f, pl.ds(at + 1, 1), :]
                            first.append(p * cx - q * sx_)
                            second.append(p * sx_ + q * cx)
                p = packed[f, 6:7, :]
                q = packed[f, 7:8, :]
                line = lax.broadcasted_iota(jnp.int32, (16, p.shape[-1]), 0)
                one_first = jnp.zeros(line.shape, jnp.float32)
                one_second = one_first
                for xr in range(xslots):
                    cx, sx_ = row(xback, xr)
                    one_first = jnp.where(line == xr, p * cx - q * sx_, one_first)
                    one_second = jnp.where(line == xr, p * sx_ + q * cx, one_second)
                firsts.append(jnp.concatenate(first + [one_first], axis=0))
                seconds.append(jnp.concatenate(second + [one_second], axis=0))

            def product(lefts, rights):
                lh, ll = split(jnp.concatenate(lefts, axis=1))
                rh, rl = split(jnp.concatenate(rights, axis=1))
                both = dot_nt(jnp.concatenate([lh, ll], axis=0), rh)
                rows = lh.shape[0]
                return both[:rows] + dot_nt(lh, rl) + both[rows:]

            acc_even[...] += product(firsts, coses)
            acc_odd[...] += product(seconds, sines)
            return carry

        lax.fori_loop(0, freqs // 2, pair, 0, unroll=8 if closing else 4)
        if not closing:
            for copy in copies:
                copy.wait()
            return

        def slot(tile):
            code = gray(tile) ^ ycode
            place = 0
            for k in range(ybit):
                place = place * 2 + ((code >> k) & 1)
            return place

        def place(zr):
            return (keep, zr) if zr < zslots // 2 else (send, zr - zslots // 2)

        extra = xslots * per * wx
        for zr in range(zslots):
            ref, z = place(zr)
            for y in range(sy):
                ref[z, y, extra : extra + 8] = jnp.zeros((8, LANES), jnp.float32)
        at_z = (1 - (iz & 1)) * (depth - 1)
        for i, field in enumerate((0, 1, 2, 3, 4, 5, 6, 8)):
            row = field * depth
            spot = extra + 4 + i % 4
            send[0, i // 4, spot : spot + 1] = packed[
                freqs + 1 + row // 8, pl.ds(row % 8 + at_z, 1), :
            ]
        turned = 2 // per
        spare = 2 % per
        for j in range(sy // 2):
            lanes = slice(j * LANES, (j + 1) * LANES)
            up = slot(sy // 2 + j)
            down = slot(sy // 2 - 1 - j)
            at = 0
            for zr in range(zslots):
                ref, z = place(zr)
                for xr in range(xslots):
                    for c2 in range(per):
                        rows = slice(at * wx, (at + 1) * wx)
                        even = acc_even[rows, lanes] * scale
                        odd = acc_odd[rows, lanes] * scale
                        into = slice((xr * per + c2) * wx, (xr * per + c2 + 1) * wx)
                        ref[z, up, into] = even - odd
                        ref[z, down, into] = even + odd
                        at += 1
            for xr in range(xslots):
                even = acc_even[main + xr : main + xr + 1, lanes] * scale
                odd = acc_odd[main + xr : main + xr + 1, lanes] * scale
                for zr in range(zslots):
                    ref, z = place(zr)
                    ref[z, up, extra + 2 * xr : extra + 2 * xr + 1] = even - odd
                    ref[z, down, extra + 2 * xr : extra + 2 * xr + 1] = even + odd
                start = (((zcode ^ turned) * xslots + xr) * per + spare) * wx
                rows = pl.ds(pl.multiple_of(start, wx), wx)
                even = (acc_even[rows, lanes] * scale).T
                odd = (acc_odd[rows, lanes] * scale).T
                lower = slot(sy // 2 - j)
                line = slice(extra + 2 * xr + 1, extra + 2 * xr + 2)
                for zr in range(zslots):
                    ref, z = place(zr)
                    ref[z, lower, line, 0:wx] = even[0:1] + odd[0:1]
                if j < sy // 2 - 1:
                    upper = slot(sy // 2 + j + 1)
                    for zr in range(zslots):
                        ref, z = place(zr)
                        ref[z, upper, line, 0:wx] = even[LANES - 1 :] - odd[LANES - 1 :]

    return body


def near_flags(index, bits):
    low, high = [], []
    for k in range(bits):
        upper = (index >> k) & 1
        rest = index & ((1 << k) - 1)
        low.append(((upper == 1) & (rest == 0)).astype(jnp.float32))
        high.append(((upper == 0) & (rest == (1 << k) - 1)).astype(jnp.float32))
    return low, high


def weighted(flags, values):
    total = flags[0] * values[0]
    for flag, value in zip(flags[1:], values[1:]):
        total = total + flag * value
    return total


def pack_kernel(freqs, depth, wx, zbits):
    def body(*refs):
        e_in, h_in, cotangent, cosines, wavenumber, time_phase, message, waves = refs[:8]
        layers = refs[8 : 8 + zbits]
        edge, cos_near, wave_near, phase_near, sems = refs[8 + zbits :]
        upper = lax.axis_index("gx") & 1
        pairs = [
            (cotangent, message.at[0:freqs]),
            (e_in.at[:, :, 0:8], edge.at[0, 0:3]),
            (h_in.at[:, :, 0:8], edge.at[0, 3:6]),
            (e_in.at[:, :, wx - 8 : wx], edge.at[1, 0:3]),
            (h_in.at[:, :, wx - 8 : wx], edge.at[1, 3:6]),
            (cosines, cos_near),
            (wavenumber, wave_near),
            (time_phase, phase_near),
        ]
        for k, layer in enumerate(layers):
            at = (1 - ((lax.axis_index("gz") >> k) & 1)) * (depth - 1)
            pairs += [(e_in.at[:, at], layer.at[0:3]), (h_in.at[:, at], layer.at[3:6])]
        copies = [
            pltpu.make_async_copy(source, target, sems.at[i])
            for i, (source, target) in enumerate(pairs)
        ]
        for copy in copies:
            copy.start()
        for copy in copies:
            copy.wait()
        message[freqs, 0:2] = cos_near[...]
        message[freqs, 2:8] = jnp.zeros((6, LANES), jnp.float32)
        which = lax.broadcasted_iota(jnp.int32, (freqs, LANES), 0)
        for i, near in enumerate((wave_near, phase_near)):
            value = jnp.zeros((freqs, LANES), jnp.float32)
            for f in range(freqs):
                value = jnp.where(which == f, near[f], value)
            waves[i] = value
        for i in range(12):
            end = 1 - upper if i < 6 else upper
            for z in range(depth):
                row = i * depth + z
                message[freqs + 1 + row // 8, row % 8 : row % 8 + 1] = edge[
                    end, i % 6, z, pl.ds(7 * end, 1), :
                ]

    return body


def early_rows(message, freqs, depth, i):
    row = i * depth
    return message[freqs + 1 + row // 8, row % 8 : row % 8 + depth]


def column_kernel(freqs, depth, wx, wy, zbits):
    def body(*refs):
        e, h, message = refs[:3]
        zs = refs[3 : 3 + zbits]
        first, last = refs[3 + zbits :]
        low, high = near_flags(lax.axis_index("gz"), zbits)
        lane = lax.broadcasted_iota(jnp.int32, (1, LANES), 1)
        first[...] = jnp.zeros_like(first)
        last[...] = jnp.zeros_like(last)
        for i, field in enumerate((e[0], e[1], e[2], h[0], h[2])):
            turned = field.reshape(depth * wx, wy).T
            first[i : i + 1] = turned[0:1]
            last[i : i + 1] = turned[wy - 1 :]
        for i, layer in (
            (5, weighted(high, [z[1, 0:wx] for z in zs])),
            (6, weighted(low, [z[2, 0:wx] for z in zs])),
        ):
            turned = layer.T
            first[i : i + 1, 0:wx] = turned[0:1]
            last[i : i + 1, 0:wx] = turned[wy - 1 :]
        for ref, y in ((first, 0), (last, wy - 1)):
            corner = jnp.zeros((1, LANES), jnp.float32)
            side_x, side_y, next_x, next_y = (
                early_rows(message, freqs, depth, i)[:, y : y + 1] for i in (0, 1, 6, 7)
            )
            for z in range(depth):
                corner = jnp.where(lane == z, side_x[z : z + 1], corner)
                corner = jnp.where(lane == z * wx + wx - 1, side_y[z : z + 1], corner)
                corner = jnp.where(lane == depth + z, next_x[z : z + 1], corner)
                corner = jnp.where(lane == z * wx + wx - 2, next_y[z : z + 1], corner)
            ref[7:8] = corner

    return body


def total_of(terms, rows):
    value = terms[0][rows]
    for term in terms[1:]:
        value = value + term[rows]
    return value


def merge_y_kernel(count, rows, k):
    def body(*refs):
        terms, (first, last), outs = refs[:count], refs[count : count + 2], refs[count + 2 :]
        iy = lax.axis_index("gy")
        size = rows // len(outs)
        swaps = (None, k) if len(outs) == 2 else (None, k + 1, k, None)
        for i, (out, swap) in enumerate(zip(outs, swaps)):
            out[0:size] = total_of(terms, slice(i * size, (i + 1) * size))
            if swap is not None:
                upper = ((iy >> swap) & 1).astype(jnp.float32)
                out[size : size + 8] = upper * first[...] + (1.0 - upper) * last[...]

    return body


def halo_at(ref):
    rows = ref.shape[0]
    return ref[rows - 8 : rows]


def merge_x_kernel(freqs, count, rows, depth, zbits, ybits, slots, side_rows):
    def body(*refs):
        terms = refs[:count]
        message = refs[count]
        sides = refs[count + 1 : count + 1 + zbits]
        ys = refs[count + 1 + zbits : count + 1 + zbits + ybits]
        keep, out = refs[count + 2 + zbits + ybits :]
        half = (rows - 8) // 2
        size = half + 8
        keep[0:half] = total_of(terms, slice(0, half))
        out[0:half] = total_of(terms, slice(half, rows - 8))
        extra = total_of(terms, slice(rows - 8, rows))
        keep[half:size] = extra
        out[half:size] = pltpu.roll(extra, 8 - slots, 0)
        zlow, zhigh = near_flags(lax.axis_index("gz"), zbits)
        ylow, yhigh = near_flags(lax.axis_index("gy"), ybits)
        for line, i in enumerate((6, 7, 8, 10, 11)):
            row = size + line * depth
            out[row : row + depth] = early_rows(message, freqs, depth, i)
        base = size + 5 * depth

        def side(flags, i):
            ats = [rows[i] for rows in side_rows]
            return weighted(flags, [ref[at : at + 1] for at, ref in zip(ats, sides)])

        halos = [halo_at(y) for y in ys]
        out[base : base + 1] = side(zhigh, 6)
        out[base + 1 : base + 2] = side(zlow, 7)
        out[base + 2 : base + 3] = weighted(yhigh, [y[7:8] for y in halos])
        out[base + 3 : base + 4] = weighted(ylow, [y[7:8] for y in halos])

    return body


def pole_kernel():
    def body(table_in, e, pole_in, material_in, after, pole_out, base, coef_out, *scratch):
        table, pole, material, new_pole, sems = scratch
        copies = [
            pltpu.make_async_copy(source, target, sems.at[i])
            for i, (source, target) in enumerate(
                ((table_in, table), (material_in, material), (pole_in, pole))
            )
        ]
        for copy in copies:
            copy.start()
        for copy in copies:
            copy.wait()
        kind = material[...]

        def chosen(i):
            value = jnp.full(kind.shape, table[i, NPOLE - 1], jnp.float32)
            for m in range(NPOLE - 1):
                value = jnp.where(kind == m, table[i, m], value)
            return value

        decay, drive, coef = (chosen(i) for i in range(3))
        coef_out[...] = coef
        for i in range(3):
            old = pole[i]
            electric = e[i]
            new = decay * old + drive * electric
            new_pole[i] = new
            base[i] = electric - coef * (0.5 * (new + old))
        copy = pltpu.make_async_copy(new_pole, pole_out, sems.at[0])
        copy.start()
        copy.wait()

    return body


def field_kernel(freqs, depth, wx, wy, xbits, ybits, zbits, side_rows):
    def body(*refs):
        e, h, base_e, coef_ref, first, message = refs[:6]
        zs = refs[6 : 6 + zbits]
        ys = refs[6 + zbits : 6 + zbits + ybits]
        xs = [x[x.shape[0] - 5 * depth - 4 :] for x in refs[6 + zbits + ybits : 5 + zbits + ybits + xbits]]
        sides = refs[5 + zbits + ybits + xbits : 5 + 2 * zbits + ybits + xbits]
        e_out, h_out = refs[5 + 2 * zbits + ybits + xbits :]
        ix, iy, iz = (lax.axis_index(name) for name in ("gx", "gy", "gz"))
        xlow, xhigh = near_flags(ix, xbits)
        ylow, yhigh = near_flags(iy, ybits)
        zlow, zhigh = near_flags(iz, zbits)
        size = depth * wx
        base = 5 * depth
        lane = lax.broadcasted_iota(jnp.int32, (size, wy), 1)
        line = lax.broadcasted_iota(jnp.int32, (size, wy), 0) & (wx - 1)
        inside_x, inside_y, inside_z = (
            (index > 0).astype(jnp.float32) for index in (ix, iy, iz)
        )

        def flat(ref, i):
            return ref[i].reshape(size, wy)

        ex, ey, ez = (flat(e, i) for i in range(3))
        oldx, oldy, oldz = (flat(h, i) for i in range(3))

        def spread(rows):
            return jnp.broadcast_to(rows[:, None, :], (depth, wx, wy)).reshape(size, wy)

        def next_y(value, column):
            rows = value.shape[0]
            return jnp.where(lane[:rows] == wy - 1, column, pltpu.roll(value, wy - 1, 1))

        def next_x(value, rows):
            return jnp.where(line == wx - 1, spread(rows), pltpu.roll(value, size - 1, 0))

        def next_z(value, layer):
            return jnp.concatenate([value[wx:], layer], axis=0)

        def last_y(value, column):
            return jnp.where(lane == 0, column, pltpu.roll(value, 1, 1))

        def last_x(value, rows):
            return jnp.where(line == 0, spread(rows), pltpu.roll(value, 1, 0))

        def last_z(value, layer):
            return jnp.concatenate([layer, value[:-wx]], axis=0)

        ylo = weighted(ylow, [halo_at(y) for y in ys])
        yhi = weighted(yhigh, [halo_at(y) for y in ys])
        above = yhi.T

        def rows_of(flags, i):
            line = i if i < 3 else i - 1
            at = slice(line * depth, (line + 1) * depth)
            return weighted(flags, [early_rows(message, freqs, depth, i)] + [x[at] for x in xs])

        def extra_of(flags, early, i):
            return weighted(flags, [early] + [x[base + i : base + i + 1] for x in xs])

        def layer_of(flags, i):
            return weighted(flags, [z[i, 0:wx] for z in zs])

        def side_of(flags, i):
            ats = [rows[i] for rows in side_rows]
            return weighted(flags, [side[at : at + 1] for at, side in zip(ats, sides)])

        up_x, up_y = layer_of(zhigh, 0), layer_of(zhigh, 1)
        hx = oldx - courant * ((next_y(ez, above[:, 2:3]) - ez) - (next_z(ey, up_y) - ey))
        hy = oldy - courant * (
            (next_z(ex, up_x) - ex) - (next_x(ez, rows_of(xhigh, 2)) - ez)
        )
        hz = oldz - courant * (
            (next_x(ey, rows_of(xhigh, 1)) - ey) - (next_y(ex, above[:, 0:1]) - ex)
        )
        mx, my, mz = (rows_of(xlow, i) for i in range(3))
        up = jnp.concatenate([mx[1:], extra_of(xlow, side_of(zhigh, 0), 0)], axis=0)
        low_hy = rows_of(xlow, 4) - courant * ((up - mx) - (e[2, :, 0, :] - mz))
        corner = xlow[0] * above[0:depth, 7:8]
        for flag, x in zip(xlow[1:], xs):
            tail = x[base : base + 8].T
            corner = corner + flag * tail[depth : 2 * depth, 2:3]
        low_hz = rows_of(xlow, 5) - courant * (
            (e[1, :, 0, :] - my) - (next_y(mx, corner) - mx)
        )
        strip = lax.broadcasted_iota(jnp.int32, (1, LANES), 1)
        lx, ly, lz = ylo[0:1], ylo[1:2], ylo[2:3]
        up = jnp.where(
            strip >= size - wx, pltpu.roll(ylo[5:6], size - wx, 1), pltpu.roll(ly, LANES - wx, 1)
        )
        side_hx = ylo[3:4] - courant * ((first[2:3] - lz) - (up - ly))
        corner = xhigh[0] * ylo[7:8]
        for flag, x in zip(xhigh[1:], xs):
            corner = corner + flag * pltpu.roll(x[base + 3 : base + 4], 1, 1)
        right = jnp.where((strip & (wx - 1)) == wx - 1, corner, pltpu.roll(ly, LANES - 1, 1))
        side_hz = ylo[4:5] - courant * ((right - ly) - (first[0:1] - lx))
        both = jnp.concatenate([side_hx, side_hz, jnp.zeros((6, LANES), jnp.float32)], axis=0)
        both = (inside_y * both).T
        bx, by, bz = (layer_of(zlow, i) for i in range(3))
        under_hx = layer_of(zlow, 3) - courant * (
            (next_y(bz, above[0:wx, 6:7]) - bz) - (ey[:wx] - by)
        )
        right = jnp.concatenate([bz[1:], extra_of(xhigh, side_of(zlow, 2), 1)], axis=0)
        under_hy = layer_of(zlow, 4) - courant * ((ex[:wx] - bx) - (right - bz))
        under_hx = inside_z * under_hx
        under_hy = inside_z * under_hy
        low_hy = inside_x * low_hy
        low_hz = inside_x * low_hz
        curl = (
            (hz - last_y(hz, both[:, 1:2])) - (hy - last_z(hy, under_hy)),
            (hx - last_z(hx, under_hx)) - (hz - last_x(hz, low_hz)),
            (hy - last_x(hy, low_hy)) - (hx - last_y(hx, both[:, 0:1])),
        )
        coef = coef_ref[...].reshape(size, wy)
        shape = (depth, wx, wy)
        for i, magnetic in enumerate((hx, hy, hz)):
            value = flat(base_e, i) + coef * curl[i]
            h_out[i] = magnetic.reshape(shape)
            e_out[i] = value.reshape(shape)

    return body


def inject_kernel(depth, wx, wy, sy, sz, per, zcut):
    def body(*refs):
        blocks = refs[: 1 << zcut]
        e_near, h_near, coef_ref, e_out, h_out, e_new, h_new, sems = refs[1 << zcut :]
        last = depth - 1
        others = slice(0, last)
        copies = [
            pltpu.make_async_copy(e_near.at[:, others], e_out.at[:, others], sems.at[0]),
            pltpu.make_async_copy(h_near.at[:, others], h_out.at[:, others], sems.at[1]),
            pltpu.make_async_copy(h_near.at[2, last], h_out.at[2, last], sems.at[2]),
        ]
        for copy in copies:
            copy.start()
        h_copy = pltpu.make_async_copy(h_new, h_out.at[0:2, last], sems.at[3])
        e_copy = pltpu.make_async_copy(e_new, e_out.at[:, last], sems.at[4])
        ix, iy, iz = (lax.axis_index(name) for name in ("gx", "gy", "gz"))

        @pl.when(iz == sz - 1)
        def _():
            inside_x, inside_y = ((index > 0).astype(jnp.float32) for index in (ix, iy))
            lane = lax.broadcasted_iota(jnp.int32, (wx, wy), 1)
            line = lax.broadcasted_iota(jnp.int32, (wx, wy), 0)
            flip = (
                lax.broadcasted_iota(jnp.int32, (wy, wy), 0)
                + lax.broadcasted_iota(jnp.int32, (wy, wy), 1)
                == wy - 1
            ).astype(jnp.float32)
            flipped = iy < sy // 2

            def straight(value):
                turned = jnp.dot(
                    value, flip, precision=lax.Precision.HIGHEST, preferred_element_type=jnp.float32
                )
                return jnp.where(flipped, turned, value)

            tiles = [straight(ref[...]) for ref in blocks]

            def channel(c):
                start = (c % per) * wx
                return tiles[c // per][start : start + wx]

            electric_x, electric_y, magnetic_x, magnetic_y = (channel(c) for c in range(4))
            before = inside_x * tiles[3 // per][per * wx : per * wx + 1]
            beside = inside_y * blocks[2 // per][per * wx : per * wx + 8].T[0:wx, 1:2]
            last_x = jnp.where(line == 0, before, pltpu.roll(magnetic_y, 1, 0))
            last_y = jnp.where(lane == 0, beside, pltpu.roll(magnetic_x, 1, 1))
            coef = coef_ref[last]
            h_new[0] = h_near[0, last] - courant * magnetic_x
            h_new[1] = h_near[1, last] - courant * magnetic_y
            e_new[0] = e_near[0, last] + coef * (courant * magnetic_y - electric_x)
            e_new[1] = e_near[1, last] - coef * (courant * magnetic_x + electric_y)
            e_new[2] = e_near[2, last] + coef * courant * (
                (magnetic_x - last_y) - (magnetic_y - last_x)
            )

        @pl.when(iz != sz - 1)
        def _():
            for i in range(3):
                e_new[i] = e_near[i, last]
            for i in range(2):
                h_new[i] = h_near[i, last]

        h_copy.start()
        e_copy.start()
        for copy in (*copies, h_copy, e_copy):
            copy.wait()

    return body


def in_hbm(*arrays):
    return [pltpu.with_memory_space_constraint(array, pltpu.HBM) for array in arrays]


def in_vmem(*arrays):
    return [pltpu.with_memory_space_constraint(array, pltpu.VMEM) for array in arrays]


def local(
    e_field, h_field, pole_current, material, pole_table, cotangent, cosines, wavenumber, time_phase
):
    depth, wx, wy = material.shape
    sizes = sx, sy, sz = tuple(lax.axis_size(name) for name in ("gx", "gy", "gz"))
    _, _, iz = (lax.axis_index(name) for name in ("gx", "gy", "gz"))
    freqs, _, count = cotangent.shape
    scale = 1.0 / math.sqrt(freqs * count * sx * sy * sz)
    assert wy == LANES and depth * wx == LANES and 1 < sx <= 4 and sy > 1 and sz > 1
    pad = -count % LANES
    if pad:
        cotangent = jnp.pad(cotangent, ((0, 0), (0, 0), (0, pad)))
        cosines = jnp.pad(cosines, ((0, 0), (0, pad)))
    f32 = jnp.float32
    smem = pl.BlockSpec(memory_space=pltpu.SMEM)
    vmem = pl.BlockSpec(memory_space=pltpu.VMEM)
    hbm = pl.BlockSpec(memory_space=pltpu.HBM)
    small = pltpu.CompilerParams(vmem_limit_bytes=8 << 20)
    xslots = sx // 2
    zslots = min(sz, 4)
    per = 4 // zslots
    xbits, ybits, zbits = bits_of(sx), bits_of(sy), bits_of(sz)
    zcut = bits_of(zslots)

    assert 8 % depth == 0
    mine, waves, *layers = pl.pallas_call(
        pack_kernel(freqs, depth, wx, zbits),
        out_shape=[
            pltpu.VMEM((freqs + 1 + 12 * depth // 8, 8, LANES), f32),
            pltpu.VMEM((2, freqs, LANES), f32),
        ]
        + [pltpu.VMEM((6, wx, wy), f32)] * zbits,
        in_specs=[hbm] * 6,
        out_specs=[vmem] * (2 + zbits),
        scratch_shapes=[
            pltpu.VMEM((2, 6, depth, 8, LANES), f32),
            pltpu.VMEM((2, LANES), f32),
            pltpu.SMEM((freqs,), f32),
            pltpu.SMEM((freqs,), f32),
            pltpu.SemaphoreType.DMA((8 + 2 * zbits,)),
        ],
        compiler_params=small,
        name="pack",
    )(*in_hbm(e_field, h_field, cotangent, cosines, wavenumber, time_phase))
    theirs = exchange(mine, "gx", 1)
    zs = [exchange(layers[k], "gz", (2 << k) - 1) for k in range(zbits)]
    zs = in_vmem(*zs)

    half = sy * wy // 2
    width = count + pad
    block = xslots * per * wx + 8
    part_shape = pltpu.VMEM((zslots // 2, sy, block, wy), f32)
    assert freqs % 2 == 0
    sums = pltpu.VMEM((4 * xslots * wx + 16, half), f32)
    tables = [
        pltpu.VMEM((xslots, 2, freqs, width), f32),
        pltpu.VMEM((xslots, turn_count(wx), 2, freqs, width), f32),
        pltpu.VMEM((turn_count(half), 2, freqs, width), f32),
    ]
    medium = pltpu.CompilerParams(vmem_limit_bytes=24 << 20)
    waves, mine = in_vmem(waves, mine)
    *own, e_near, h_near = pl.pallas_call(
        source_kernel(freqs, depth, wx, half, sizes, zslots, xslots, scale, zbits, False),
        out_shape=(sums, sums, pltpu.VMEM(e_field.shape, f32), pltpu.VMEM(h_field.shape, f32)),
        in_specs=[vmem, vmem, hbm, hbm],
        out_specs=(vmem,) * 4,
        scratch_shapes=tables + [pltpu.SemaphoreType.DMA((2,))],
        compiler_params=medium,
        name="source_own",
    )(waves, mine, *in_hbm(e_field, h_field))
    e_near, h_near = in_vmem(e_near, h_near)
    keep, send = pl.pallas_call(
        source_kernel(freqs, depth, wx, half, sizes, zslots, xslots, scale, zbits, True),
        out_shape=(part_shape, part_shape),
        in_specs=[vmem] * (4 + zbits),
        out_specs=(vmem, vmem),
        scratch_shapes=tables + [sums, sums],
        compiler_params=medium,
        name="source_both",
    )(waves, *in_vmem(theirs, *own), *zs)

    strip = pltpu.VMEM((8, LANES), f32)
    first, last = pl.pallas_call(
        column_kernel(freqs, depth, wx, wy, zbits),
        out_shape=(strip, strip),
        in_specs=[vmem] * (3 + zbits),
        out_specs=(vmem, vmem),
        compiler_params=small,
        name="columns",
    )(e_near, h_near, *in_vmem(theirs), *zs)

    whole = jax.ShapeDtypeStruct((3, depth, wx, wy), f32)
    pole_next, base_e, coef = pl.pallas_call(
        pole_kernel(),
        out_shape=(whole, pltpu.VMEM(whole.shape, f32), pltpu.VMEM((depth, wx, wy), f32)),
        in_specs=[hbm, vmem, hbm, hbm, vmem],
        out_specs=(hbm, vmem, vmem),
        scratch_shapes=[
            pltpu.SMEM(pole_table.shape, f32),
            pltpu.VMEM(whole.shape, f32),
            pltpu.VMEM((depth, wx, wy), jnp.int32),
            pltpu.VMEM(whole.shape, f32),
            pltpu.SemaphoreType.DMA((3,)),
        ],
        compiler_params=small,
        name="pole",
    )(*in_hbm(pole_table), e_near, *in_hbm(pole_current, material), *in_vmem(first))
    base_e, coef = in_vmem(base_e, coef)

    def flat(value):
        return value.reshape(-1, LANES)

    terms = [keep, exchange(send, "gz", 1)]
    sides = [flat(terms[1])]
    side_rows = [[(i // 4) * block + block - 4 + i % 4 for i in range(8)]]
    for k in range(1, zbits):
        at = (1 - ((iz >> k) & 1)) * (depth - 1)
        rows = theirs[freqs + 1 :].reshape(12, depth, LANES)
        rows = lax.dynamic_index_in_dim(rows, at, 1, keepdims=False)
        sides.append(exchange(jnp.concatenate([rows[:7], rows[8:9]]), "gz", (2 << k) - 1))
        side_rows.append(list(range(8)))
    for k in range(1, zbits):
        part = terms[0] + terms[1]
        mask = (2 << k) - 1
        if k < zcut:
            middle = part.shape[0] // 2
            terms = [part[:middle], exchange(part[middle:], "gz", mask)]
        else:
            terms = [part, exchange(part, "gz", mask)]
    terms = [flat(term) for term in terms]
    rows = sy * block

    ys = [None] * ybits
    k = 0
    while k < ybits:
        both = k + 1 < ybits
        size = rows // 4 if both else rows // 2
        plain, laden = pltpu.VMEM((size, LANES), f32), pltpu.VMEM((size + 8, LANES), f32)
        shapes = (plain, laden, laden, plain) if both else (plain, laden)
        keep, *away = pl.pallas_call(
            merge_y_kernel(len(terms), rows, k),
            out_shape=shapes,
            in_specs=[vmem] * (len(terms) + 2),
            out_specs=(vmem,) * len(shapes),
            compiler_params=small,
            name="merge_y",
        )(*in_vmem(*terms, first, last))
        if both:
            ys[k] = exchange(away[1], "gy", (2 << k) - 1)
            other = exchange(away[2], "gy", 2 << k)
            ys[k + 1] = exchange(away[0], "gy", (4 << k) - 1)
            terms = [keep, ys[k], ys[k + 1], other]
            k += 2
        else:
            ys[k] = exchange(away[0], "gy", (2 << k) - 1)
            terms = [keep, ys[k]]
            k += 1
        rows = size
    near = [*zs, *in_vmem(*ys)]
    xs = []
    slots = xslots
    for k in range(1, xbits):
        size = (rows - 8) // 2 + 8
        keep, away = pl.pallas_call(
            merge_x_kernel(freqs, len(terms), rows, depth, zbits, ybits, slots, side_rows),
            out_shape=(
                pltpu.VMEM((size, LANES), f32),
                pltpu.VMEM((size + 5 * depth + 4, LANES), f32),
            ),
            in_specs=[vmem] * (len(terms) + 2 + zbits + ybits),
            out_specs=(vmem, vmem),
            compiler_params=small,
            name="merge_x",
        )(*in_vmem(*terms, theirs, *sides, *ys), coef)
        xs.append(exchange(away, "gx", 1 << k))
        rows = size
        slots //= 2
        terms = [keep, xs[-1]]
    part = sum(term[:rows] for term in terms)

    e_most, h_most = pl.pallas_call(
        field_kernel(freqs, depth, wx, wy, xbits, ybits, zbits, side_rows),
        out_shape=(pltpu.VMEM(whole.shape, f32), pltpu.VMEM(whole.shape, f32)),
        in_specs=[vmem] * (5 + xbits + ybits + 2 * zbits),
        out_specs=(vmem,) * 2,
        compiler_params=pltpu.CompilerParams(vmem_limit_bytes=16 << 20),
        name="fields",
    )(e_near, h_near, base_e, coef, *in_vmem(first, theirs), *near, *in_vmem(*xs, *sides))

    top = gray(sz - 1)
    blocks = [part]
    for k in reversed(range(zcut)):
        others = [exchange(value, "gz", (2 << k) - 1) for value in blocks]
        blocks = others + blocks if (top >> k) & 1 else blocks + others
    e_next, h_next = pl.pallas_call(
        inject_kernel(depth, wx, wy, sy, sz, per, zcut),
        out_shape=(whole, whole),
        in_specs=[vmem] * (len(blocks) + 3),
        out_specs=(hbm, hbm),
        scratch_shapes=[
            pltpu.VMEM((3, wx, wy), f32),
            pltpu.VMEM((2, wx, wy), f32),
            pltpu.SemaphoreType.DMA((5,)),
        ],
        compiler_params=small,
        name="inject",
    )(*in_vmem(*blocks, e_most, h_most), coef)
    return (e_next, h_next, pole_next)


def solution(mesh):
    in_specs = (
        P(None, "gz", "gx", "gy"),
        P(None, "gz", "gx", "gy"),
        P(None, "gz", "gx", "gy"),
        P("gz", "gx", "gy"),
        P(),
        P(None, None, ("gx", "gy", "gz")),
        P(None, ("gx", "gy", "gz")),
        P(),
        P(),
    )
    out_specs = (P(None, "gz", "gx", "gy"), P(None, "gz", "gx", "gy"), P(None, "gz", "gx", "gy"))
    return jax.shard_map(
        local, mesh=mesh, in_specs=in_specs, out_specs=out_specs, check_vma=False
    )
```

```python
import math

import jax
import jax.numpy as jnp
from jax import lax
from jax.experimental import pallas as pl
from jax.experimental.pallas import tpu as pltpu
from jax.sharding import PartitionSpec as P


NPOLE = 4
LANES = 128


courant = 0.5


def exchange(array, axis, mask):
    return lax.ppermute(array, axis, [(i, i ^ mask) for i in range(lax.axis_size(axis))])


def gray(index):
    return index ^ (index >> 1)


def bits_of(size):
    return size.bit_length() - 1


def cmul(a, b):
    return (a[0] * b[0] - a[1] * b[1], a[0] * b[1] + a[1] * b[0])


def small_turn(angle):
    q = angle * angle
    c = 1.0 + q * (-1 / 2 + q * (1 / 24 + q * (-1 / 720 + q * (1 / 40320))))
    s = angle * (1.0 + q * (-1 / 6 + q * (1 / 120 + q * (-1 / 5040 + q * (1 / 362880)))))
    return c, s


def doubled(turn):
    c, s = turn
    return (c - s) * (c + s), 2.0 * (c * s)


def tree_levels(rows):
    levels = 0
    while 3 ** (levels + 1) * 8 <= rows:
        levels += 1
    return levels


def turn_table(first, unit, rows):
    powers = [unit]
    for _ in range(2):
        powers.append(doubled(powers[-1]))
    step = doubled(powers[-1])
    for level in range(max(1, tree_levels(rows))):
        powers.append(step)
        if level < tree_levels(rows):
            first = cmul(first, step)
        step = cmul(step, doubled(step))
    return [first, *powers]


def turn_count(rows):
    return 4 + max(1, tree_levels(rows))


def both_ways(value, turn):
    cc, ss = value[0] * turn[0], value[1] * turn[1]
    cs, sc = value[0] * turn[1], value[1] * turn[0]
    return (cc - ss, sc + cs), (cc + ss, sc - cs)


def rotations(table, rows):
    base, powers = table[0], table[1:]
    sub = lax.broadcasted_iota(jnp.int32, (8, base[0].shape[-1]), 0)
    value = tuple(jnp.broadcast_to(part, sub.shape) for part in base)
    for k in range(3):
        picked = (sub & (1 << k)) != 0
        value = cmul(value, (jnp.where(picked, powers[k][0], 1.0), jnp.where(picked, powers[k][1], 0.0)))
    blocks = [value]
    last = 0
    for level in range(tree_levels(rows)):
        last = level
        pairs = [both_ways(block, powers[3 + level]) for block in blocks]
        blocks = [pair[1] for pair in pairs] + blocks + [pair[0] for pair in pairs]
    while len(blocks) * 8 < rows:
        blocks.append(cmul(blocks[len(blocks) - 3**last], powers[3 + last]))
    return tuple(jnp.concatenate([block[i] for block in blocks], axis=0)[:rows] for i in (0, 1))


def split(value):
    high = value.astype(jnp.bfloat16)
    return high, (value - high.astype(jnp.float32)).astype(jnp.bfloat16)


def dot_nt(a, b):
    return lax.dot_general(a, b, (((1,), (1,)), ((), ())), preferred_element_type=jnp.float32)


def source_kernel(freqs, depth, wx, half, sizes, zslots, xslots, scale, zbits, closing):
    sx, sy, _ = sizes
    per = 4 // zslots
    main = 4 * xslots * wx

    def body(*refs):
        waves, packed = refs[:2]
        if closing:
            old_even, old_odd = refs[2:4]
            keep, send, xback, xturn, yturn, acc_even, acc_odd = refs[4 + zbits :]
        else:
            e_in, h_in, acc_even, acc_odd, e_near, h_near, xback, xturn, yturn, sems = refs[2:]
            copies = [
                pltpu.make_async_copy(source, target, sems.at[i])
                for i, (source, target) in enumerate(((e_in, e_near), (h_in, h_near)))
            ]
            for copy in copies:
                copy.start()
        ix, iy, iz = (lax.axis_index(name) for name in ("gx", "gy", "gz"))
        xbit, ybit, zbit = bits_of(sx), bits_of(sy), bits_of(zslots)
        starts = []
        for slot in range(xslots):
            code = ix
            for k in range(1, xbit):
                code = code ^ (((slot >> (xbit - 1 - k)) & 1) << k)
            starts.append((code * wx).astype(jnp.float32))
        zcode = 0
        for k in range(zbit):
            zcode = zcode * 2 + ((gray(iz) >> k) & 1)
        ycode = gray(iy)
        center = (2 * half - 1) / 2.0
        wave, phase = waves[0], waves[1]
        along_x = wave * packed[freqs, 0:1, :]
        along_y = wave * packed[freqs, 1:2, :]
        origin = along_y * center - phase
        unit = doubled(small_turn(0.5 * along_x))
        for xr in range(xslots):
            angle = along_x * starts[xr] + origin
            first = jnp.cos(angle), jnp.sin(angle)
            xback[xr, 0], xback[xr, 1] = cmul(first, (unit[0], -unit[1]))
            for k, turn in enumerate(turn_table(first, unit, wx)):
                xturn[xr, k, 0], xturn[xr, k, 1] = turn
        first = small_turn(0.5 * along_y)
        for k, turn in enumerate(turn_table(first, doubled(first), half)):
            yturn[k, 0], yturn[k, 1] = turn
        if closing:
            acc_even[...] = old_even[...]
            acc_odd[...] = old_odd[...]
        else:
            acc_even[...] = jnp.zeros_like(acc_even)
            acc_odd[...] = jnp.zeros_like(acc_odd)

        def pair(step, carry):
            firsts, seconds, coses, sines = [], [], [], []
            for n in range(2):
                f = 2 * step + n

                def row(ref, *where):
                    return tuple(ref[(*where, i, pl.ds(f, 1), slice(None))] for i in (0, 1))

                cy, sy_ = rotations([row(yturn, k) for k in range(turn_count(half))], half)
                coses.append(cy)
                sines.append(sy_)
                turns = [
                    rotations([row(xturn, xr, k) for k in range(turn_count(wx))], wx)
                    for xr in range(xslots)
                ]
                first, second = [], []
                for zr in range(zslots):
                    for xr in range(xslots):
                        cx, sx_ = turns[xr]
                        for c2 in range(per):
                            at = 2 * ((zcode ^ zr) * per + c2)
                            p = packed[f, pl.ds(at, 1), :]
                            q = packed[f, pl.ds(at + 1, 1), :]
                            first.append(p * cx - q * sx_)
                            second.append(p * sx_ + q * cx)
                p = packed[f, 6:7, :]
                q = packed[f, 7:8, :]
                line = lax.broadcasted_iota(jnp.int32, (16, p.shape[-1]), 0)
                one_first = jnp.zeros(line.shape, jnp.float32)
                one_second = one_first
                for xr in range(xslots):
                    cx, sx_ = row(xback, xr)
                    one_first = jnp.where(line == xr, p * cx - q * sx_, one_first)
                    one_second = jnp.where(line == xr, p * sx_ + q * cx, one_second)
                firsts.append(jnp.concatenate(first + [one_first], axis=0))
                seconds.append(jnp.concatenate(second + [one_second], axis=0))

            def product(lefts, rights):
                lh, ll = split(jnp.concatenate(lefts, axis=1))
                rh, rl = split(jnp.concatenate(rights, axis=1))
                both = dot_nt(jnp.concatenate([lh, ll], axis=0), rh)
                rows = lh.shape[0]
                return both[:rows] + dot_nt(lh, rl) + both[rows:]

            acc_even[...] += product(firsts, coses)
            acc_odd[...] += product(seconds, sines)
            return carry

        lax.fori_loop(0, freqs // 2, pair, 0, unroll=8 if closing else 4)
        if not closing:
            for copy in copies:
                copy.wait()
            return

        def slot(tile):
            code = gray(tile) ^ ycode
            place = 0
            for k in range(ybit):
                place = place * 2 + ((code >> k) & 1)
            return place

        def place(zr):
            return (keep, zr) if zr < zslots // 2 else (send, zr - zslots // 2)

        extra = xslots * per * wx
        for zr in range(zslots):
            ref, z = place(zr)
            for y in range(sy):
                ref[z, y, extra : extra + 8] = jnp.zeros((8, LANES), jnp.float32)
        at_z = (1 - (iz & 1)) * (depth - 1)
        for i, field in enumerate((0, 1, 2, 3, 4, 5, 6, 8)):
            row = field * depth
            spot = extra + 4 + i % 4
            send[0, i // 4, spot : spot + 1] = packed[
                freqs + 1 + row // 8, pl.ds(row % 8 + at_z, 1), :
            ]
        turned = 2 // per
        spare = 2 % per
        for j in range(sy // 2):
            lanes = slice(j * LANES, (j + 1) * LANES)
            up = slot(sy // 2 + j)
            down = slot(sy // 2 - 1 - j)
            at = 0
            for zr in range(zslots):
                ref, z = place(zr)
                for xr in range(xslots):
                    for c2 in range(per):
                        rows = slice(at * wx, (at + 1) * wx)
                        even = acc_even[rows, lanes] * scale
                        odd = acc_odd[rows, lanes] * scale
                        into = slice((xr * per + c2) * wx, (xr * per + c2 + 1) * wx)
                        ref[z, up, into] = even - odd
                        ref[z, down, into] = even + odd
                        at += 1
            for xr in range(xslots):
                even = acc_even[main + xr : main + xr + 1, lanes] * scale
                odd = acc_odd[main + xr : main + xr + 1, lanes] * scale
                for zr in range(zslots):
                    ref, z = place(zr)
                    ref[z, up, extra + 2 * xr : extra + 2 * xr + 1] = even - odd
                    ref[z, down, extra + 2 * xr : extra + 2 * xr + 1] = even + odd
                start = (((zcode ^ turned) * xslots + xr) * per + spare) * wx
                rows = pl.ds(pl.multiple_of(start, wx), wx)
                even = (acc_even[rows, lanes] * scale).T
                odd = (acc_odd[rows, lanes] * scale).T
                lower = slot(sy // 2 - j)
                line = slice(extra + 2 * xr + 1, extra + 2 * xr + 2)
                for zr in range(zslots):
                    ref, z = place(zr)
                    ref[z, lower, line, 0:wx] = even[0:1] + odd[0:1]
                if j < sy // 2 - 1:
                    upper = slot(sy // 2 + j + 1)
                    for zr in range(zslots):
                        ref, z = place(zr)
                        ref[z, upper, line, 0:wx] = even[LANES - 1 :] - odd[LANES - 1 :]

    return body


def near_flags(index, bits):
    low, high = [], []
    for k in range(bits):
        upper = (index >> k) & 1
        rest = index & ((1 << k) - 1)
        low.append(((upper == 1) & (rest == 0)).astype(jnp.float32))
        high.append(((upper == 0) & (rest == (1 << k) - 1)).astype(jnp.float32))
    return low, high


def weighted(flags, values):
    total = flags[0] * values[0]
    for flag, value in zip(flags[1:], values[1:]):
        total = total + flag * value
    return total


def pack_kernel(freqs, depth, wx, zbits):
    def body(*refs):
        e_in, h_in, cotangent, cosines, wavenumber, time_phase, message, waves = refs[:8]
        layers = refs[8 : 8 + zbits]
        edge, cos_near, wave_near, phase_near, sems = refs[8 + zbits :]
        upper = lax.axis_index("gx") & 1
        pairs = [
            (cotangent, message.at[0:freqs]),
            (e_in.at[:, :, 0:8], edge.at[0, 0:3]),
            (h_in.at[:, :, 0:8], edge.at[0, 3:6]),
            (e_in.at[:, :, wx - 8 : wx], edge.at[1, 0:3]),
            (h_in.at[:, :, wx - 8 : wx], edge.at[1, 3:6]),
            (cosines, cos_near),
            (wavenumber, wave_near),
            (time_phase, phase_near),
        ]
        for k, layer in enumerate(layers):
            at = (1 - ((lax.axis_index("gz") >> k) & 1)) * (depth - 1)
            pairs += [(e_in.at[:, at], layer.at[0:3]), (h_in.at[:, at], layer.at[3:6])]
        copies = [
            pltpu.make_async_copy(source, target, sems.at[i])
            for i, (source, target) in enumerate(pairs)
        ]
        for copy in copies:
            copy.start()
        for copy in copies:
            copy.wait()
        message[freqs, 0:2] = cos_near[...]
        message[freqs, 2:8] = jnp.zeros((6, LANES), jnp.float32)
        which = lax.broadcasted_iota(jnp.int32, (freqs, LANES), 0)
        for i, near in enumerate((wave_near, phase_near)):
            value = jnp.zeros((freqs, LANES), jnp.float32)
            for f in range(freqs):
                value = jnp.where(which == f, near[f], value)
            waves[i] = value
        for i in range(12):
            end = 1 - upper if i < 6 else upper
            for z in range(depth):
                row = i * depth + z
                message[freqs + 1 + row // 8, row % 8 : row % 8 + 1] = edge[
                    end, i % 6, z, pl.ds(7 * end, 1), :
                ]

    return body


def early_rows(message, freqs, depth, i):
    row = i * depth
    return message[freqs + 1 + row // 8, row % 8 : row % 8 + depth]


def column_kernel(freqs, depth, wx, wy, zbits):
    def body(*refs):
        e, h, message = refs[:3]
        zs = refs[3 : 3 + zbits]
        first, last = refs[3 + zbits :]
        low, high = near_flags(lax.axis_index("gz"), zbits)
        lane = lax.broadcasted_iota(jnp.int32, (1, LANES), 1)
        first[...] = jnp.zeros_like(first)
        last[...] = jnp.zeros_like(last)
        for i, field in enumerate((e[0], e[1], e[2], h[0], h[2])):
            turned = field.reshape(depth * wx, wy).T
            first[i : i + 1] = turned[0:1]
            last[i : i + 1] = turned[wy - 1 :]
        for i, layer in (
            (5, weighted(high, [z[1, 0:wx] for z in zs])),
            (6, weighted(low, [z[2, 0:wx] for z in zs])),
        ):
            turned = layer.T
            first[i : i + 1, 0:wx] = turned[0:1]
            last[i : i + 1, 0:wx] = turned[wy - 1 :]
        for ref, y in ((first, 0), (last, wy - 1)):
            corner = jnp.zeros((1, LANES), jnp.float32)
            side_x, side_y, next_x, next_y = (
                early_rows(message, freqs, depth, i)[:, y : y + 1] for i in (0, 1, 6, 7)
            )
            for z in range(depth):
                corner = jnp.where(lane == z, side_x[z : z + 1], corner)
                corner = jnp.where(lane == z * wx + wx - 1, side_y[z : z + 1], corner)
                corner = jnp.where(lane == depth + z, next_x[z : z + 1], corner)
                corner = jnp.where(lane == z * wx + wx - 2, next_y[z : z + 1], corner)
            ref[7:8] = corner

    return body


def total_of(terms, rows):
    value = terms[0][rows]
    for term in terms[1:]:
        value = value + term[rows]
    return value


def merge_y_kernel(count, rows, k):
    def body(*refs):
        terms, (first, last), outs = refs[:count], refs[count : count + 2], refs[count + 2 :]
        iy = lax.axis_index("gy")
        size = rows // len(outs)
        swaps = (None, k) if len(outs) == 2 else (None, k + 1, k, None)
        for i, (out, swap) in enumerate(zip(outs, swaps)):
            out[0:size] = total_of(terms, slice(i * size, (i + 1) * size))
            if swap is not None:
                upper = ((iy >> swap) & 1).astype(jnp.float32)
                out[size : size + 8] = upper * first[...] + (1.0 - upper) * last[...]

    return body


def halo_at(ref):
    rows = ref.shape[0]
    return ref[rows - 8 : rows]


def merge_x_kernel(freqs, count, rows, depth, zbits, ybits, slots, side_rows):
    def body(*refs):
        terms = refs[:count]
        message = refs[count]
        sides = refs[count + 1 : count + 1 + zbits]
        ys = refs[count + 1 + zbits : count + 1 + zbits + ybits]
        keep, out = refs[count + 2 + zbits + ybits :]
        half = (rows - 8) // 2
        size = half + 8
        keep[0:half] = total_of(terms, slice(0, half))
        out[0:half] = total_of(terms, slice(half, rows - 8))
        extra = total_of(terms, slice(rows - 8, rows))
        keep[half:size] = extra
        out[half:size] = pltpu.roll(extra, 8 - slots, 0)
        zlow, zhigh = near_flags(lax.axis_index("gz"), zbits)
        ylow, yhigh = near_flags(lax.axis_index("gy"), ybits)
        for line, i in enumerate((6, 7, 8, 10, 11)):
            row = size + line * depth
            out[row : row + depth] = early_rows(message, freqs, depth, i)
        base = size + 5 * depth

        def side(flags, i):
            ats = [rows[i] for rows in side_rows]
            return weighted(flags, [ref[at : at + 1] for at, ref in zip(ats, sides)])

        halos = [halo_at(y) for y in ys]
        out[base : base + 1] = side(zhigh, 6)
        out[base + 1 : base + 2] = side(zlow, 7)
        out[base + 2 : base + 3] = weighted(yhigh, [y[7:8] for y in halos])
        out[base + 3 : base + 4] = weighted(ylow, [y[7:8] for y in halos])

    return body


def pole_kernel():
    def body(table_in, e, pole_in, material_in, after, pole_out, base, coef_out, *scratch):
        table, pole, material, new_pole, sems = scratch
        copies = [
            pltpu.make_async_copy(source, target, sems.at[i])
            for i, (source, target) in enumerate(
                ((table_in, table), (material_in, material), (pole_in, pole))
            )
        ]
        for copy in copies:
            copy.start()
        for copy in copies:
            copy.wait()
        kind = material[...]

        def chosen(i):
            value = jnp.full(kind.shape, table[i, NPOLE - 1], jnp.float32)
            for m in range(NPOLE - 1):
                value = jnp.where(kind == m, table[i, m], value)
            return value

        decay, drive, coef = (chosen(i) for i in range(3))
        coef_out[...] = coef
        for i in range(3):
            old = pole[i]
            electric = e[i]
            new = decay * old + drive * electric
            new_pole[i] = new
            base[i] = electric - coef * (0.5 * (new + old))
        copy = pltpu.make_async_copy(new_pole, pole_out, sems.at[0])
        copy.start()
        copy.wait()

    return body


def field_kernel(freqs, depth, wx, wy, xbits, ybits, zbits, side_rows):
    def body(*refs):
        e, h, base_e, coef_ref, first, message = refs[:6]
        zs = refs[6 : 6 + zbits]
        ys = refs[6 + zbits : 6 + zbits + ybits]
        xs = [x[x.shape[0] - 5 * depth - 4 :] for x in refs[6 + zbits + ybits : 5 + zbits + ybits + xbits]]
        sides = refs[5 + zbits + ybits + xbits : 5 + 2 * zbits + ybits + xbits]
        e_out, h_out = refs[5 + 2 * zbits + ybits + xbits :]
        ix, iy, iz = (lax.axis_index(name) for name in ("gx", "gy", "gz"))
        xlow, xhigh = near_flags(ix, xbits)
        ylow, yhigh = near_flags(iy, ybits)
        zlow, zhigh = near_flags(iz, zbits)
        size = depth * wx
        base = 5 * depth
        lane = lax.broadcasted_iota(jnp.int32, (size, wy), 1)
        line = lax.broadcasted_iota(jnp.int32, (size, wy), 0) & (wx - 1)
        inside_x, inside_y, inside_z = (
            (index > 0).astype(jnp.float32) for index in (ix, iy, iz)
        )

        def flat(ref, i):
            return ref[i].reshape(size, wy)

        ex, ey, ez = (flat(e, i) for i in range(3))
        oldx, oldy, oldz = (flat(h, i) for i in range(3))

        def spread(rows):
            return jnp.broadcast_to(rows[:, None, :], (depth, wx, wy)).reshape(size, wy)

        def next_y(value, column):
            rows = value.shape[0]
            return jnp.where(lane[:rows] == wy - 1, column, pltpu.roll(value, wy - 1, 1))

        def next_x(value, rows):
            return jnp.where(line == wx - 1, spread(rows), pltpu.roll(value, size - 1, 0))

        def next_z(value, layer):
            return jnp.concatenate([value[wx:], layer], axis=0)

        def last_y(value, column):
            return jnp.where(lane == 0, column, pltpu.roll(value, 1, 1))

        def last_x(value, rows):
            return jnp.where(line == 0, spread(rows), pltpu.roll(value, 1, 0))

        def last_z(value, layer):
            return jnp.concatenate([layer, value[:-wx]], axis=0)

        ylo = weighted(ylow, [halo_at(y) for y in ys])
        yhi = weighted(yhigh, [halo_at(y) for y in ys])
        above = yhi.T

        def rows_of(flags, i):
            line = i if i < 3 else i - 1
            at = slice(line * depth, (line + 1) * depth)
            return weighted(flags, [early_rows(message, freqs, depth, i)] + [x[at] for x in xs])

        def extra_of(flags, early, i):
            return weighted(flags, [early] + [x[base + i : base + i + 1] for x in xs])

        def layer_of(flags, i):
            return weighted(flags, [z[i, 0:wx] for z in zs])

        def side_of(flags, i):
            ats = [rows[i] for rows in side_rows]
            return weighted(flags, [side[at : at + 1] for at, side in zip(ats, sides)])

        up_x, up_y = layer_of(zhigh, 0), layer_of(zhigh, 1)
        hx = oldx - courant * ((next_y(ez, above[:, 2:3]) - ez) - (next_z(ey, up_y) - ey))
        hy = oldy - courant * (
            (next_z(ex, up_x) - ex) - (next_x(ez, rows_of(xhigh, 2)) - ez)
        )
        hz = oldz - courant * (
            (next_x(ey, rows_of(xhigh, 1)) - ey) - (next_y(ex, above[:, 0:1]) - ex)
        )
        mx, my, mz = (rows_of(xlow, i) for i in range(3))
        up = jnp.concatenate([mx[1:], extra_of(xlow, side_of(zhigh, 0), 0)], axis=0)
        low_hy = rows_of(xlow, 4) - courant * ((up - mx) - (e[2, :, 0, :] - mz))
        corner = xlow[0] * above[0:depth, 7:8]
        for flag, x in zip(xlow[1:], xs):
            tail = x[base : base + 8].T
            corner = corner + flag * tail[depth : 2 * depth, 2:3]
        low_hz = rows_of(xlow, 5) - courant * (
            (e[1, :, 0, :] - my) - (next_y(mx, corner) - mx)
        )
        strip = lax.broadcasted_iota(jnp.int32, (1, LANES), 1)
        lx, ly, lz = ylo[0:1], ylo[1:2], ylo[2:3]
        up = jnp.where(
            strip >= size - wx, pltpu.roll(ylo[5:6], size - wx, 1), pltpu.roll(ly, LANES - wx, 1)
        )
        side_hx = ylo[3:4] - courant * ((first[2:3] - lz) - (up - ly))
        corner = xhigh[0] * ylo[7:8]
        for flag, x in zip(xhigh[1:], xs):
            corner = corner + flag * pltpu.roll(x[base + 3 : base + 4], 1, 1)
        right = jnp.where((strip & (wx - 1)) == wx - 1, corner, pltpu.roll(ly, LANES - 1, 1))
        side_hz = ylo[4:5] - courant * ((right - ly) - (first[0:1] - lx))
        both = jnp.concatenate([side_hx, side_hz, jnp.zeros((6, LANES), jnp.float32)], axis=0)
        both = (inside_y * both).T
        bx, by, bz = (layer_of(zlow, i) for i in range(3))
        under_hx = layer_of(zlow, 3) - courant * (
            (next_y(bz, above[0:wx, 6:7]) - bz) - (ey[:wx] - by)
        )
        right = jnp.concatenate([bz[1:], extra_of(xhigh, side_of(zlow, 2), 1)], axis=0)
        under_hy = layer_of(zlow, 4) - courant * ((ex[:wx] - bx) - (right - bz))
        under_hx = inside_z * under_hx
        under_hy = inside_z * under_hy
        low_hy = inside_x * low_hy
        low_hz = inside_x * low_hz
        curl = (
            (hz - last_y(hz, both[:, 1:2])) - (hy - last_z(hy, under_hy)),
            (hx - last_z(hx, under_hx)) - (hz - last_x(hz, low_hz)),
            (hy - last_x(hy, low_hy)) - (hx - last_y(hx, both[:, 0:1])),
        )
        coef = coef_ref[...].reshape(size, wy)
        shape = (depth, wx, wy)
        for i, magnetic in enumerate((hx, hy, hz)):
            value = flat(base_e, i) + coef * curl[i]
            h_out[i] = magnetic.reshape(shape)
            e_out[i] = value.reshape(shape)

    return body


def inject_kernel(depth, wx, wy, sy, sz, per, zcut):
    def body(*refs):
        blocks = refs[: 1 << zcut]
        e_near, h_near, coef_ref, e_out, h_out, e_new, h_new, sems = refs[1 << zcut :]
        last = depth - 1
        others = slice(0, last)
        copies = [
            pltpu.make_async_copy(e_near.at[:, others], e_out.at[:, others], sems.at[0]),
            pltpu.make_async_copy(h_near.at[:, others], h_out.at[:, others], sems.at[1]),
            pltpu.make_async_copy(h_near.at[2, last], h_out.at[2, last], sems.at[2]),
        ]
        for copy in copies:
            copy.start()
        h_copy = pltpu.make_async_copy(h_new, h_out.at[0:2, last], sems.at[3])
        e_copy = pltpu.make_async_copy(e_new, e_out.at[:, last], sems.at[4])
        ix, iy, iz = (lax.axis_index(name) for name in ("gx", "gy", "gz"))

        @pl.when(iz == sz - 1)
        def _():
            inside_x, inside_y = ((index > 0).astype(jnp.float32) for index in (ix, iy))
            lane = lax.broadcasted_iota(jnp.int32, (wx, wy), 1)
            line = lax.broadcasted_iota(jnp.int32, (wx, wy), 0)
            flip = (
                lax.broadcasted_iota(jnp.int32, (wy, wy), 0)
                + lax.broadcasted_iota(jnp.int32, (wy, wy), 1)
                == wy - 1
            ).astype(jnp.bfloat16)
            flipped = iy < sy // 2

            def straight(value):
                high, rest = value.astype(jnp.bfloat16), value
                rest = rest - high.astype(jnp.float32)
                middle = rest.astype(jnp.bfloat16)
                low = (rest - middle.astype(jnp.float32)).astype(jnp.bfloat16)
                parts = [
                    jnp.dot(part, flip, preferred_element_type=jnp.float32)
                    for part in (high, middle, low)
                ]
                turned = (parts[0] + parts[1]) + parts[2]
                return jnp.where(flipped, turned, value)

            tiles = [straight(ref[...]) for ref in blocks]

            def channel(c):
                start = (c % per) * wx
                return tiles[c // per][start : start + wx]

            electric_x, electric_y, magnetic_x, magnetic_y = (channel(c) for c in range(4))
            before = inside_x * tiles[3 // per][per * wx : per * wx + 1]
            beside = inside_y * blocks[2 // per][per * wx : per * wx + 8].T[0:wx, 1:2]
            last_x = jnp.where(line == 0, before, pltpu.roll(magnetic_y, 1, 0))
            last_y = jnp.where(lane == 0, beside, pltpu.roll(magnetic_x, 1, 1))
            coef = coef_ref[last]
            h_new[0] = h_near[0, last] - courant * magnetic_x
            h_new[1] = h_near[1, last] - courant * magnetic_y
            e_new[0] = e_near[0, last] + coef * (courant * magnetic_y - electric_x)
            e_new[1] = e_near[1, last] - coef * (courant * magnetic_x + electric_y)
            e_new[2] = e_near[2, last] + coef * courant * (
                (magnetic_x - last_y) - (magnetic_y - last_x)
            )

        @pl.when(iz != sz - 1)
        def _():
            for i in range(3):
                e_new[i] = e_near[i, last]
            for i in range(2):
                h_new[i] = h_near[i, last]

        h_copy.start()
        e_copy.start()
        for copy in (*copies, h_copy, e_copy):
            copy.wait()

    return body


def in_hbm(*arrays):
    return [pltpu.with_memory_space_constraint(array, pltpu.HBM) for array in arrays]


def in_vmem(*arrays):
    return [pltpu.with_memory_space_constraint(array, pltpu.VMEM) for array in arrays]


def local(
    e_field, h_field, pole_current, material, pole_table, cotangent, cosines, wavenumber, time_phase
):
    depth, wx, wy = material.shape
    sizes = sx, sy, sz = tuple(lax.axis_size(name) for name in ("gx", "gy", "gz"))
    _, _, iz = (lax.axis_index(name) for name in ("gx", "gy", "gz"))
    freqs, _, count = cotangent.shape
    scale = 1.0 / math.sqrt(freqs * count * sx * sy * sz)
    assert wy == LANES and depth * wx == LANES and 1 < sx <= 4 and sy > 1 and sz > 1
    pad = -count % LANES
    if pad:
        cotangent = jnp.pad(cotangent, ((0, 0), (0, 0), (0, pad)))
        cosines = jnp.pad(cosines, ((0, 0), (0, pad)))
    f32 = jnp.float32
    smem = pl.BlockSpec(memory_space=pltpu.SMEM)
    vmem = pl.BlockSpec(memory_space=pltpu.VMEM)
    hbm = pl.BlockSpec(memory_space=pltpu.HBM)
    small = pltpu.CompilerParams(vmem_limit_bytes=8 << 20)
    xslots = sx // 2
    zslots = min(sz, 4)
    per = 4 // zslots
    xbits, ybits, zbits = bits_of(sx), bits_of(sy), bits_of(sz)
    zcut = bits_of(zslots)

    assert 8 % depth == 0
    mine, waves, *layers = pl.pallas_call(
        pack_kernel(freqs, depth, wx, zbits),
        out_shape=[
            pltpu.VMEM((freqs + 1 + 12 * depth // 8, 8, LANES), f32),
            pltpu.VMEM((2, freqs, LANES), f32),
        ]
        + [pltpu.VMEM((6, wx, wy), f32)] * zbits,
        in_specs=[hbm] * 6,
        out_specs=[vmem] * (2 + zbits),
        scratch_shapes=[
            pltpu.VMEM((2, 6, depth, 8, LANES), f32),
            pltpu.VMEM((2, LANES), f32),
            pltpu.SMEM((freqs,), f32),
            pltpu.SMEM((freqs,), f32),
            pltpu.SemaphoreType.DMA((8 + 2 * zbits,)),
        ],
        compiler_params=small,
        name="pack",
    )(*in_hbm(e_field, h_field, cotangent, cosines, wavenumber, time_phase))
    theirs = exchange(mine, "gx", 1)
    zs = [exchange(layers[k], "gz", (2 << k) - 1) for k in range(zbits)]
    zs = in_vmem(*zs)

    half = sy * wy // 2
    width = count + pad
    block = xslots * per * wx + 8
    part_shape = pltpu.VMEM((zslots // 2, sy, block, wy), f32)
    assert freqs % 2 == 0
    sums = pltpu.VMEM((4 * xslots * wx + 16, half), f32)
    tables = [
        pltpu.VMEM((xslots, 2, freqs, width), f32),
        pltpu.VMEM((xslots, turn_count(wx), 2, freqs, width), f32),
        pltpu.VMEM((turn_count(half), 2, freqs, width), f32),
    ]
    medium = pltpu.CompilerParams(vmem_limit_bytes=24 << 20)
    waves, mine = in_vmem(waves, mine)
    *own, e_near, h_near = pl.pallas_call(
        source_kernel(freqs, depth, wx, half, sizes, zslots, xslots, scale, zbits, False),
        out_shape=(sums, sums, pltpu.VMEM(e_field.shape, f32), pltpu.VMEM(h_field.shape, f32)),
        in_specs=[vmem, vmem, hbm, hbm],
        out_specs=(vmem,) * 4,
        scratch_shapes=tables + [pltpu.SemaphoreType.DMA((2,))],
        compiler_params=medium,
        name="source_own",
    )(waves, mine, *in_hbm(e_field, h_field))
    e_near, h_near = in_vmem(e_near, h_near)
    keep, send = pl.pallas_call(
        source_kernel(freqs, depth, wx, half, sizes, zslots, xslots, scale, zbits, True),
        out_shape=(part_shape, part_shape),
        in_specs=[vmem] * (4 + zbits),
        out_specs=(vmem, vmem),
        scratch_shapes=tables + [sums, sums],
        compiler_params=medium,
        name="source_both",
    )(waves, *in_vmem(theirs, *own), *zs)

    strip = pltpu.VMEM((8, LANES), f32)
    first, last = pl.pallas_call(
        column_kernel(freqs, depth, wx, wy, zbits),
        out_shape=(strip, strip),
        in_specs=[vmem] * (3 + zbits),
        out_specs=(vmem, vmem),
        compiler_params=small,
        name="columns",
    )(e_near, h_near, *in_vmem(theirs), *zs)

    whole = jax.ShapeDtypeStruct((3, depth, wx, wy), f32)
    pole_next, base_e, coef = pl.pallas_call(
        pole_kernel(),
        out_shape=(whole, pltpu.VMEM(whole.shape, f32), pltpu.VMEM((depth, wx, wy), f32)),
        in_specs=[hbm, vmem, hbm, hbm, vmem],
        out_specs=(hbm, vmem, vmem),
        scratch_shapes=[
            pltpu.SMEM(pole_table.shape, f32),
            pltpu.VMEM(whole.shape, f32),
            pltpu.VMEM((depth, wx, wy), jnp.int32),
            pltpu.VMEM(whole.shape, f32),
            pltpu.SemaphoreType.DMA((3,)),
        ],
        compiler_params=small,
        name="pole",
    )(*in_hbm(pole_table), e_near, *in_hbm(pole_current, material), *in_vmem(first))
    base_e, coef = in_vmem(base_e, coef)

    def flat(value):
        return value.reshape(-1, LANES)

    terms = [keep, exchange(send, "gz", 1)]
    sides = [flat(terms[1])]
    side_rows = [[(i // 4) * block + block - 4 + i % 4 for i in range(8)]]
    for k in range(1, zbits):
        at = (1 - ((iz >> k) & 1)) * (depth - 1)
        rows = theirs[freqs + 1 :].reshape(12, depth, LANES)
        rows = lax.dynamic_index_in_dim(rows, at, 1, keepdims=False)
        sides.append(exchange(jnp.concatenate([rows[:7], rows[8:9]]), "gz", (2 << k) - 1))
        side_rows.append(list(range(8)))
    for k in range(1, zbits):
        part = terms[0] + terms[1]
        mask = (2 << k) - 1
        if k < zcut:
            middle = part.shape[0] // 2
            terms = [part[:middle], exchange(part[middle:], "gz", mask)]
        else:
            terms = [part, exchange(part, "gz", mask)]
    terms = [flat(term) for term in terms]
    rows = sy * block

    ys = [None] * ybits
    k = 0
    while k < ybits:
        both = k + 1 < ybits
        size = rows // 4 if both else rows // 2
        plain, laden = pltpu.VMEM((size, LANES), f32), pltpu.VMEM((size + 8, LANES), f32)
        shapes = (plain, laden, laden, plain) if both else (plain, laden)
        keep, *away = pl.pallas_call(
            merge_y_kernel(len(terms), rows, k),
            out_shape=shapes,
            in_specs=[vmem] * (len(terms) + 2),
            out_specs=(vmem,) * len(shapes),
            compiler_params=small,
            name="merge_y",
        )(*in_vmem(*terms, first, last))
        if both:
            ys[k] = exchange(away[1], "gy", (2 << k) - 1)
            other = exchange(away[2], "gy", 2 << k)
            ys[k + 1] = exchange(away[0], "gy", (4 << k) - 1)
            terms = [keep, ys[k], ys[k + 1], other]
            k += 2
        else:
            ys[k] = exchange(away[0], "gy", (2 << k) - 1)
            terms = [keep, ys[k]]
            k += 1
        rows = size
    near = [*zs, *in_vmem(*ys)]
    xs = []
    slots = xslots
    for k in range(1, xbits):
        size = (rows - 8) // 2 + 8
        keep, away = pl.pallas_call(
            merge_x_kernel(freqs, len(terms), rows, depth, zbits, ybits, slots, side_rows),
            out_shape=(
                pltpu.VMEM((size, LANES), f32),
                pltpu.VMEM((size + 5 * depth + 4, LANES), f32),
            ),
            in_specs=[vmem] * (len(terms) + 2 + zbits + ybits),
            out_specs=(vmem, vmem),
            compiler_params=small,
            name="merge_x",
        )(*in_vmem(*terms, theirs, *sides, *ys), coef)
        xs.append(exchange(away, "gx", 1 << k))
        rows = size
        slots //= 2
        terms = [keep, xs[-1]]
    part = sum(term[:rows] for term in terms)

    e_most, h_most = pl.pallas_call(
        field_kernel(freqs, depth, wx, wy, xbits, ybits, zbits, side_rows),
        out_shape=(pltpu.VMEM(whole.shape, f32), pltpu.VMEM(whole.shape, f32)),
        in_specs=[vmem] * (5 + xbits + ybits + 2 * zbits),
        out_specs=(vmem,) * 2,
        compiler_params=pltpu.CompilerParams(vmem_limit_bytes=16 << 20),
        name="fields",
    )(e_near, h_near, base_e, coef, *in_vmem(first, theirs), *near, *in_vmem(*xs, *sides))

    top = gray(sz - 1)
    blocks = [part]
    for k in reversed(range(zcut)):
        others = [exchange(value, "gz", (2 << k) - 1) for value in blocks]
        blocks = others + blocks if (top >> k) & 1 else blocks + others
    e_next, h_next = pl.pallas_call(
        inject_kernel(depth, wx, wy, sy, sz, per, zcut),
        out_shape=(whole, whole),
        in_specs=[vmem] * (len(blocks) + 3),
        out_specs=(hbm, hbm),
        scratch_shapes=[
            pltpu.VMEM((3, wx, wy), f32),
            pltpu.VMEM((2, wx, wy), f32),
            pltpu.SemaphoreType.DMA((5,)),
        ],
        compiler_params=small,
        name="inject",
    )(*in_vmem(*blocks, e_most, h_most), coef)
    return (e_next, h_next, pole_next)


def solution(mesh):
    in_specs = (
        P(None, "gz", "gx", "gy"),
        P(None, "gz", "gx", "gy"),
        P(None, "gz", "gx", "gy"),
        P("gz", "gx", "gy"),
        P(),
        P(None, None, ("gx", "gy", "gz")),
        P(None, ("gx", "gy", "gz")),
        P(),
        P(),
    )
    out_specs = (P(None, "gz", "gx", "gy"), P(None, "gz", "gx", "gy"), P(None, "gz", "gx", "gy"))
    return jax.shard_map(
        local, mesh=mesh, in_specs=in_specs, out_specs=out_specs, check_vma=False
    )
```
